128 devices in a mesh: group: 8 (over z, core), dev: 16 (over y, x).
Axes of the slice: x: 4, y: 4, z: 4, core: 2. Of those that a mesh axis runs over, the one named last changes fastest.
Arguments:
- points: bfloat16 [196608, 512], P(('group', 'dev')), may hold values from -5 to 5
- targets: float32 [8, 196608], P(None, ('group', 'dev')), may hold values from -16 to 16
- partner_tiles: int32 [8, 16, 8, 2], replicated, may hold values from -1 to 5, as said below
Outputs:
- solution: float32 [8, 196608], P(None, ('group', 'dev'))
- residual: float32 [8, 196608], P(None, ('group', 'dev'))
The draws below stay inside these ranges and needn't reach their ends.
Inputs may be any that keep to these rules, and one draw needn't show every extreme that they name: `partner_tiles`: entry [g, v, h, c] names a tile of block (h, v) whose points are coupled with every point of block (g, v), or is -1. For one v and two groups at most one of the two blocks names tiles of the other, and no block names tiles of its own group. The tiles named in [g, v, h] are distinct and stand before its -1 entries. In every draw some block names 2 tiles of one other group.
All inputs are finite; a program needn't handle non-finite values.
Results may differ from the reference program's by a relative error of at most 0.0003.
Values may be sent and summed in bfloat16 or wider, within the bound.
No kernel may reach another device: no remote copies, remote signals or barrier semaphores. Data moves between devices by JAX's collectives and lax.ppermute only.
A program may use at most 192 MiB of HBM per device.

```python
import jax
import jax.numpy as jnp
from jax import lax

D = 512
TILE = 256
TILES_DEV = 6
PROBES = 8
CAP = 2
ITERS = 2
POINTS = 196608
N_GROUP = 8
N_DEV = 16


def draw_points(key, part):
    latent_key, jitter_key, flip_key = jax.random.split(key, 3)
    latent_scale = (4.0 / D) ** 0.5
    jitter_scale = (1.28 / D) ** 0.5
    latent = jnp.clip(jax.random.normal(latent_key, (POINTS, 8), jnp.float32), -4.0, 4.0) * latent_scale
    jitter = jnp.clip(jax.random.normal(jitter_key, (POINTS, D), jnp.float32), -4.0, 4.0) * jitter_scale
    flips = (jax.random.randint(flip_key, (D,), 0, 2) * 2 - 1).astype(jnp.float32)
    columns = jnp.arange(D) % 8
    return (latent[:, columns] * flips[None, :] + jitter).astype(jnp.bfloat16)


def draw_targets(key, part):
    fraction = jnp.arange(POINTS).astype(jnp.float32)[None, :] / POINTS
    values = jnp.clip(jax.random.normal(key, (PROBES, POINTS), jnp.float32), -5.0, 5.0) * (1.0 + 2.0 * fraction)
    return values


def draw_partner_tiles(key, part):
    weight_key = jax.random.fold_in(key, 0)
    start_key = jax.random.fold_in(key, 3)
    weights = jax.random.randint(weight_key, (N_GROUP, N_DEV), 0, 1 << 20)
    start_tile = jax.random.randint(start_key, (N_GROUP, N_GROUP, N_DEV), 0, TILES_DEV)
    own_group = jnp.arange(N_GROUP)[:, None, None] + jnp.zeros((N_GROUP, N_GROUP, N_DEV), jnp.int32)
    peer_group = jnp.arange(N_GROUP)[None, :, None] + jnp.zeros((N_GROUP, N_GROUP, N_DEV), jnp.int32)
    dev_index = jnp.arange(N_DEV)[None, None, :] + jnp.zeros((N_GROUP, N_GROUP, N_DEV), jnp.int32)
    lower_group = jnp.minimum(own_group, peer_group)
    upper_group = jnp.maximum(own_group, peer_group)
    own_weight = weights[own_group, dev_index]
    peer_weight = weights[peer_group, dev_index]
    owns_pair = jnp.logical_or(own_weight > peer_weight, jnp.logical_and(own_weight == peer_weight, own_group < peer_group))
    listed = jnp.logical_and(owns_pair, own_group != peer_group)
    slot_range = jnp.arange(CAP)[None, None, None, :]
    filled = jnp.logical_and(listed[..., None], slot_range < CAP)
    tiles_named = jnp.where(filled, (start_tile[lower_group, upper_group, dev_index][..., None] + slot_range) % TILES_DEV, -1)
    return jnp.transpose(tiles_named, (0, 2, 1, 3)).astype(jnp.int32)


def setup_inputs(seed: int = 0) -> dict:
    splits = jax.random.split(jax.random.key(seed), 4)
    return {
        "points": draw_points(jax.random.fold_in(splits[3], 71), 0),
        "targets": draw_targets(jax.random.fold_in(splits[3], 71), 0),
        "partner_tiles": draw_partner_tiles(jax.random.fold_in(splits[3], 71), 0),
    }


length_scale = 3.9
noise_level = 1.0
coupling_weight = 0.5
highest = lax.Precision.HIGHEST

def affinity(left_points, right_points, left_norms, right_norms):
    inner_prod = lax.dot_general(left_points, right_points, (((1,), (1,)), ((), ())), preferred_element_type=jnp.float32)
    dist_sq = jnp.maximum(left_norms[:, None] + right_norms[None, :] - 2.0 * inner_prod, 0.0)
    scaled = jnp.sqrt(dist_sq) / length_scale
    return jnp.maximum(1.0 - scaled, 0.0) ** 4 * (4.0 * scaled + 1.0)

def contract_last(left_values, right_values):
    return lax.dot_general(left_values, right_values, (((1,), (1,)), ((), ())), precision=highest, preferred_element_type=jnp.float32)

def add_rows(accumulated, start, addition):
    axis_last = accumulated.ndim - 1
    current = lax.dynamic_slice_in_dim(accumulated, start, addition.shape[-1], axis_last)
    return lax.dynamic_update_slice_in_dim(accumulated, current + addition, start, axis_last)

def couple_all(points, row_norms, vector, partner_tiles):
    row_count = TILES_DEV * TILE

    def visit(running, device):
        degree, coupled = running
        group_index = device // N_DEV
        position = device % N_DEV
        start = (device * row_count).astype(jnp.int32)
        own_points = lax.dynamic_slice_in_dim(points, start, row_count, 0)
        own_sq = lax.dynamic_slice_in_dim(row_norms, start, row_count, 0)
        own_vector = lax.dynamic_slice_in_dim(vector, start, row_count, 1)
        local_block = affinity(own_points, own_points, own_sq, own_sq)
        own_degree = lax.optimization_barrier(jnp.sum(local_block, axis=1))
        own_coupled = contract_last(own_vector, local_block)

        def pair_with(totals, remote_start, size):
            degree_now, coupled_now, degree_own, coupled_own = totals
            remote_points = lax.dynamic_slice_in_dim(points, remote_start, size, 0)
            remote_sq = lax.dynamic_slice_in_dim(row_norms, remote_start, size, 0)
            remote_vector = lax.dynamic_slice_in_dim(vector, remote_start, size, 1)
            blocks = affinity(own_points, remote_points, own_sq, remote_sq)
            degree_own = degree_own + lax.optimization_barrier(jnp.sum(blocks, axis=1))
            coupled_own = coupled_own + contract_last(remote_vector, blocks)
            degree_now = add_rows(degree_now, remote_start, lax.optimization_barrier(jnp.sum(blocks, axis=0)))
            coupled_now = add_rows(coupled_now, remote_start, jnp.dot(own_vector, blocks, precision=highest, preferred_element_type=jnp.float32))
            return (degree_now, coupled_now, degree_own, coupled_own)
        totals = (degree, coupled, own_degree, own_coupled)
        for offset in (1, 2):
            remote_start = (jnp.maximum(device - offset, 0) * row_count).astype(jnp.int32)
            totals = lax.cond(position >= offset, lambda held: pair_with(held, remote_start, row_count), lambda held: held, totals)
        own_list = lax.dynamic_index_in_dim(lax.dynamic_index_in_dim(partner_tiles, group_index, 0, keepdims=False), position, 0, keepdims=False)
        for partner in range(N_GROUP):
            for column in range(CAP):
                tile_id = own_list[partner, column]
                remote_start = ((partner * N_DEV + position) * row_count + jnp.maximum(tile_id, 0) * TILE).astype(jnp.int32)
                totals = lax.cond(tile_id >= 0, lambda held: pair_with(held, remote_start, TILE), lambda held: held, totals)
        degree, coupled, own_degree, own_coupled = totals
        degree = add_rows(degree, start, own_degree)
        coupled = add_rows(coupled, start, own_coupled)
        return ((degree, coupled), None)
    initial = (jnp.zeros((POINTS,), jnp.float32), jnp.zeros((PROBES, POINTS), jnp.float32))
    (degree, coupled), unused = lax.scan(visit, initial, jnp.arange(N_GROUP * N_DEV, dtype=jnp.int32))
    return (degree, coupled)

def reference(points, targets, partner_tiles):
    row_norms = lax.optimization_barrier(jnp.sum(jnp.square(points.astype(jnp.float32)), axis=1))
    degree, coupled = couple_all(points, row_norms, targets, partner_tiles)

    def operate(vector, coupled_part):
        return noise_level * vector + coupling_weight * (degree[None, :] * vector - coupled_part)
    solution = jnp.zeros_like(targets)
    residual = targets
    direction = targets
    applied = operate(targets, coupled)
    norm_now = lax.optimization_barrier(jnp.sum(residual * residual, axis=1))
    for iteration in range(ITERS):
        if iteration > 0:
            unused, coupled = couple_all(points, row_norms, direction, partner_tiles)
            applied = operate(direction, coupled)
        curvature = lax.optimization_barrier(jnp.sum(direction * applied, axis=1))
        step_size = norm_now / curvature
        solution = solution + step_size[:, None] * direction
        residual = residual - step_size[:, None] * applied
        if iteration + 1 < ITERS:
            norm_next = lax.optimization_barrier(jnp.sum(residual * residual, axis=1))
            direction = residual + (norm_next / norm_now)[:, None] * direction
            norm_now = norm_next
    return (solution, residual)
```

```python
import jax
import jax.numpy as jnp
from jax import lax
from jax.experimental import pallas as pl
from jax.experimental.pallas import tpu as pltpu
from jax.sharding import PartitionSpec as P

TILE = 256
SCALE = 3.9
C5 = 5.0 / SCALE**4
C4 = 4.0 / SCALE**5
NT = (((1,), (1,)), ((), ()))
NN = (((1,), (0,)), ((), ()))
F32 = jnp.float32
BF16 = jnp.bfloat16


def mm(a, b, dims):
    return lax.dot_general(a, b, dims, preferred_element_type=F32)


def col_norms(x):
    x = x.astype(F32)
    return jnp.broadcast_to(jnp.sum(x * x, axis=1, keepdims=True), (x.shape[0], 128))


def row_norms(x):
    return col_norms(x).T[0:1, :]


def kernel_tile(a, b_scaled, na, nb):
    q = mm(a, b_scaled, NT) + (jnp.concatenate([na, na], axis=1) + nb)
    q = jnp.maximum(q, 1e-30)
    u = jnp.maximum(SCALE - q * lax.rsqrt(q), 0.0)
    t = u * u
    return (t * t * (C5 - C4 * u)).astype(BF16)


def split(v):
    hi = v.astype(BF16)
    lo = (v - hi.astype(F32)).astype(BF16)
    return jnp.concatenate([hi, lo], axis=0)


def split_ones(v, one):
    return jnp.concatenate([split(v), jnp.full((16, v.shape[1]), one, F32).astype(BF16)], axis=0)


def fold(acc):
    return acc[0:8] + acc[8:16]


def fold_ones(acc):
    return jnp.concatenate([acc[0:8] + acc[8:16], acc[16:24]], axis=0)


def params():
    return pltpu.CompilerParams(vmem_limit_bytes=60 * 1024 * 1024)


def full(shape):
    return pl.BlockSpec(shape, lambda *_: (0,) * len(shape))


def cost(tiles, k_bytes):
    return pl.CostEstimate(
        flops=tiles * 2 * TILE * TILE * 600, transcendentals=tiles * TILE * TILE, bytes_accessed=k_bytes
    )


SMEM = pl.BlockSpec(memory_space=pltpu.SMEM)
ANY = pl.BlockSpec(memory_space=pl.ANY)


def prep(table, points, targets):
    def body(table_ref, pts_ref, r_ref, out0, out1, xr_ref, sems):
        copies = []
        for h in range(8):
            for c in range(2):
                t = jnp.maximum(table_ref[h * 2 + c], 0)
                cp = pltpu.make_async_copy(
                    pts_ref.at[pl.ds(pl.multiple_of(t * TILE, TILE), TILE), :],
                    (out0, out1)[c].at[h],
                    sems.at[h * 2 + c],
                )
                cp.start()
                copies.append(cp)
        for h in range(8):
            for c in range(2):
                t = jnp.maximum(table_ref[h * 2 + c], 0)
                xr_ref[h, c * 8 : c * 8 + 8, :] = r_ref[:, pl.ds(pl.multiple_of(t * TILE, TILE), TILE)]
        for cp in copies:
            cp.wait()

    tiles = jax.ShapeDtypeStruct((8, TILE, points.shape[1]), BF16)
    return pl.pallas_call(
        body,
        out_shape=(tiles, tiles, jax.ShapeDtypeStruct((8, 16, TILE), F32)),
        in_specs=[SMEM, ANY, full(targets.shape)],
        out_specs=(ANY, ANY, full((8, 16, TILE))),
        scratch_shapes=[pltpu.SemaphoreType.DMA((16,))],
        compiler_params=params(),
        name="prep",
    )(table, points, targets)


def local_first(points, r):
    n, d = points.shape
    nt = n // TILE

    def body(a_ref, b_ref, r_ref, k_ref, acc_ref, na, va):
        @pl.when(pl.program_id(0) == 0)
        def _():
            na[...] = col_norms(a_ref[...])
            va[...] = split_ones(r_ref[...], 1.0)

        b = b_ref[...]
        nb = row_norms(b)
        b = b * jnp.asarray(-2.0, BF16)
        acc = jnp.zeros((32, TILE), F32)
        for i in range(nt):
            s = slice(i * TILE, (i + 1) * TILE)
            k = kernel_tile(a_ref[s, :], b, na[s, :], nb)
            k_ref[0, s, :] = k
            acc += mm(va[:, s], k, NN)
        acc_ref[...] = fold_ones(acc)

    return pl.pallas_call(
        body,
        grid=(nt,),
        out_shape=(jax.ShapeDtypeStruct((nt, n, TILE), BF16), jax.ShapeDtypeStruct((16, n), F32)),
        in_specs=[full((n, d)), pl.BlockSpec((TILE, d), lambda t: (t, 0)), full((8, n))],
        out_specs=(pl.BlockSpec((1, n, TILE), lambda t: (t, 0, 0)), pl.BlockSpec((16, TILE), lambda t: (0, t))),
        scratch_shapes=[pltpu.VMEM((n, 128), F32), pltpu.VMEM((32, n), BF16)],
        compiler_params=params(),
        cost_estimate=cost(nt * nt, n * n * 2),
        name="local_first",
    )(points, points, r)


def pair_step(a_refs, b, va, vb, na, k_ref, acc_row, nt):
    nb = row_norms(b)
    b = b * jnp.asarray(-2.0, BF16)
    acc = jnp.zeros((32, TILE), F32)
    for j, a_ref in enumerate(a_refs):
        for i in range(nt):
            s = slice(i * TILE, (i + 1) * TILE)
            g = slice((j * nt + i) * TILE, (j * nt + i + 1) * TILE)
            k = kernel_tile(a_ref[s, :], b, na[g, :], nb)
            k_ref[0, g, :] = k
            acc += mm(va[:, g], k, NN)
            acc_row[:, g] += mm(vb, k, NT)
    return fold_ones(acc)


def band_first(flags, left, own, right, r_left, r, r_right):
    n, d = own.shape
    nt = n // TILE

    def body(flag_ref, l_ref, a_ref, b_ref, rl_ref, r_ref, rb_ref, k_ref, col_ref, rowl_ref, rowo_ref, na, va, acc):
        t = pl.program_id(0)
        has_left = flag_ref[0].astype(F32)
        has_right = flag_ref[1].astype(F32)

        @pl.when(t == 0)
        def _():
            na[0:n, :] = col_norms(l_ref[...])
            na[n:, :] = col_norms(a_ref[...])
            va[:, 0:n] = split_ones(rl_ref[...], has_left)
            va[:, n:] = split_ones(r_ref[...], 1.0)
            acc[...] = jnp.zeros_like(acc)

        vb = split_ones(rb_ref[...], has_right)
        col_ref[...] = pair_step((l_ref, a_ref), b_ref[...], va, vb, na, k_ref, acc, nt)

        @pl.when(t == nt - 1)
        def _():
            rows = fold_ones(acc[...])
            rowl_ref[...] = rows[:, 0:n]
            rowo_ref[...] = rows[:, n:]

    acc_shape = jax.ShapeDtypeStruct((16, n), F32)
    return pl.pallas_call(
        body,
        grid=(nt,),
        out_shape=(jax.ShapeDtypeStruct((nt, 2 * n, TILE), BF16), acc_shape, acc_shape, acc_shape),
        in_specs=[
            SMEM,
            full((n, d)),
            full((n, d)),
            pl.BlockSpec((TILE, d), lambda t: (t, 0)),
            full((8, n)),
            full((8, n)),
            pl.BlockSpec((8, TILE), lambda t: (0, t)),
        ],
        out_specs=(
            pl.BlockSpec((1, 2 * n, TILE), lambda t: (t, 0, 0)),
            pl.BlockSpec((16, TILE), lambda t: (0, t)),
            full((16, n)),
            full((16, n)),
        ),
        scratch_shapes=[
            pltpu.VMEM((2 * n, 128), F32),
            pltpu.VMEM((32, 2 * n), BF16),
            pltpu.VMEM((32, 2 * n), F32),
        ],
        compiler_params=params(),
        cost_estimate=cost(2 * nt * nt, 2 * n * n * 2),
        name="band_first",
    )(flags, left, own, right, r_left, r, r_right)


def cross_first(wanted, own, r, tiles, xr, c):
    n, d = own.shape
    nt = n // TILE

    def body(w_ref, a_ref, r_ref, b_ref, xr_ref, k_ref, col_ref, row_ref, na, va, acc):
        h = pl.program_id(0)

        @pl.when(h == 0)
        def _():
            na[...] = col_norms(a_ref[...])
            va[...] = split_ones(r_ref[...], 1.0)
            acc[...] = jnp.zeros_like(acc)

        @pl.when(w_ref[h * 2 + c] >= 0)
        def _():
            vb = split_ones(xr_ref[0], 1.0)
            col_ref[0] = pair_step((a_ref,), b_ref[0], va, vb, na, k_ref, acc, nt)

        @pl.when(h == 7)
        def _():
            row_ref[...] = fold_ones(acc[...])

    return pl.pallas_call(
        body,
        grid=(8,),
        out_shape=(
            jax.ShapeDtypeStruct((8, n, TILE), BF16),
            jax.ShapeDtypeStruct((8, 16, TILE), F32),
            jax.ShapeDtypeStruct((16, n), F32),
        ),
        in_specs=[
            SMEM,
            full((n, d)),
            full((8, n)),
            pl.BlockSpec((1, TILE, d), lambda h: (h, 0, 0)),
            pl.BlockSpec((1, 8, TILE), lambda h: (h, c, 0)),
        ],
        out_specs=(
            pl.BlockSpec((1, n, TILE), lambda h: (h, 0, 0)),
            pl.BlockSpec((1, 16, TILE), lambda h: (h, 0, 0)),
            full((16, n)),
        ),
        scratch_shapes=[
            pltpu.VMEM((n, 128), F32),
            pltpu.VMEM((32, n), BF16),
            pltpu.VMEM((32, n), F32),
        ],
        compiler_params=params(),
        cost_estimate=cost(7 * nt, 8 * n * TILE * 2),
        name="cross_first",
    )(wanted, own, r, tiles, xr)


def combine(requested, r, parts, ret0, ret1):
    n = r.shape[1]
    m = len(parts)

    def body(q_ref, r_ref, *refs):
        part_refs, (x0, x1, w_ref, xw_ref, deg_ref, sum_ref, acc) = refs[:m], refs[m:]
        total = part_refs[0][...]
        for p in part_refs[1:]:
            total = total + p[...]
        acc[...] = total
        for h in range(8):
            for c, x in enumerate((x0, x1)):
                t = q_ref[h * 2 + c]

                @pl.when(t >= 0)
                def _():
                    s = pl.ds(pl.multiple_of(t * TILE, TILE), TILE)
                    acc[:, s] = acc[:, s] + x[h]

        rv = r_ref[...]
        deg = acc[8:16, :]
        w = 0.5 * (deg * rv - acc[0:8, :])
        w_ref[...] = w
        deg_ref[...] = deg
        for h in range(8):
            for c in range(2):
                t = jnp.maximum(q_ref[h * 2 + c], 0)
                xw_ref[h, c * 8 : c * 8 + 8, :] = w_ref[:, pl.ds(pl.multiple_of(t * TILE, TILE), TILE)]
        lane = lax.broadcasted_iota(jnp.int32, (8, 128), 1)
        sums = jnp.zeros((8, 128), F32)
        for k, v in enumerate((rv * rv, rv * w, w * w, 0.5 * deg * w * w)):
            sums = jnp.where(lane == k, jnp.sum(v, axis=1, keepdims=True), sums)
        sum_ref[...] = sums

    return pl.pallas_call(
        body,
        out_shape=(
            jax.ShapeDtypeStruct((8, n), F32),
            jax.ShapeDtypeStruct((8, 16, TILE), F32),
            jax.ShapeDtypeStruct((8, n), F32),
            jax.ShapeDtypeStruct((8, 128), F32),
        ),
        in_specs=[SMEM, full((8, n))] + [full((16, n))] * m + [full((8, 16, TILE))] * 2,
        out_specs=(full((8, n)), full((8, 16, TILE)), full((8, n)), full((8, 128))),
        scratch_shapes=[pltpu.VMEM((16, n), F32)],
        compiler_params=params(),
        name="combine",
    )(requested, r, *parts, ret0, ret1)


def local_second(k_local, w):
    nt, n, _ = k_local.shape

    def body(k_ref, w_ref, out_ref, va):
        @pl.when(pl.program_id(0) == 0)
        def _():
            va[...] = split(w_ref[...])

        out_ref[...] = fold(mm(va[...], k_ref[0], NN))

    return pl.pallas_call(
        body,
        grid=(nt,),
        out_shape=jax.ShapeDtypeStruct((8, n), F32),
        in_specs=[pl.BlockSpec((1, n, TILE), lambda t: (t, 0, 0)), full((8, n))],
        out_specs=pl.BlockSpec((8, TILE), lambda t: (0, t)),
        scratch_shapes=[pltpu.VMEM((16, n), BF16)],
        compiler_params=params(),
        cost_estimate=pl.CostEstimate(flops=2 * n * n * 128, transcendentals=0, bytes_accessed=n * n * 2),
        name="local_second",
    )(k_local, w)


def band_second(k_band, w_left, w, w_right):
    nt, n2, _ = k_band.shape
    n = n2 // 2

    def body(k_ref, wl_ref, w_ref, wb_ref, col_ref, rowl_ref, rowo_ref, va, acc):
        t = pl.program_id(0)

        @pl.when(t == 0)
        def _():
            va[:, 0:n] = split(wl_ref[...])
            va[:, n:] = split(w_ref[...])
            acc[...] = jnp.zeros_like(acc)

        k = k_ref[0]
        col_ref[...] = fold(mm(va[...], k, NN))
        acc[...] += mm(split(wb_ref[...]), k, NT)

        @pl.when(t == nt - 1)
        def _():
            rows = fold(acc[...])
            rowl_ref[...] = rows[:, 0:n]
            rowo_ref[...] = rows[:, n:]

    acc_shape = jax.ShapeDtypeStruct((8, n), F32)
    return pl.pallas_call(
        body,
        grid=(nt,),
        out_shape=(acc_shape, acc_shape, acc_shape),
        in_specs=[
            pl.BlockSpec((1, n2, TILE), lambda t: (t, 0, 0)),
            full((8, n)),
            full((8, n)),
            pl.BlockSpec((8, TILE), lambda t: (0, t)),
        ],
        out_specs=(pl.BlockSpec((8, TILE), lambda t: (0, t)), full((8, n)), full((8, n))),
        scratch_shapes=[pltpu.VMEM((16, n2), BF16), pltpu.VMEM((16, n2), F32)],
        compiler_params=params(),
        cost_estimate=pl.CostEstimate(flops=8 * n * n * 128, transcendentals=0, bytes_accessed=2 * n * n * 2),
        name="band_second",
    )(k_band, w_left, w, w_right)


def cross_second(wanted, k0, k1, w, xw, sums, loc, row_left, row_own, w_left):
    _, n, _ = k0.shape

    def body(
        q_ref, k0_ref, k1_ref, w_ref, xw_ref, sum_ref, loc_ref, rl_ref, ro_ref, wl_ref, col_ref, row_ref, pay_ref, va, acc
    ):
        h = pl.program_id(0)

        @pl.when(h == 0)
        def _():
            va[...] = split(w_ref[...])
            acc[...] = jnp.zeros_like(acc)

        for c, k_ref in enumerate((k0_ref, k1_ref)):

            @pl.when(q_ref[h * 2 + c] >= 0)
            def _():
                k = k_ref[0]
                vb = split(xw_ref[0, c * 8 : c * 8 + 8, :])
                col_ref[0, c * 8 : c * 8 + 8, :] = fold(mm(va[...], k, NN))
                acc[...] += mm(vb, k, NT)

        @pl.when(h == 7)
        def _():
            row = fold(acc[...])
            row_ref[...] = row
            w = w_ref[...]
            pairs = w * (0.5 * loc_ref[...] + ro_ref[...] + row) + wl_ref[...] * rl_ref[...]
            lane = lax.broadcasted_iota(jnp.int32, (8, 128), 1)
            sub = lax.broadcasted_iota(jnp.int32, (8, 128), 0)
            sums = sum_ref[...]
            total = jnp.zeros((8, 128), F32)
            for k in range(4):
                v = jnp.sum(jnp.where(lane == k, sums, 0.0), axis=1, keepdims=True)
                if k == 3:
                    v = v - jnp.sum(pairs, axis=1, keepdims=True)
                total = total + jnp.where(lane == k * 8 + sub, v, 0.0)
            pay_ref[...] = jnp.broadcast_to(jnp.sum(total, axis=0, keepdims=True), (128, 128))

    return pl.pallas_call(
        body,
        grid=(8,),
        out_shape=(
            jax.ShapeDtypeStruct((8, 16, TILE), F32),
            jax.ShapeDtypeStruct((8, n), F32),
            jax.ShapeDtypeStruct((128, 128), F32),
        ),
        in_specs=[
            SMEM,
            pl.BlockSpec((1, n, TILE), lambda h: (h, 0, 0)),
            pl.BlockSpec((1, n, TILE), lambda h: (h, 0, 0)),
            full((8, n)),
            pl.BlockSpec((1, 16, TILE), lambda h: (h, 0, 0)),
            full((8, 128)),
            full((8, n)),
            full((8, n)),
            full((8, n)),
            full((8, n)),
        ],
        out_specs=(pl.BlockSpec((1, 16, TILE), lambda h: (h, 0, 0)), full((8, n)), full((128, 128))),
        scratch_shapes=[pltpu.VMEM((16, n), BF16), pltpu.VMEM((16, n), F32)],
        compiler_params=params(),
        cost_estimate=pl.CostEstimate(
            flops=16 * n * TILE * 2 * 256, transcendentals=0, bytes_accessed=16 * n * TILE * 2
        ),
        name="cross_second",
    )(wanted, k0, k1, w, xw, sums, loc, row_left, row_own, w_left)


def finish(requested, gathered, r, w, deg, parts, ret):
    n = r.shape[1]
    m = len(parts)

    def body(q_ref, g_ref, r_ref, w_ref, deg_ref, *refs):
        part_refs, (x_ref, sol_ref, res_ref, acc) = refs[:m], refs[m:]
        total = part_refs[0][...]
        for p in part_refs[1:]:
            total = total + p[...]
        acc[...] = total
        for h in range(8):
            for c in range(2):
                t = q_ref[h * 2 + c]

                @pl.when(t >= 0)
                def _():
                    s = pl.ds(pl.multiple_of(t * TILE, TILE), TILE)
                    acc[:, s] = acc[:, s] + x_ref[h, c * 8 : c * 8 + 8, :]

        row = jnp.sum(g_ref[...], axis=0, keepdims=True)
        lane = lax.broadcasted_iota(jnp.int32, (8, 128), 1)
        sub = lax.broadcasted_iota(jnp.int32, (8, 128), 0)
        rho, mu, nu, xi = (
            jnp.sum(jnp.where(lane == k * 8 + sub, row, 0.0), axis=1, keepdims=True) for k in range(4)
        )
        rv = r_ref[...]
        wv = w_ref[...]
        w2 = 0.5 * (deg_ref[...] * wv - acc[...])
        first = rho / (rho + mu)
        gap = (nu - mu * (mu / rho)) * (first * first)
        beta = gap / rho
        cr = mu / (rho + mu) + beta
        curvature = cr * cr * (rho + mu) - 2.0 * cr * first * (mu + nu) + first * first * (nu + xi)
        second = gap / curvature
        sol_ref[...] = (first + second * cr) * rv - (second * first) * wv
        res_ref[...] = (
            (mu / (rho + mu) - second * cr) * rv
            + (second * (first - cr) - first) * wv
            + (second * first) * w2
        )

    out = jax.ShapeDtypeStruct((8, n), F32)
    return pl.pallas_call(
        body,
        out_shape=(out, out),
        in_specs=[SMEM, full((128, 128))] + [full((8, n))] * (3 + m) + [full((8, 16, TILE))],
        out_specs=(full((8, n)), full((8, n))),
        scratch_shapes=[pltpu.VMEM((8, n), F32)],
        compiler_params=params(),
        name="finish",
    )(requested, gathered, r, w, deg, *parts, ret)


def on_device(points, targets, partner_tiles):
    dev_count = lax.axis_size("dev")
    group = lax.axis_index("group")
    position = lax.axis_index("dev")
    to_right = [(i, i + 1) for i in range(dev_count - 1)]
    to_left = [(i + 1, i) for i in range(dev_count - 1)]

    def right_of(x):
        return lax.ppermute(x, "dev", to_left)

    def left_of(x):
        return lax.ppermute(x, "dev", to_right)

    def trade(x):
        return lax.all_to_all(x, "group", split_axis=0, concat_axis=0, tiled=True)

    by_position = lax.dynamic_index_in_dim(partner_tiles, position, 1, keepdims=False)
    requested = lax.dynamic_index_in_dim(by_position, group, 1, keepdims=False).reshape(16)
    wanted = lax.dynamic_index_in_dim(by_position, group, 0, keepdims=False).reshape(16)
    flags = jnp.stack([position > 0, position < dev_count - 1]).astype(jnp.int32)

    out0, out1, xr_out = prep(requested, points, targets)
    in0 = trade(out0)
    xr = trade(xr_out)
    left, right = left_of(points), right_of(points)
    r_left, r_right = left_of(targets), right_of(targets)
    in1 = trade(out1)

    k_local, acc_local = local_first(points, targets)
    k_band, to_r, to_l, acc_band = band_first(flags, left, points, right, r_left, targets, r_right)
    from_left, from_right = left_of(to_r), right_of(to_l)
    k0, col0, row0 = cross_first(wanted, points, targets, in0, xr, 0)
    ret0 = trade(col0)
    k1, col1, row1 = cross_first(wanted, points, targets, in1, xr, 1)
    ret1 = trade(col1)
    w, xw_out, deg, sums = combine(
        requested, targets, (acc_local, acc_band, from_left, from_right, row0, row1), ret0, ret1
    )
    xw = trade(xw_out)
    w_left, w_right = left_of(w), right_of(w)
    loc2 = local_second(k_local, w)
    col_b, rowl_b, rowo_b = band_second(k_band, w_left, w, w_right)
    from_left2, from_right2 = left_of(col_b), right_of(rowl_b)
    col_x, row_x, pay = cross_second(wanted, k0, k1, w, xw, sums, loc2, rowl_b, rowo_b, w_left)
    gathered = lax.all_to_all(pay, ("group", "dev"), split_axis=0, concat_axis=0, tiled=True)
    ret2 = trade(col_x)
    return finish(requested, gathered, targets, w, deg, (loc2, rowo_b, row_x, from_left2, from_right2), ret2)


def solution(mesh):
    return jax.shard_map(
        on_device,
        mesh=mesh,
        in_specs=(P(("group", "dev"), None), P(None, ("group", "dev")), P()),
        out_specs=(P(None, ("group", "dev")), P(None, ("group", "dev"))),
        check_vma=False,
    )
```

```python
import jax
import jax.numpy as jnp
from jax import lax
from jax.experimental import pallas as pl
from jax.experimental.pallas import tpu as pltpu
from jax.sharding import PartitionSpec as P

TILE = 256
EXTRA = 8
SCALE = 3.9
C4 = 4.0 / SCALE**5
CUT = 5.0 * SCALE / 4.0
NT = (((1,), (1,)), ((), ()))
NN = (((1,), (0,)), ((), ()))
F32 = jnp.float32
BF16 = jnp.bfloat16
NEAR = (2, 3, 6, 7, 1)
FAR = (4, 5)

SMEM = pl.BlockSpec(memory_space=pltpu.SMEM)
ANY = pl.BlockSpec(memory_space=pl.ANY)
VM = pl.BlockSpec(memory_space=pltpu.VMEM)


def mm(a, b, dims):
    return lax.dot_general(a, b, dims, preferred_element_type=F32)


def col_norms(x):
    x = x.astype(F32)
    return jnp.broadcast_to(jnp.sum(x * x, axis=1, keepdims=True), (x.shape[0], 128))


def row_norms(x):
    return col_norms(x).T[0:1, :]


def kernel_tile(a, b_scaled, na, nb):
    q = mm(a, b_scaled, NT) + (jnp.concatenate([na, na], axis=1) + nb)
    q = jnp.maximum(q, 1e-30)
    u = jnp.maximum(SCALE - q * lax.rsqrt(q), 0.0)
    t = u * u
    return (t * t * (CUT - u)).astype(BF16)


def split(v):
    hi = v.astype(BF16)
    lo = (v - hi.astype(F32)).astype(BF16)
    return jnp.concatenate([hi, lo], axis=0)


def split_ones(v, one):
    return jnp.concatenate([split(v), jnp.full((16, v.shape[1]), one, F32).astype(BF16)], axis=0)


def fold(acc):
    return (acc[0:8] + acc[8:16]) * C4


def fold_ones(acc):
    return jnp.concatenate([acc[0:8] + acc[8:16], acc[16:24]], axis=0) * C4


def span(t):
    return pl.ds(pl.multiple_of(t * TILE, TILE), TILE)


def params(mib=12):
    return pltpu.CompilerParams(vmem_limit_bytes=mib * 1024 * 1024)


def f32(*shape):
    return jax.ShapeDtypeStruct(shape, F32)


def vmem_bf16(*shape):
    return pltpu.VMEM(shape, BF16)


def prep(partners, points, targets):
    d = points.shape[1]
    order = NEAR + FAR

    def body(p_ref, pts_ref, r_ref, table_ref, *outs):
        g = lax.axis_index("group")
        dev = lax.axis_index("dev")
        for h in range(8):
            for c in range(2):
                table_ref[h * 2 + c] = p_ref[h, g, c, dev]
                table_ref[16 + h * 2 + c] = p_ref[g, h, c, dev]
        for k, out in zip(order, outs):
            for c in range(2):
                s = span(jnp.maximum(p_ref[g ^ k, g, c, dev], 0))
                out[c, 0:TILE, :] = pts_ref[s, :]
                v = r_ref[:, s]
                hi = v.astype(BF16).astype(F32)
                out[c, TILE:, :] = jnp.concatenate([hi, v - hi], axis=1).astype(BF16)

    return pl.pallas_call(
        body,
        out_shape=[jax.ShapeDtypeStruct((32,), jnp.int32)] + [vmem_bf16(2, TILE + EXTRA, d) for _ in order],
        in_specs=[SMEM, VM, VM],
        out_specs=[SMEM] + [VM] * len(order),
        compiler_params=params(),
        name="prep",
    )(partners, points, targets)


def gate(held, arrived):
    m = len(held)

    def body(*refs):
        pass

    return pl.pallas_call(
        body,
        out_shape=[vmem_bf16(*x.shape) for x in held],
        in_specs=[VM] * m + [ANY] * len(arrived),
        out_specs=[VM] * m,
        input_output_aliases={i: i for i in range(m)},
        compiler_params=params(4),
        name="gate",
    )(*held, *arrived)


def local_first(points, r):
    n, d = points.shape
    nt = n // TILE

    def body(a_ref, r_ref, k_ref, acc_ref, na, nb, va):
        for i in range(nt):
            s = slice(i * TILE, (i + 1) * TILE)
            x = col_norms(a_ref[s, :])
            na[s, :] = x
            nb[:, s] = x.T[0:8]
        va[...] = split_ones(r_ref[...], 1.0)

        def step(t, carry):
            s = span(t)
            b = a_ref[s, :] * jnp.asarray(-2.0, BF16)
            for i in range(nt):
                c = slice(i * TILE, (i + 1) * TILE)
                k_ref[t, c, :] = kernel_tile(a_ref[c, :], b, na[c, :], nb[0:1, s])
            acc_ref[:, s] = fold_ones(mm(va[...], k_ref[t], NN))
            return carry

        lax.fori_loop(0, nt, step, 0)

    return pl.pallas_call(
        body,
        out_shape=(vmem_bf16(nt, n, TILE), f32(16, n)),
        in_specs=[VM, VM],
        out_specs=(VM, VM),
        scratch_shapes=[pltpu.VMEM((n, 128), F32), pltpu.VMEM((8, n), F32), pltpu.VMEM((32, n), BF16)],
        compiler_params=params(),
        name="local_first",
    )(points, r)


def band_first(left, own, right, r_left, r, r_right, after):
    n, d = own.shape
    nt = n // TILE

    def body(l_ref, a_ref, b_ref, rl_ref, r_ref, rb_ref, _, k_ref, col_ref, rowl_ref, rowo_ref, na, nb, va, vb, acc):
        v = lax.axis_index("dev")
        has_left = (v > 0).astype(F32)
        has_right = (v < lax.axis_size("dev") - 1).astype(F32)
        for i in range(nt):
            s = slice(i * TILE, (i + 1) * TILE)
            na[s, :] = col_norms(l_ref[s, :])
            na[n + i * TILE : n + (i + 1) * TILE, :] = col_norms(a_ref[s, :])
            nb[:, s] = col_norms(b_ref[s, :]).T[0:8]
        va[:, 0:n] = split_ones(rl_ref[...], has_left)
        va[:, n:] = split_ones(r_ref[...], 1.0)
        vb[...] = split_ones(rb_ref[...], has_right)
        acc[...] = jnp.zeros_like(acc)

        def step(t, carry):
            s = span(t)
            b = b_ref[s, :] * jnp.asarray(-2.0, BF16)
            for j, x in enumerate((l_ref, a_ref)):
                for i in range(nt):
                    c = slice(i * TILE, (i + 1) * TILE)
                    e = slice((j * nt + i) * TILE, (j * nt + i + 1) * TILE)
                    k_ref[t, e, :] = kernel_tile(x[c, :], b, na[e, :], nb[0:1, s])
            k = k_ref[t]
            col_ref[:, s] = fold_ones(mm(va[...], k, NN))
            acc[...] += mm(vb[:, s], k, NT)
            return carry

        lax.fori_loop(0, nt, step, 0)
        rows = fold_ones(acc[...])
        rowl_ref[...] = rows[:, 0:n]
        rowo_ref[...] = rows[:, n:]

    return pl.pallas_call(
        body,
        out_shape=(vmem_bf16(nt, 2 * n, TILE), f32(16, n), f32(16, n), f32(16, n)),
        in_specs=[VM] * 6 + [ANY],
        out_specs=(VM,) * 4,
        scratch_shapes=[
            pltpu.VMEM((2 * n, 128), F32),
            pltpu.VMEM((8, n), F32),
            pltpu.VMEM((32, 2 * n), BF16),
            pltpu.VMEM((32, n), BF16),
            pltpu.VMEM((32, 2 * n), F32),
        ],
        compiler_params=params(),
        name="band_first",
    )(left, own, right, r_left, r, r_right, after)


def cross_first(ks, table, own, r, tiles, after):
    n, d = own.shape
    nt = n // TILE
    m = len(ks)
    slots = 2 * m
    far = ks == FAR

    def body(q_ref, a_ref, r_ref, _, *refs):
        tile_refs = refs[:m]
        k_ref, row_ref, *cols = refs[m : 2 * m + 2]
        buf, jobs, sems, na, va, acc, nb, col = refs[2 * m + 2 :]
        g = lax.axis_index("group")
        count = jnp.int32(0)
        for i, k in enumerate(ks):
            for c in range(2):
                live = q_ref[16 + (g ^ k) * 2 + c] >= 0

                @pl.when(live)
                def _(count=count, i=i, k=k, c=c):
                    pltpu.make_async_copy(tile_refs[i].at[c], buf.at[count], sems.at[count]).start()
                    jobs[count] = 2 * i + c

                count = count + live.astype(jnp.int32)
        for i in range(nt):
            s = slice(i * TILE, (i + 1) * TILE)
            na[s, :] = col_norms(a_ref[s, :])
        va[...] = split_ones(r_ref[...], 1.0)
        acc[...] = jnp.zeros_like(acc)

        def step(j, carry):
            pltpu.make_async_copy(tile_refs[0].at[0], buf.at[j], sems.at[j]).wait()
            b = buf[j, 0:TILE, :]
            nb[...] = col_norms(b).T[0:8]
            b = b * jnp.asarray(-2.0, BF16)
            v = buf[j, TILE:, :].astype(F32)
            vb = jnp.concatenate([v[:, 0:TILE], v[:, TILE:], jnp.ones((16, TILE), F32)], axis=0).astype(BF16)
            for i in range(nt):
                c = slice(i * TILE, (i + 1) * TILE)
                k_ref[j, c, :] = kernel_tile(a_ref[c, :], b, na[c, :], nb[0:1, :])
            k = k_ref[j]
            col[jobs[j]] = fold_ones(mm(va[...], k, NN))
            acc[...] += mm(vb, k, NT)
            return carry

        lax.fori_loop(0, count, step, 0)
        row_ref[...] = fold_ones(acc[...])
        for i, out in enumerate(cols):
            out[...] = col[2 * i : 2 * i + 2]

    return pl.pallas_call(
        body,
        out_shape=[vmem_bf16(slots, n, TILE), f32(16, n)] + [f32(2, 16, TILE)] * m,
        in_specs=[SMEM, VM, VM, ANY] + [ANY] * m,
        out_specs=[VM] * (2 + m),
        scratch_shapes=[
            pltpu.VMEM((slots, TILE + EXTRA, d), BF16),
            pltpu.SMEM((slots,), jnp.int32),
            pltpu.SemaphoreType.DMA((slots,)),
            pltpu.VMEM((n, 128), F32),
            pltpu.VMEM((32, n), BF16),
            pltpu.VMEM((32, n), F32),
            pltpu.VMEM((8, TILE), F32),
            pltpu.VMEM((slots, 16, TILE), F32),
        ],
        compiler_params=params(),
        name="cross_far" if far else "cross_near",
    )(table, own, r, after, *tiles)


def combine(table, r, parts, ret):
    n = r.shape[1]
    m = len(parts)

    def body(q_ref, r_ref, *refs):
        part_refs, (*x_refs, w_ref, deg_ref, sum_ref, acc) = refs[:m], refs[m:]
        x_refs, out_refs = x_refs[:7], x_refs[7:]
        g = lax.axis_index("group")
        total = part_refs[0][...]
        for p in part_refs[1:]:
            total = total + p[...]
        acc[...] = total
        for k, x in zip(NEAR + FAR, x_refs):
            for c in range(2):
                t = q_ref[(g ^ k) * 2 + c]

                @pl.when(t >= 0)
                def _(x=x, c=c, t=t):
                    acc[:, span(t)] = acc[:, span(t)] + x[c]

        rv = r_ref[...]
        deg = acc[8:16, :]
        w = 0.5 * (deg * rv - acc[0:8, :])
        w_ref[...] = w
        deg_ref[...] = deg
        for k, out in zip(NEAR + FAR, out_refs):
            for c in range(2):
                t = jnp.maximum(q_ref[(g ^ k) * 2 + c], 0)
                out[c * 8 : c * 8 + 8, :] = w_ref[:, span(t)]
        lane = lax.broadcasted_iota(jnp.int32, (8, 128), 1)
        sums = jnp.zeros((8, 128), F32)
        for k, v in enumerate((rv * rv, rv * w, w * w, 0.5 * deg * w * w)):
            sums = jnp.where(lane == k, jnp.sum(v, axis=1, keepdims=True), sums)
        sum_ref[...] = sums

    return pl.pallas_call(
        body,
        out_shape=[f32(16, TILE)] * 7 + [f32(8, n), f32(8, n), f32(8, 128)],
        in_specs=[SMEM] + [VM] * (m + 8),
        out_specs=[VM] * 10,
        scratch_shapes=[pltpu.VMEM((16, n), F32)],
        compiler_params=params(),
        name="combine",
    )(table, r, *parts, *ret)


def local_second(k_local, w):
    nt, n, _ = k_local.shape

    def body(k_ref, w_ref, out_ref):
        va = split(w_ref[...])
        for t in range(nt):
            out_ref[:, t * TILE : (t + 1) * TILE] = fold(mm(va, k_ref[t], NN))

    return pl.pallas_call(
        body,
        out_shape=f32(8, n),
        in_specs=[VM, VM],
        out_specs=VM,
        compiler_params=params(),
        name="local_second",
    )(k_local, w)


def band_second(k_band, w_left, w, w_right, after):
    nt, n2, _ = k_band.shape
    n = n2 // 2

    def body(k_ref, wl_ref, w_ref, wb_ref, _, col_ref, rowl_ref, rowo_ref, va, acc):
        va[:, 0:n] = split(wl_ref[...])
        va[:, n:] = split(w_ref[...])
        vb = split(wb_ref[...])
        for t in range(nt):
            s = slice(t * TILE, (t + 1) * TILE)
            col_ref[:, s] = fold(mm(va[...], k_ref[t], NN))
            new = mm(vb[:, s], k_ref[t], NT)
            acc[...] = new if t == 0 else acc[...] + new
        rows = fold(acc[...])
        rowl_ref[...] = rows[:, 0:n]
        rowo_ref[...] = rows[:, n:]

    return pl.pallas_call(
        body,
        out_shape=(f32(8, n), f32(8, n), f32(8, n)),
        in_specs=[VM] * 4 + [ANY],
        out_specs=(VM,) * 3,
        scratch_shapes=[pltpu.VMEM((16, n2), BF16), pltpu.VMEM((16, n2), F32)],
        compiler_params=params(),
        name="band_second",
    )(k_band, w_left, w, w_right, after)


def cross_second(table, k_near, k_far, w, xw, sums, loc, row_left, row_own, w_left):
    _, n, _ = k_near.shape

    def body(
        q_ref, kn_ref, kf_ref, w_ref, sum_ref, loc_ref, rl_ref, ro_ref, wl_ref, *refs
    ):
        xw_refs, (col_ref, row_ref, va, acc, jobs, xw_ref) = refs[:7], refs[7:]
        g = lax.axis_index("group")
        for k, x in zip(NEAR + FAR, xw_refs):
            xw_ref[g ^ k] = x[...]
        va[...] = split(w_ref[...])
        acc[...] = jnp.zeros_like(acc)
        for ks, k_ref in ((NEAR, kn_ref), (FAR, kf_ref)):
            count = jnp.int32(0)
            for k in ks:
                for c in range(2):
                    live = q_ref[16 + (g ^ k) * 2 + c] >= 0

                    @pl.when(live)
                    def _(count=count, k=k, c=c):
                        jobs[count] = (g ^ k) * 2 + c

                    count = count + live.astype(jnp.int32)

            def step(j, carry, k_ref=k_ref):
                slot = jobs[j]
                h, c = slot >> 1, slot & 1
                rows = pl.ds(pl.multiple_of(c * 8, 8), 8)
                k = k_ref[j]
                col_ref[h, rows, :] = fold(mm(va[...], k, NN))
                acc[...] += mm(split(xw_ref[h, rows, :]), k, NT)
                return carry

            lax.fori_loop(0, count, step, 0)
        row = fold(acc[...])
        row_ref[...] = row
        pairs = w_ref[...] * (0.5 * loc_ref[...] + ro_ref[...] + row) + wl_ref[...] * rl_ref[...]
        lane = lax.broadcasted_iota(jnp.int32, (8, 128), 1)
        pay = jnp.where(lane == 3, sum_ref[...] - jnp.sum(pairs, axis=1, keepdims=True), sum_ref[...])
        for h in range(8):
            col_ref[h, 16:24, 0:128] = pay
            col_ref[h, 16:24, 128:] = jnp.zeros((8, 128), F32)

    return pl.pallas_call(
        body,
        out_shape=(f32(8, 24, TILE), f32(8, n)),
        in_specs=[SMEM] + [VM] * 15,
        out_specs=(VM, VM),
        scratch_shapes=[
            pltpu.VMEM((16, n), BF16),
            pltpu.VMEM((16, n), F32),
            pltpu.SMEM((16,), jnp.int32),
            pltpu.VMEM((8, 16, TILE), F32),
        ],
        compiler_params=params(),
        name="cross_second",
    )(table, k_near, k_far, w, sums, loc, row_left, row_own, w_left, *xw)


def group_sum(table, w, deg, parts, ret):
    n = w.shape[1]
    m = len(parts)

    def body(q_ref, w_ref, deg_ref, *refs):
        part_refs, (x_ref, w2_ref, out_ref, acc) = refs[:m], refs[m:]
        total = part_refs[0][...]
        for p in part_refs[1:]:
            total = total + p[...]
        acc[...] = total
        for h in range(8):
            for c in range(2):
                t = q_ref[h * 2 + c]

                @pl.when(t >= 0)
                def _(h=h, c=c, t=t):
                    acc[:, span(t)] = acc[:, span(t)] + x_ref[h, c * 8 : c * 8 + 8, :]

        w2_ref[...] = 0.5 * (deg_ref[...] * w_ref[...] - acc[...])
        sums = x_ref[0, 16:24, 0:128]
        for h in range(1, 8):
            sums = sums + x_ref[h, 16:24, 0:128]
        for v in range(16):
            out_ref[v] = sums

    return pl.pallas_call(
        body,
        out_shape=(f32(8, n), f32(16, 8, 128)),
        in_specs=[SMEM] + [VM] * (3 + m),
        out_specs=(VM, VM),
        scratch_shapes=[pltpu.VMEM((8, n), F32)],
        compiler_params=params(),
        name="group_sum",
    )(table, w, deg, *parts, ret)


def finish(gathered, r, w, w2):
    n = r.shape[1]

    def body(g_ref, r_ref, w_ref, w2_ref, sol_ref, res_ref):
        sums = g_ref[0]
        for v in range(1, 16):
            sums = sums + g_ref[v]
        rho, mu, nu, xi = (sums[:, k : k + 1] for k in range(4))
        rv = r_ref[...]
        wv = w_ref[...]
        first = rho / (rho + mu)
        gap = (nu - mu * (mu / rho)) * (first * first)
        beta = gap / rho
        cr = mu / (rho + mu) + beta
        curvature = cr * cr * (rho + mu) - 2.0 * cr * first * (mu + nu) + first * first * (nu + xi)
        second = gap / curvature
        sol_ref[...] = (first + second * cr) * rv - (second * first) * wv
        res_ref[...] = (
            (mu / (rho + mu) - second * cr) * rv
            + (second * (first - cr) - first) * wv
            + (second * first) * w2_ref[...]
        )

    return pl.pallas_call(
        body,
        out_shape=(f32(8, n), f32(8, n)),
        in_specs=[VM] * 4,
        out_specs=(VM, VM),
        compiler_params=params(),
        name="finish",
    )(gathered, r, w, w2)


def on_device(points, targets, partner_tiles):
    dev_count = lax.axis_size("dev")
    to_right = [(i, i + 1) for i in range(dev_count - 1)]
    to_left = [(i + 1, i) for i in range(dev_count - 1)]

    def right_of(x):
        return lax.ppermute(x, "dev", to_left)

    def left_of(x):
        return lax.ppermute(x, "dev", to_right)

    def swap(x, k):
        return lax.ppermute(x, "group", [(i, i ^ k) for i in range(8)])

    def trade(x, axis="group"):
        return lax.all_to_all(x, axis, split_axis=0, concat_axis=0, tiled=True)

    table, *outgoing = prep(jnp.transpose(partner_tiles, (0, 2, 3, 1)), points, targets)
    near = [swap(x, k) for x, k in zip(outgoing, NEAR)]
    left, right = left_of(points), right_of(points)
    r_left, r_right = left_of(targets), right_of(targets)
    k_local, acc_local = local_first(points, targets)
    far = [swap(x, k) for x, k in zip(gate(outgoing[len(NEAR) :], [*near, acc_local]), FAR)]
    k_near, row_near, *col_near = cross_first(NEAR, table, points, targets, near, acc_local)
    k_band, to_r, to_l, acc_band = band_first(left, points, right, r_left, targets, r_right, row_near)
    from_left, from_right = left_of(to_r), right_of(to_l)
    ret_near = [swap(x, k) for x, k in zip(col_near, NEAR)]
    k_far, row_far, *col_far = cross_first(FAR, table, points, targets, far, acc_band)
    ret = ret_near + [swap(x, k) for x, k in zip(col_far, FAR)]
    *xw_out, w, deg, sums = combine(
        table, targets, (acc_local, acc_band, from_left, from_right, row_near, row_far), ret
    )
    w_left, w_right = left_of(w), right_of(w)
    xw = [swap(x, k) for x, k in zip(xw_out, NEAR + FAR)]
    loc2 = local_second(k_local, w)
    col_b, rowl_b, rowo_b = band_second(k_band, w_left, w, w_right, loc2)
    from_left2, from_right2 = left_of(col_b), right_of(rowl_b)
    col_x, row_x = cross_second(table, k_near, k_far, w, xw, sums, loc2, rowl_b, rowo_b, w_left)
    w2, column = group_sum(table, w, deg, (loc2, rowo_b, row_x, from_left2, from_right2), trade(col_x))
    return finish(trade(column, "dev"), targets, w, w2)


def solution(mesh):
    return jax.shard_map(
        on_device,
        mesh=mesh,
        in_specs=(P(("group", "dev"), None), P(None, ("group", "dev")), P()),
        out_specs=(P(None, ("group", "dev")), P(None, ("group", "dev"))),
        check_vma=False,
    )
```

```python
import jax
import jax.numpy as jnp
from jax import lax
from jax.experimental import pallas as pl
from jax.experimental.pallas import tpu as pltpu
from jax.sharding import PartitionSpec as P

TILE = 256
EXTRA = 8
SCALE = 3.9
C4 = 4.0 / SCALE**5
CUT = 5.0 * SCALE / 4.0
NT = (((1,), (1,)), ((), ()))
NN = (((1,), (0,)), ((), ()))
F32 = jnp.float32
BF16 = jnp.bfloat16
STAGES = ((2, 6, 1), (3, 7), (4, 5))
SWAPS = STAGES[0] + STAGES[1] + STAGES[2]

SMEM = pl.BlockSpec(memory_space=pltpu.SMEM)
ANY = pl.BlockSpec(memory_space=pl.ANY)
VM = pl.BlockSpec(memory_space=pltpu.VMEM)


def mm(a, b, dims):
    return lax.dot_general(a, b, dims, preferred_element_type=F32)


def col_norms(x):
    x = x.astype(F32)
    return jnp.broadcast_to(jnp.sum(x * x, axis=1, keepdims=True), (x.shape[0], 128))


def row_norms(x):
    return col_norms(x).T[0:1, :]


def kernel_tile(a, b_scaled, na, nb):
    q = mm(a, b_scaled, NT) + (jnp.concatenate([na, na], axis=1) + nb)
    q = jnp.maximum(q, 1e-30)
    u = jnp.maximum(SCALE - q * lax.rsqrt(q), 0.0)
    t = u * u
    return (t * t * (CUT - u)).astype(BF16)


def split(v):
    hi = v.astype(BF16)
    lo = (v - hi.astype(F32)).astype(BF16)
    return jnp.concatenate([hi, lo], axis=0)


def rhs_ones(rows, one):
    v = rows.astype(F32)
    return jnp.concatenate([v[:, 0:TILE], v[:, TILE:], jnp.full((16, TILE), one, F32)], axis=0).astype(BF16)


def fold(acc):
    return (acc[0:8] + acc[8:16]) * C4


def fold_ones(acc):
    return jnp.concatenate([acc[0:8] + acc[8:16], acc[16:24]], axis=0) * C4


def span(t):
    return pl.ds(pl.multiple_of(t * TILE, TILE), TILE)


def params(mib=12):
    return pltpu.CompilerParams(vmem_limit_bytes=mib * 1024 * 1024)


def f32(*shape):
    return jax.ShapeDtypeStruct(shape, F32)


def vmem_bf16(*shape):
    return pltpu.VMEM(shape, BF16)


def prep(partners, points, targets):
    n, d = points.shape
    nt = n // TILE

    def body(p_ref, pts_ref, r_ref, table_ref, msg_ref, *outs):
        g = lax.axis_index("group")
        dev = lax.axis_index("dev")
        for h in range(8):
            for c in range(2):
                table_ref[h * 2 + c] = p_ref[h, g, c, dev]
                table_ref[16 + h * 2 + c] = p_ref[g, h, c, dev]
        for t in range(nt):
            s = slice(t * TILE, (t + 1) * TILE)
            msg_ref[t, 0:TILE, :] = pts_ref[s, :]
            v = r_ref[:, s]
            hi = v.astype(BF16).astype(F32)
            msg_ref[t, TILE:, :] = jnp.concatenate([hi, v - hi], axis=1).astype(BF16)
        for k, out in zip(SWAPS, outs):
            for c in range(2):
                out[c] = msg_ref[jnp.maximum(p_ref[g ^ k, g, c, dev], 0)]

    return pl.pallas_call(
        body,
        out_shape=[jax.ShapeDtypeStruct((32,), jnp.int32), vmem_bf16(nt, TILE + EXTRA, d)]
        + [vmem_bf16(2, TILE + EXTRA, d) for _ in SWAPS],
        in_specs=[SMEM, VM, VM],
        out_specs=[SMEM] + [VM] * (1 + len(SWAPS)),
        compiler_params=params(),
        name="prep",
    )(partners, points, targets)


def local_first(own):
    nt, _, d = own.shape
    n = nt * TILE

    def body(a_ref, k_ref, acc_ref, na, nb, va):
        for i in range(nt):
            s = slice(i * TILE, (i + 1) * TILE)
            x = col_norms(a_ref[i, 0:TILE, :])
            na[s, :] = x
            nb[:, s] = x.T[0:8]
            va[:, s] = rhs_ones(a_ref[i, TILE:, :], 1.0)

        def step(t, carry):
            s = span(t)
            b = a_ref[t, 0:TILE, :] * jnp.asarray(-2.0, BF16)
            for i in range(nt):
                c = slice(i * TILE, (i + 1) * TILE)
                k_ref[t, c, :] = kernel_tile(a_ref[i, 0:TILE, :], b, na[c, :], nb[0:1, s])
            acc_ref[:, s] = fold_ones(mm(va[...], k_ref[t], NN))
            return carry

        lax.fori_loop(0, nt, step, 0)

    return pl.pallas_call(
        body,
        out_shape=(vmem_bf16(nt, n, TILE), f32(16, n)),
        in_specs=[VM],
        out_specs=(VM, VM),
        scratch_shapes=[pltpu.VMEM((n, 128), F32), pltpu.VMEM((8, n), F32), pltpu.VMEM((32, n), BF16)],
        compiler_params=params(),
        name="local_first",
    )(own)


def band_first(left, own, right, after):
    nt, _, d = own.shape
    n = nt * TILE
    m = len(after)

    def body(l_ref, a_ref, b_ref, *refs):
        k_ref, col_ref, rowl_ref, rowo_ref, na, nb, va, vb, acc = refs[m:]
        v = lax.axis_index("dev")
        has_left = (v > 0).astype(F32)
        has_right = (v < lax.axis_size("dev") - 1).astype(F32)
        for i in range(nt):
            s = slice(i * TILE, (i + 1) * TILE)
            e = slice(n + i * TILE, n + (i + 1) * TILE)
            na[s, :] = col_norms(l_ref[i, 0:TILE, :])
            na[e, :] = col_norms(a_ref[i, 0:TILE, :])
            nb[:, s] = col_norms(b_ref[i, 0:TILE, :]).T[0:8]
            va[:, s] = rhs_ones(l_ref[i, TILE:, :], has_left)
            va[:, e] = rhs_ones(a_ref[i, TILE:, :], 1.0)
            vb[:, s] = rhs_ones(b_ref[i, TILE:, :], has_right)
        acc[...] = jnp.zeros_like(acc)

        def step(t, carry):
            s = span(t)
            b = b_ref[t, 0:TILE, :] * jnp.asarray(-2.0, BF16)
            for j, x in enumerate((l_ref, a_ref)):
                for i in range(nt):
                    e = slice((j * nt + i) * TILE, (j * nt + i + 1) * TILE)
                    k_ref[t, e, :] = kernel_tile(x[i, 0:TILE, :], b, na[e, :], nb[0:1, s])
            k = k_ref[t]
            col_ref[:, s] = fold_ones(mm(va[...], k, NN))
            acc[...] += mm(vb[:, s], k, NT)
            return carry

        lax.fori_loop(0, nt, step, 0)
        rows = fold_ones(acc[...])
        rowl_ref[...] = rows[:, 0:n]
        rowo_ref[...] = rows[:, n:]

    return pl.pallas_call(
        body,
        out_shape=(vmem_bf16(nt, 2 * n, TILE), f32(16, n), f32(16, n), f32(16, n)),
        in_specs=[VM] * 3 + [ANY] * m,
        out_specs=(VM,) * 4,
        scratch_shapes=[
            pltpu.VMEM((2 * n, 128), F32),
            pltpu.VMEM((8, n), F32),
            pltpu.VMEM((32, 2 * n), BF16),
            pltpu.VMEM((32, n), BF16),
            pltpu.VMEM((32, 2 * n), F32),
        ],
        compiler_params=params(),
        name="band_first",
    )(left, own, right, *after)


def cross_first(ks, table, own, tiles, after):
    nt, _, d = own.shape
    n = nt * TILE
    m = len(ks)
    slots = 2 * m

    def body(q_ref, a_ref, _, *refs):
        tile_refs = refs[:m]
        k_ref, row_ref, *cols = refs[m : 2 * m + 2]
        buf, jobs, sems, na, va, acc, nb, col = refs[2 * m + 2 :]
        g = lax.axis_index("group")
        count = jnp.int32(0)
        for i, k in enumerate(ks):
            for c in range(2):
                live = q_ref[16 + (g ^ k) * 2 + c] >= 0

                @pl.when(live)
                def _(count=count, i=i, k=k, c=c):
                    pltpu.make_async_copy(tile_refs[i].at[c], buf.at[count], sems.at[count]).start()
                    jobs[count] = 2 * i + c

                count = count + live.astype(jnp.int32)
        for i in range(nt):
            s = slice(i * TILE, (i + 1) * TILE)
            na[s, :] = col_norms(a_ref[i, 0:TILE, :])
            va[:, s] = rhs_ones(a_ref[i, TILE:, :], 1.0)
        acc[...] = jnp.zeros_like(acc)

        def step(j, carry):
            pltpu.make_async_copy(tile_refs[0].at[0], buf.at[j], sems.at[j]).wait()
            b = buf[j, 0:TILE, :]
            nb[...] = col_norms(b).T[0:8]
            b = b * jnp.asarray(-2.0, BF16)
            vb = rhs_ones(buf[j, TILE:, :], 1.0)
            for i in range(nt):
                c = slice(i * TILE, (i + 1) * TILE)
                k_ref[j, c, :] = kernel_tile(a_ref[i, 0:TILE, :], b, na[c, :], nb[0:1, :])
            k = k_ref[j]
            col[jobs[j]] = fold_ones(mm(va[...], k, NN))
            acc[...] += mm(vb, k, NT)
            return carry

        lax.fori_loop(0, count, step, 0)
        row_ref[...] = fold_ones(acc[...])
        for i, out in enumerate(cols):
            out[...] = col[2 * i : 2 * i + 2]

    return pl.pallas_call(
        body,
        out_shape=[vmem_bf16(slots, n, TILE), f32(16, n)] + [f32(2, 16, TILE)] * m,
        in_specs=[SMEM, VM, ANY] + [ANY] * m,
        out_specs=[VM] * (2 + m),
        scratch_shapes=[
            pltpu.VMEM((slots, TILE + EXTRA, d), BF16),
            pltpu.SMEM((slots,), jnp.int32),
            pltpu.SemaphoreType.DMA((slots,)),
            pltpu.VMEM((n, 128), F32),
            pltpu.VMEM((32, n), BF16),
            pltpu.VMEM((32, n), F32),
            pltpu.VMEM((8, TILE), F32),
            pltpu.VMEM((slots, 16, TILE), F32),
        ],
        compiler_params=params(),
        name=f"cross_first_{ks[0]}",
    )(table, own, after, *tiles)


def combine(table, r, parts, ret):
    n = r.shape[1]
    m = len(parts)

    def body(q_ref, r_ref, *refs):
        part_refs, (*x_refs, w_ref, deg_ref, sum_ref, acc) = refs[:m], refs[m:]
        x_refs, out_refs = x_refs[:7], x_refs[7:]
        g = lax.axis_index("group")
        total = part_refs[0][...]
        for p in part_refs[1:]:
            total = total + p[...]
        acc[...] = total
        for k, x in zip(SWAPS, x_refs):
            for c in range(2):
                t = q_ref[(g ^ k) * 2 + c]

                @pl.when(t >= 0)
                def _(x=x, c=c, t=t):
                    acc[:, span(t)] = acc[:, span(t)] + x[c]

        rv = r_ref[...]
        deg = acc[8:16, :]
        w = 0.5 * (deg * rv - acc[0:8, :])
        w_ref[...] = w
        deg_ref[...] = deg
        for k, out in zip(SWAPS, out_refs):
            for c in range(2):
                t = jnp.maximum(q_ref[(g ^ k) * 2 + c], 0)
                out[c * 8 : c * 8 + 8, :] = w_ref[:, span(t)]
        lane = lax.broadcasted_iota(jnp.int32, (8, 128), 1)
        sums = jnp.zeros((8, 128), F32)
        for k, v in enumerate((rv * rv, rv * w, w * w, 0.5 * deg * w * w)):
            sums = jnp.where(lane == k, jnp.sum(v, axis=1, keepdims=True), sums)
        sum_ref[...] = sums

    return pl.pallas_call(
        body,
        out_shape=[f32(16, TILE)] * 7 + [f32(8, n), f32(8, n), f32(8, 128)],
        in_specs=[SMEM] + [VM] * (m + 8),
        out_specs=[VM] * 10,
        scratch_shapes=[pltpu.VMEM((16, n), F32)],
        compiler_params=params(),
        name="combine",
    )(table, r, *parts, *ret)


def local_second(k_local, w):
    nt, n, _ = k_local.shape

    def body(k_ref, w_ref, out_ref):
        va = split(w_ref[...])
        for t in range(nt):
            out_ref[:, t * TILE : (t + 1) * TILE] = fold(mm(va, k_ref[t], NN))

    return pl.pallas_call(
        body,
        out_shape=f32(8, n),
        in_specs=[VM, VM],
        out_specs=VM,
        compiler_params=params(),
        name="local_second",
    )(k_local, w)


def band_second(k_band, w_left, w, w_right, after):
    nt, n2, _ = k_band.shape
    n = n2 // 2

    def body(k_ref, wl_ref, w_ref, wb_ref, _, col_ref, rowl_ref, rowo_ref, va, acc):
        va[:, 0:n] = split(wl_ref[...])
        va[:, n:] = split(w_ref[...])
        vb = split(wb_ref[...])
        for t in range(nt):
            s = slice(t * TILE, (t + 1) * TILE)
            col_ref[:, s] = fold(mm(va[...], k_ref[t], NN))
            new = mm(vb[:, s], k_ref[t], NT)
            acc[...] = new if t == 0 else acc[...] + new
        rows = fold(acc[...])
        rowl_ref[...] = rows[:, 0:n]
        rowo_ref[...] = rows[:, n:]

    return pl.pallas_call(
        body,
        out_shape=(f32(8, n), f32(8, n), f32(8, n)),
        in_specs=[VM] * 4 + [ANY],
        out_specs=(VM,) * 3,
        scratch_shapes=[pltpu.VMEM((16, n2), BF16), pltpu.VMEM((16, n2), F32)],
        compiler_params=params(),
        name="band_second",
    )(k_band, w_left, w, w_right, after)


def cross_second(ks, table, k_cache, w, xw, after):
    m = len(k_cache)
    n = w.shape[1]
    partners = [k for stage in ks for k in stage]
    p = len(partners)

    def body(q_ref, w_ref, *refs):
        k_refs, xw_refs = refs[:m], refs[m : m + p]
        col_ref, row_ref, va, acc, jobs, xws = refs[m + p + len(after) :]
        g = lax.axis_index("group")
        for k, x in zip(partners, xw_refs):
            xws[g ^ k] = x[...]
        va[...] = split(w_ref[...])
        acc[...] = jnp.zeros_like(acc)
        for stage, k_ref in zip(ks, k_refs):
            count = jnp.int32(0)
            for k in stage:
                for c in range(2):
                    live = q_ref[16 + (g ^ k) * 2 + c] >= 0

                    @pl.when(live)
                    def _(count=count, k=k, c=c):
                        jobs[count] = (g ^ k) * 2 + c

                    count = count + live.astype(jnp.int32)

            def step(j, carry, k_ref=k_ref):
                slot = jobs[j]
                h, c = slot >> 1, slot & 1
                rows = pl.ds(pl.multiple_of(c * 8, 8), 8)
                k = k_ref[j]
                col_ref[h, rows, :] = fold(mm(va[...], k, NN))
                acc[...] += mm(split(xws[h, rows, :]), k, NT)
                return carry

            lax.fori_loop(0, count, step, 0)
        row_ref[...] = fold(acc[...])

    return pl.pallas_call(
        body,
        out_shape=(f32(8, 16, TILE), f32(8, n)),
        in_specs=[SMEM, VM] + [VM] * (m + p) + [ANY] * len(after),
        out_specs=(VM, VM),
        scratch_shapes=[
            pltpu.VMEM((16, n), BF16),
            pltpu.VMEM((16, n), F32),
            pltpu.SMEM((16,), jnp.int32),
            pltpu.VMEM((8, 16, TILE), F32),
        ],
        compiler_params=params(),
        name=f"cross_second_{p}",
    )(table, w, *k_cache, *xw, *after)


def pack(near, far, w, sums, loc, row_left, row_own, rows, w_left):
    far_ks = STAGES[2]

    def body(near_ref, far_ref, w_ref, sum_ref, loc_ref, rl_ref, ro_ref, ra_ref, rb_ref, wl_ref, out_ref):
        g = lax.axis_index("group")
        row = ra_ref[...] + rb_ref[...]
        pairs = w_ref[...] * (0.5 * loc_ref[...] + ro_ref[...] + row) + wl_ref[...] * rl_ref[...]
        lane = lax.broadcasted_iota(jnp.int32, (8, 128), 1)
        pay = jnp.where(lane == 3, sum_ref[...] - jnp.sum(pairs, axis=1, keepdims=True), sum_ref[...])
        for h in range(8):
            out_ref[h, 0:16, :] = near_ref[h]
            out_ref[h, 16:24, 0:128] = pay
            out_ref[h, 16:24, 128:] = jnp.zeros((8, 128), F32)
        for k in far_ks:
            out_ref[g ^ k, 0:16, :] = far_ref[g ^ k]

    return pl.pallas_call(
        body,
        out_shape=f32(8, 24, TILE),
        in_specs=[VM] * 10,
        out_specs=VM,
        compiler_params=params(),
        name="pack",
    )(near, far, w, sums, loc, row_left, row_own, *rows, w_left)


def group_sum(table, w, deg, parts, ret):
    n = w.shape[1]
    m = len(parts)

    def body(q_ref, w_ref, deg_ref, *refs):
        part_refs, (x_ref, w2_ref, out_ref, acc) = refs[:m], refs[m:]
        total = part_refs[0][...]
        for p in part_refs[1:]:
            total = total + p[...]
        acc[...] = total
        for h in range(8):
            for c in range(2):
                t = q_ref[h * 2 + c]

                @pl.when(t >= 0)
                def _(h=h, c=c, t=t):
                    acc[:, span(t)] = acc[:, span(t)] + x_ref[h, c * 8 : c * 8 + 8, :]

        w2_ref[...] = 0.5 * (deg_ref[...] * w_ref[...] - acc[...])
        sums = x_ref[0, 16:24, 0:128]
        for h in range(1, 8):
            sums = sums + x_ref[h, 16:24, 0:128]
        for v in range(16):
            out_ref[v] = sums

    return pl.pallas_call(
        body,
        out_shape=(f32(8, n), f32(16, 8, 128)),
        in_specs=[SMEM] + [VM] * (3 + m),
        out_specs=(VM, VM),
        scratch_shapes=[pltpu.VMEM((8, n), F32)],
        compiler_params=params(),
        name="group_sum",
    )(table, w, deg, *parts, ret)


def finish(gathered, r, w, w2):
    n = r.shape[1]

    def body(g_ref, r_ref, w_ref, w2_ref, sol_ref, res_ref):
        sums = g_ref[0]
        for v in range(1, 16):
            sums = sums + g_ref[v]
        rho, mu, nu, xi = (sums[:, k : k + 1] for k in range(4))
        rv = r_ref[...]
        wv = w_ref[...]
        first = rho / (rho + mu)
        gap = (nu - mu * (mu / rho)) * (first * first)
        beta = gap / rho
        cr = mu / (rho + mu) + beta
        curvature = cr * cr * (rho + mu) - 2.0 * cr * first * (mu + nu) + first * first * (nu + xi)
        second = gap / curvature
        sol_ref[...] = (first + second * cr) * rv - (second * first) * wv
        res_ref[...] = (
            (mu / (rho + mu) - second * cr) * rv
            + (second * (first - cr) - first) * wv
            + (second * first) * w2_ref[...]
        )

    return pl.pallas_call(
        body,
        out_shape=(f32(8, n), f32(8, n)),
        in_specs=[VM] * 4,
        out_specs=(VM, VM),
        compiler_params=params(),
        name="finish",
    )(gathered, r, w, w2)


def on_device(points, targets, partner_tiles):
    dev_count = lax.axis_size("dev")
    to_right = [(i, i + 1) for i in range(dev_count - 1)]
    to_left = [(i + 1, i) for i in range(dev_count - 1)]

    def right_of(x):
        return lax.ppermute(x, "dev", to_left)

    def left_of(x):
        return lax.ppermute(x, "dev", to_right)

    def swap(x, k):
        return lax.ppermute(x, "group", [(i, i ^ k) for i in range(8)])

    def trade(x, axis="group"):
        return lax.all_to_all(x, axis, split_axis=0, concat_axis=0, tiled=True)

    table, own, *outgoing = prep(jnp.transpose(partner_tiles, (0, 2, 3, 1)), points, targets)
    arrived = dict(zip(SWAPS, [swap(x, k) for x, k in zip(outgoing, SWAPS)]))
    left, right = left_of(own), right_of(own)
    k_local, acc_local = local_first(own)

    def cross(stage, after):
        return cross_first(stage, table, own, [arrived[k] for k in stage], after)

    k_a, row_a, *col_a = cross(STAGES[0], acc_local)
    k_b, row_b, *col_b = cross(STAGES[1], row_a)
    ret_near = [swap(x, k) for x, k in zip(col_a + col_b, SWAPS)]
    k_band, to_r, to_l, acc_band = band_first(left, own, right, [row_b, *ret_near])
    from_left, from_right = left_of(to_r), right_of(to_l)
    k_c, row_c, *col_c = cross(STAGES[2], acc_band)
    ret = ret_near + [swap(x, k) for x, k in zip(col_c, STAGES[2])]
    *xw_out, w, deg, sums = combine(
        table, targets, (acc_local, acc_band, from_left, from_right, row_a, row_b, row_c), ret
    )
    w_left, w_right = left_of(w), right_of(w)
    xw = [swap(x, k) for x, k in zip(xw_out, SWAPS)]
    loc2 = local_second(k_local, w)
    col_r, rowl_b, rowo_b = band_second(k_band, w_left, w, w_right, loc2)
    from_left2, from_right2 = left_of(col_r), right_of(rowl_b)
    near2, row_near2 = cross_second(STAGES[:2], table, (k_a, k_b), w, xw[:5], [rowo_b])
    far2, row_far2 = cross_second(STAGES[2:], table, (k_c,), w, xw[5:], [row_near2, from_left2, from_right2])
    ret2 = trade(pack(near2, far2, w, sums, loc2, rowl_b, rowo_b, (row_near2, row_far2), w_left))
    w2, column = group_sum(table, w, deg, (loc2, rowo_b, row_near2, row_far2, from_left2, from_right2), ret2)
    return finish(trade(column, "dev"), targets, w, w2)


def solution(mesh):
    return jax.shard_map(
        on_device,
        mesh=mesh,
        in_specs=(P(("group", "dev"), None), P(None, ("group", "dev")), P()),
        out_specs=(P(None, ("group", "dev")), P(None, ("group", "dev"))),
        check_vma=False,
    )
```

```python
import jax
import jax.numpy as jnp
from jax import lax
from jax.experimental import pallas as pl
from jax.experimental.pallas import tpu as pltpu
from jax.sharding import PartitionSpec as P

TILE = 256
EXTRA = 8
SCALE = 3.9
C4 = 4.0 / SCALE**5
CUT = 5.0 * SCALE / 4.0
NT = (((1,), (1,)), ((), ()))
NN = (((1,), (0,)), ((), ()))
F32 = jnp.float32
BF16 = jnp.bfloat16
STAGES = ((2, 6, 1), (3, 7), (4, 5))
SWAPS = STAGES[0] + STAGES[1] + STAGES[2]

SMEM = pl.BlockSpec(memory_space=pltpu.SMEM)
ANY = pl.BlockSpec(memory_space=pl.ANY)
HBM = pl.BlockSpec(memory_space=pltpu.HBM)
VM = pl.BlockSpec(memory_space=pltpu.VMEM)


def mm(a, b, dims):
    return lax.dot_general(a, b, dims, preferred_element_type=F32)


def col_norms(x):
    x = x.astype(F32)
    return jnp.broadcast_to(jnp.sum(x * x, axis=1, keepdims=True), (x.shape[0], 128))


def row_norms(x):
    return col_norms(x).T[0:1, :]


def kernel_tile(a, b_scaled, na, nb):
    q = mm(a, b_scaled, NT) + (jnp.concatenate([na, na], axis=1) + nb)
    q = jnp.maximum(q, 1e-30)
    u = jnp.maximum(SCALE - q * lax.rsqrt(q), 0.0)
    t = u * u
    return (t * t * (CUT - u)).astype(BF16)


def split(v):
    hi = v.astype(BF16)
    lo = (v - hi.astype(F32)).astype(BF16)
    return jnp.concatenate([hi, lo], axis=0)


def rhs_ones(rows, one):
    v = rows.astype(F32)
    return jnp.concatenate([v[:, 0:TILE], v[:, TILE:], jnp.full((16, TILE), one, F32)], axis=0).astype(BF16)


def fold(acc):
    return (acc[0:8] + acc[8:16]) * C4


def fold_ones(acc):
    return jnp.concatenate([acc[0:8] + acc[8:16], acc[16:24]], axis=0) * C4


def span(t):
    return pl.ds(pl.multiple_of(t * TILE, TILE), TILE)


def params(mib=12):
    return pltpu.CompilerParams(vmem_limit_bytes=mib * 1024 * 1024)


def f32(*shape):
    return jax.ShapeDtypeStruct(shape, F32)


def vmem_bf16(*shape):
    return pltpu.VMEM(shape, BF16)


def prep(partners, points, targets):
    n, d = points.shape
    nt = n // TILE

    def body(p_hbm, pts_ref, r_hbm, table_ref, msg_ref, *refs):
        outs, (r_ref, p_ref, sems) = refs[:-3], refs[-3:]
        g = lax.axis_index("group")
        dev = lax.axis_index("dev")
        copies = [pltpu.make_async_copy(r_hbm, r_ref, sems.at[nt])]
        for t in range(nt):
            s = slice(t * TILE, (t + 1) * TILE)
            copies.append(pltpu.make_async_copy(pts_ref.at[s, :], msg_ref.at[t, pl.ds(0, TILE), :], sems.at[t]))
        table_copy = pltpu.make_async_copy(p_hbm, p_ref, sems.at[nt + 1])
        table_copy.start()
        for cp in copies:
            cp.start()
        table_copy.wait()
        for h in range(8):
            for c in range(2):
                table_ref[h * 2 + c] = p_ref[h, g, c, dev]
                table_ref[16 + h * 2 + c] = p_ref[g, h, c, dev]
        for cp in copies:
            cp.wait()
        for t in range(nt):
            s = slice(t * TILE, (t + 1) * TILE)
            v = r_ref[:, s]
            hi = v.astype(BF16).astype(F32)
            msg_ref[t, TILE:, :] = jnp.concatenate([hi, v - hi], axis=1).astype(BF16)
        for k, out in zip(SWAPS, outs):
            for c in range(2):
                out[c] = msg_ref[jnp.maximum(p_ref[g ^ k, g, c, dev], 0)]

    return pl.pallas_call(
        body,
        out_shape=[jax.ShapeDtypeStruct((32,), jnp.int32), vmem_bf16(nt, TILE + EXTRA, d)]
        + [vmem_bf16(2, TILE + EXTRA, d) for _ in SWAPS],
        in_specs=[HBM, HBM, HBM],
        out_specs=[SMEM] + [VM] * (1 + len(SWAPS)),
        scratch_shapes=[
            pltpu.VMEM((8, n), F32),
            pltpu.SMEM(partners.shape, jnp.int32),
            pltpu.SemaphoreType.DMA((nt + 2,)),
        ],
        compiler_params=params(),
        name="prep",
    )(*(pltpu.with_memory_space_constraint(x, pltpu.HBM) for x in (partners, points, targets)))


def gate(held, arrived):
    m = len(held)

    def body(*refs):
        pass

    return pl.pallas_call(
        body,
        out_shape=[vmem_bf16(*x.shape) for x in held],
        in_specs=[VM] * m + [ANY] * len(arrived),
        out_specs=[VM] * m,
        input_output_aliases={i: i for i in range(m)},
        compiler_params=params(4),
        name="gate",
    )(*held, *arrived)


def local_first(own):
    nt, _, d = own.shape
    n = nt * TILE

    def body(a_ref, k_ref, acc_ref, na, nb, va):
        for i in range(nt):
            s = slice(i * TILE, (i + 1) * TILE)
            x = col_norms(a_ref[i, 0:TILE, :])
            na[s, :] = x
            nb[:, s] = x.T[0:8]
            va[:, s] = rhs_ones(a_ref[i, TILE:, :], 1.0)

        def step(t, carry):
            s = span(t)
            b = a_ref[t, 0:TILE, :] * jnp.asarray(-2.0, BF16)
            for i in range(nt):
                c = slice(i * TILE, (i + 1) * TILE)
                k_ref[t, c, :] = kernel_tile(a_ref[i, 0:TILE, :], b, na[c, :], nb[0:1, s])
            acc_ref[:, s] = fold_ones(mm(va[...], k_ref[t], NN))
            return carry

        lax.fori_loop(0, nt, step, 0)

    return pl.pallas_call(
        body,
        out_shape=(vmem_bf16(nt, n, TILE), f32(16, n)),
        in_specs=[VM],
        out_specs=(VM, VM),
        scratch_shapes=[pltpu.VMEM((n, 128), F32), pltpu.VMEM((8, n), F32), pltpu.VMEM((32, n), BF16)],
        compiler_params=params(),
        name="local_first",
    )(own)


def band_first(left, own, right, after):
    nt, _, d = own.shape
    n = nt * TILE
    m = len(after)

    def body(l_ref, a_ref, b_ref, *refs):
        k_ref, col_ref, rowl_ref, rowo_ref, na, nb, va, vb, acc = refs[m:]
        v = lax.axis_index("dev")
        has_left = (v > 0).astype(F32)
        has_right = (v < lax.axis_size("dev") - 1).astype(F32)
        for i in range(nt):
            s = slice(i * TILE, (i + 1) * TILE)
            e = slice(n + i * TILE, n + (i + 1) * TILE)
            na[s, :] = col_norms(l_ref[i, 0:TILE, :])
            na[e, :] = col_norms(a_ref[i, 0:TILE, :])
            nb[:, s] = col_norms(b_ref[i, 0:TILE, :]).T[0:8]
            va[:, s] = rhs_ones(l_ref[i, TILE:, :], has_left)
            va[:, e] = rhs_ones(a_ref[i, TILE:, :], 1.0)
            vb[:, s] = rhs_ones(b_ref[i, TILE:, :], has_right)
        acc[...] = jnp.zeros_like(acc)

        def step(t, carry):
            s = span(t)
            b = b_ref[t, 0:TILE, :] * jnp.asarray(-2.0, BF16)
            for j, x in enumerate((l_ref, a_ref)):
                for i in range(nt):
                    e = slice((j * nt + i) * TILE, (j * nt + i + 1) * TILE)
                    k_ref[t, e, :] = kernel_tile(x[i, 0:TILE, :], b, na[e, :], nb[0:1, s])
            k = k_ref[t]
            col_ref[:, s] = fold_ones(mm(va[...], k, NN))
            acc[...] += mm(vb[:, s], k, NT)
            return carry

        lax.fori_loop(0, nt, step, 0)
        rows = fold_ones(acc[...])
        rowl_ref[...] = rows[:, 0:n]
        rowo_ref[...] = rows[:, n:]

    return pl.pallas_call(
        body,
        out_shape=(vmem_bf16(nt, 2 * n, TILE), f32(16, n), f32(16, n), f32(16, n)),
        in_specs=[VM] * 3 + [ANY] * m,
        out_specs=(VM,) * 4,
        scratch_shapes=[
            pltpu.VMEM((2 * n, 128), F32),
            pltpu.VMEM((8, n), F32),
            pltpu.VMEM((32, 2 * n), BF16),
            pltpu.VMEM((32, n), BF16),
            pltpu.VMEM((32, 2 * n), F32),
        ],
        compiler_params=params(),
        name="band_first",
    )(left, own, right, *after)


def cross_first(ks, table, own, tiles, after, held=()):
    nt, _, d = own.shape
    n = nt * TILE
    m = len(ks)
    slots = 2 * m
    p = len(held)

    def body(q_ref, a_ref, _, *refs):
        tile_refs = refs[:m]
        k_ref, row_ref, *cols = refs[m + p : 2 * m + p + 2]
        buf, jobs, sems, na, va, acc, nb, col = refs[2 * m + 2 * p + 2 :]
        g = lax.axis_index("group")
        count = jnp.int32(0)
        for i, k in enumerate(ks):
            for c in range(2):
                live = q_ref[16 + (g ^ k) * 2 + c] >= 0

                @pl.when(live)
                def _(count=count, i=i, k=k, c=c):
                    pltpu.make_async_copy(tile_refs[i].at[c], buf.at[count], sems.at[count]).start()
                    jobs[count] = 2 * i + c

                count = count + live.astype(jnp.int32)
        for i in range(nt):
            s = slice(i * TILE, (i + 1) * TILE)
            na[s, :] = col_norms(a_ref[i, 0:TILE, :])
            va[:, s] = rhs_ones(a_ref[i, TILE:, :], 1.0)
        acc[...] = jnp.zeros_like(acc)

        def step(j, carry):
            pltpu.make_async_copy(tile_refs[0].at[0], buf.at[j], sems.at[j]).wait()
            b = buf[j, 0:TILE, :]
            nb[...] = col_norms(b).T[0:8]
            b = b * jnp.asarray(-2.0, BF16)
            vb = rhs_ones(buf[j, TILE:, :], 1.0)
            for i in range(nt):
                c = slice(i * TILE, (i + 1) * TILE)
                k_ref[j, c, :] = kernel_tile(a_ref[i, 0:TILE, :], b, na[c, :], nb[0:1, :])
            k = k_ref[j]
            col[jobs[j]] = fold_ones(mm(va[...], k, NN))
            acc[...] += mm(vb, k, NT)
            return carry

        lax.fori_loop(0, count, step, 0)
        row_ref[...] = fold_ones(acc[...])
        for i, out in enumerate(cols):
            out[...] = col[2 * i : 2 * i + 2]

    return pl.pallas_call(
        body,
        out_shape=[vmem_bf16(slots, n, TILE), f32(16, n)] + [f32(2, 16, TILE)] * (m + p),
        in_specs=[SMEM, VM, ANY] + [ANY] * m + [VM] * p,
        out_specs=[VM] * (2 + m + p),
        input_output_aliases={3 + m + i: 2 + m + i for i in range(p)},
        scratch_shapes=[
            pltpu.VMEM((slots, TILE + EXTRA, d), BF16),
            pltpu.SMEM((slots,), jnp.int32),
            pltpu.SemaphoreType.DMA((slots,)),
            pltpu.VMEM((n, 128), F32),
            pltpu.VMEM((32, n), BF16),
            pltpu.VMEM((32, n), F32),
            pltpu.VMEM((8, TILE), F32),
            pltpu.VMEM((slots, 16, TILE), F32),
        ],
        compiler_params=params(),
        name=f"cross_first_{ks[0]}",
    )(table, own, after, *tiles, *held)


def combine(table, r, parts, ret):
    n = r.shape[1]
    m = len(parts)

    def body(q_ref, r_ref, *refs):
        part_refs, (*x_refs, w_ref, deg_ref, sum_ref, acc) = refs[:m], refs[m:]
        x_refs, out_refs = x_refs[:7], x_refs[7:]
        g = lax.axis_index("group")
        total = part_refs[0][...]
        for p in part_refs[1:]:
            total = total + p[...]
        acc[...] = total
        for k, x in zip(SWAPS, x_refs):
            for c in range(2):
                t = q_ref[(g ^ k) * 2 + c]

                @pl.when(t >= 0)
                def _(x=x, c=c, t=t):
                    acc[:, span(t)] = acc[:, span(t)] + x[c]

        rv = r_ref[...]
        deg = acc[8:16, :]
        w = 0.5 * (deg * rv - acc[0:8, :])
        w_ref[...] = w
        deg_ref[...] = deg
        for k, out in zip(SWAPS, out_refs):
            for c in range(2):
                t = jnp.maximum(q_ref[(g ^ k) * 2 + c], 0)
                out[c * 8 : c * 8 + 8, :] = w_ref[:, span(t)]
        lane = lax.broadcasted_iota(jnp.int32, (8, 128), 1)
        sums = jnp.zeros((8, 128), F32)
        for k, v in enumerate((rv * rv, rv * w, w * w, 0.5 * deg * w * w)):
            sums = jnp.where(lane == k, jnp.sum(v, axis=1, keepdims=True), sums)
        sum_ref[...] = sums

    return pl.pallas_call(
        body,
        out_shape=[f32(16, TILE)] * 7 + [f32(8, n), f32(8, n), f32(8, 128)],
        in_specs=[SMEM] + [VM] * (m + 8),
        out_specs=[VM] * 10,
        scratch_shapes=[pltpu.VMEM((16, n), F32)],
        compiler_params=params(),
        name="combine",
    )(table, r, *parts, *ret)


def local_second(k_local, w):
    nt, n, _ = k_local.shape

    def body(k_ref, w_ref, out_ref):
        va = split(w_ref[...])
        for t in range(nt):
            out_ref[:, t * TILE : (t + 1) * TILE] = fold(mm(va, k_ref[t], NN))

    return pl.pallas_call(
        body,
        out_shape=f32(8, n),
        in_specs=[VM, VM],
        out_specs=VM,
        compiler_params=params(),
        name="local_second",
    )(k_local, w)


def band_second(k_band, w_left, w, w_right, after):
    nt, n2, _ = k_band.shape
    n = n2 // 2

    def body(k_ref, wl_ref, w_ref, wb_ref, _, col_ref, rowl_ref, rowo_ref, va, acc):
        va[:, 0:n] = split(wl_ref[...])
        va[:, n:] = split(w_ref[...])
        vb = split(wb_ref[...])
        for t in range(nt):
            s = slice(t * TILE, (t + 1) * TILE)
            col_ref[:, s] = fold(mm(va[...], k_ref[t], NN))
            new = mm(vb[:, s], k_ref[t], NT)
            acc[...] = new if t == 0 else acc[...] + new
        rows = fold(acc[...])
        rowl_ref[...] = rows[:, 0:n]
        rowo_ref[...] = rows[:, n:]

    return pl.pallas_call(
        body,
        out_shape=(f32(8, n), f32(8, n), f32(8, n)),
        in_specs=[VM] * 4 + [ANY],
        out_specs=(VM,) * 3,
        scratch_shapes=[pltpu.VMEM((16, n2), BF16), pltpu.VMEM((16, n2), F32)],
        compiler_params=params(),
        name="band_second",
    )(k_band, w_left, w, w_right, after)


def cross_second(table, k_caches, w, xw, sums, loc, row_left, row_own, w_left):
    n = w.shape[1]

    def body(
        q_ref, ka_ref, kb_ref, kc_ref, w_ref, sum_ref, loc_ref, rl_ref, ro_ref, wl_ref, *refs
    ):
        xw_refs, (col_ref, row_ref, va, acc, jobs, xw_ref) = refs[:7], refs[7:]
        g = lax.axis_index("group")
        for k, x in zip(SWAPS, xw_refs):
            xw_ref[g ^ k] = x[...]
        va[...] = split(w_ref[...])
        acc[...] = jnp.zeros_like(acc)
        for ks, k_ref in zip(STAGES, (ka_ref, kb_ref, kc_ref)):
            count = jnp.int32(0)
            for k in ks:
                for c in range(2):
                    live = q_ref[16 + (g ^ k) * 2 + c] >= 0

                    @pl.when(live)
                    def _(count=count, k=k, c=c):
                        jobs[count] = (g ^ k) * 2 + c

                    count = count + live.astype(jnp.int32)

            def step(j, carry, k_ref=k_ref):
                slot = jobs[j]
                h, c = slot >> 1, slot & 1
                rows = pl.ds(pl.multiple_of(c * 8, 8), 8)
                k = k_ref[j]
                col_ref[h, rows, :] = fold(mm(va[...], k, NN))
                acc[...] += mm(split(xw_ref[h, rows, :]), k, NT)
                return carry

            lax.fori_loop(0, count, step, 0)
        row = fold(acc[...])
        row_ref[...] = row
        pairs = w_ref[...] * (0.5 * loc_ref[...] + ro_ref[...] + row) + wl_ref[...] * rl_ref[...]
        lane = lax.broadcasted_iota(jnp.int32, (8, 128), 1)
        pay = jnp.where(lane == 3, sum_ref[...] - jnp.sum(pairs, axis=1, keepdims=True), sum_ref[...])
        for h in range(8):
            col_ref[h, 16:24, 0:128] = pay
            col_ref[h, 16:24, 128:] = jnp.zeros((8, 128), F32)

    return pl.pallas_call(
        body,
        out_shape=(f32(8, 24, TILE), f32(8, n)),
        in_specs=[SMEM] + [VM] * 16,
        out_specs=(VM, VM),
        scratch_shapes=[
            pltpu.VMEM((16, n), BF16),
            pltpu.VMEM((16, n), F32),
            pltpu.SMEM((16,), jnp.int32),
            pltpu.VMEM((8, 16, TILE), F32),
        ],
        compiler_params=params(),
        name="cross_second",
    )(table, *k_caches, w, sums, loc, row_left, row_own, w_left, *xw)


def group_sum(table, w, deg, parts, ret):
    n = w.shape[1]
    m = len(parts)

    def body(q_ref, w_ref, deg_ref, *refs):
        part_refs, (x_ref, w2_ref, out_ref, acc) = refs[:m], refs[m:]
        total = part_refs[0][...]
        for p in part_refs[1:]:
            total = total + p[...]
        acc[...] = total
        for h in range(8):
            for c in range(2):
                t = q_ref[h * 2 + c]

                @pl.when(t >= 0)
                def _(h=h, c=c, t=t):
                    acc[:, span(t)] = acc[:, span(t)] + x_ref[h, c * 8 : c * 8 + 8, :]

        w2_ref[...] = 0.5 * (deg_ref[...] * w_ref[...] - acc[...])
        sums = x_ref[0, 16:24, 0:128]
        for h in range(1, 8):
            sums = sums + x_ref[h, 16:24, 0:128]
        for v in range(16):
            out_ref[v] = sums

    return pl.pallas_call(
        body,
        out_shape=(f32(8, n), f32(16, 8, 128)),
        in_specs=[SMEM] + [VM] * (3 + m),
        out_specs=(VM, VM),
        scratch_shapes=[pltpu.VMEM((8, n), F32)],
        compiler_params=params(),
        name="group_sum",
    )(table, w, deg, *parts, ret)


def finish(gathered, r, w, w2):
    n = r.shape[1]

    def body(g_ref, r_ref, w_ref, w2_ref, sol_ref, res_ref):
        sums = g_ref[0]
        for v in range(1, 16):
            sums = sums + g_ref[v]
        rho, mu, nu, xi = (sums[:, k : k + 1] for k in range(4))
        rv = r_ref[...]
        wv = w_ref[...]
        first = rho / (rho + mu)
        gap = (nu - mu * (mu / rho)) * (first * first)
        beta = gap / rho
        cr = mu / (rho + mu) + beta
        curvature = cr * cr * (rho + mu) - 2.0 * cr * first * (mu + nu) + first * first * (nu + xi)
        second = gap / curvature
        sol_ref[...] = (first + second * cr) * rv - (second * first) * wv
        res_ref[...] = (
            (mu / (rho + mu) - second * cr) * rv
            + (second * (first - cr) - first) * wv
            + (second * first) * w2_ref[...]
        )

    return pl.pallas_call(
        body,
        out_shape=(f32(8, n), f32(8, n)),
        in_specs=[VM] * 4,
        out_specs=(VM, VM),
        compiler_params=params(),
        name="finish",
    )(gathered, r, w, w2)


def on_device(points, targets, partner_tiles):
    dev_count = lax.axis_size("dev")
    to_right = [(i, i + 1) for i in range(dev_count - 1)]
    to_left = [(i + 1, i) for i in range(dev_count - 1)]

    def right_of(x):
        return lax.ppermute(x, "dev", to_left)

    def left_of(x):
        return lax.ppermute(x, "dev", to_right)

    def swap(x, k):
        return lax.ppermute(x, "group", [(i, i ^ k) for i in range(8)])

    def trade(x, axis="group"):
        return lax.all_to_all(x, axis, split_axis=0, concat_axis=0, tiled=True)

    table, own, *outgoing = prep(jnp.transpose(partner_tiles, (0, 2, 3, 1)), points, targets)
    arrived = dict(zip(SWAPS[:5], [swap(x, k) for x, k in zip(outgoing, SWAPS[:5])]))
    left, right = left_of(own), right_of(own)
    k_local, acc_local = local_first(own)

    def cross(stage, after, held=()):
        return cross_first(stage, table, own, [arrived[k] for k in stage], after, held)

    k_a, row_a, *col_a = cross(STAGES[0], acc_local)
    for x, k in zip(gate(outgoing[5:], [row_a]), STAGES[2]):
        arrived[k] = swap(x, k)
    k_b, row_b, *col_b = cross(STAGES[1], row_a, col_a)
    ret_near = [swap(x, k) for x, k in zip(col_b, STAGES[1] + STAGES[0])]
    k_band, to_r, to_l, acc_band = band_first(left, own, right, [row_b, *ret_near])
    from_left, from_right = left_of(to_r), right_of(to_l)
    k_c, row_c, *col_c = cross(STAGES[2], acc_band)
    ret = ret_near[2:] + ret_near[:2] + [swap(x, k) for x, k in zip(col_c, STAGES[2])]
    *xw_out, w, deg, sums = combine(
        table, targets, (acc_local, acc_band, from_left, from_right, row_a, row_b, row_c), ret
    )
    w_left, w_right = left_of(w), right_of(w)
    xw = [swap(x, k) for x, k in zip(xw_out, SWAPS)]
    loc2 = local_second(k_local, w)
    col_r, rowl_b, rowo_b = band_second(k_band, w_left, w, w_right, loc2)
    from_left2, from_right2 = left_of(col_r), right_of(rowl_b)
    col_x, row_x = cross_second(table, (k_a, k_b, k_c), w, xw, sums, loc2, rowl_b, rowo_b, w_left)
    w2, column = group_sum(table, w, deg, (loc2, rowo_b, row_x, from_left2, from_right2), trade(col_x))
    return finish(trade(column, "dev"), targets, w, w2)


def solution(mesh):
    return jax.shard_map(
        on_device,
        mesh=mesh,
        in_specs=(P(("group", "dev"), None), P(None, ("group", "dev")), P()),
        out_specs=(P(None, ("group", "dev")), P(None, ("group", "dev"))),
        check_vma=False,
    )
```

```python
import jax
import jax.numpy as jnp
from jax import lax
from jax.experimental import pallas as pl
from jax.experimental.pallas import tpu as pltpu
from jax.sharding import PartitionSpec as P

TILE = 256
EXTRA = 8
SCALE = 3.9
C4 = 4.0 / SCALE**5
CUT = 5.0 * SCALE / 4.0
NT = (((1,), (1,)), ((), ()))
NN = (((1,), (0,)), ((), ()))
F32 = jnp.float32
BF16 = jnp.bfloat16
STAGES = ((2, 6, 1), (3, 7), (4, 5))
SWAPS = STAGES[0] + STAGES[1] + STAGES[2]

SMEM = pl.BlockSpec(memory_space=pltpu.SMEM)
ANY = pl.BlockSpec(memory_space=pl.ANY)
HBM = pl.BlockSpec(memory_space=pltpu.HBM)
VM = pl.BlockSpec(memory_space=pltpu.VMEM)


def mm(a, b, dims):
    return lax.dot_general(a, b, dims, preferred_element_type=F32)


def col_norms(x):
    x = x.astype(F32)
    return jnp.broadcast_to(jnp.sum(x * x, axis=1, keepdims=True), (x.shape[0], 128))


def row_norms(x):
    return col_norms(x).T[0:1, :]


def kernel_tile(a, b_scaled, na, nb):
    q = mm(a, b_scaled, NT) + (jnp.concatenate([na, na], axis=1) + nb)
    q = jnp.maximum(q, 1e-30)
    u = jnp.maximum(SCALE - q * lax.rsqrt(q), 0.0)
    t = u * u
    return (t * t * (CUT - u)).astype(BF16)


def split(v):
    hi = v.astype(BF16)
    lo = (v - hi.astype(F32)).astype(BF16)
    return jnp.concatenate([hi, lo], axis=0)


def rhs_ones(rows, one):
    v = rows.astype(F32)
    return jnp.concatenate([v[:, 0:TILE], v[:, TILE:], jnp.full((16, TILE), one, F32)], axis=0).astype(BF16)


def fold(acc):
    return (acc[0:8] + acc[8:16]) * C4


def fold_ones(acc):
    return jnp.concatenate([acc[0:8] + acc[8:16], acc[16:24]], axis=0) * C4


def span(t):
    return pl.ds(pl.multiple_of(t * TILE, TILE), TILE)


def params(mib=12):
    return pltpu.CompilerParams(vmem_limit_bytes=mib * 1024 * 1024)


def f32(*shape):
    return jax.ShapeDtypeStruct(shape, F32)


def vmem_bf16(*shape):
    return pltpu.VMEM(shape, BF16)


def prep(partners, points, targets):
    n, d = points.shape
    nt = n // TILE

    def body(p_hbm, pts_ref, r_hbm, table_ref, msg_ref, *refs):
        outs, (r_ref, p_ref, sems) = refs[:-3], refs[-3:]
        g = lax.axis_index("group")
        dev = lax.axis_index("dev")
        copies = [pltpu.make_async_copy(r_hbm, r_ref, sems.at[nt])]
        for t in range(nt):
            s = slice(t * TILE, (t + 1) * TILE)
            copies.append(pltpu.make_async_copy(pts_ref.at[s, :], msg_ref.at[t, pl.ds(0, TILE), :], sems.at[t]))
        table_copy = pltpu.make_async_copy(p_hbm, p_ref, sems.at[nt + 1])
        table_copy.start()
        for cp in copies:
            cp.start()
        table_copy.wait()
        for h in range(8):
            for c in range(2):
                table_ref[h * 2 + c] = p_ref[h, g, c, dev]
                table_ref[16 + h * 2 + c] = p_ref[g, h, c, dev]
        for cp in copies:
            cp.wait()
        for t in range(nt):
            s = slice(t * TILE, (t + 1) * TILE)
            v = r_ref[:, s]
            hi = v.astype(BF16).astype(F32)
            msg_ref[t, TILE:, :] = jnp.concatenate([hi, v - hi], axis=1).astype(BF16)
        for k, out in zip(SWAPS, outs):
            for c in range(2):
                out[c] = msg_ref[jnp.maximum(p_ref[g ^ k, g, c, dev], 0)]

    return pl.pallas_call(
        body,
        out_shape=[jax.ShapeDtypeStruct((32,), jnp.int32), vmem_bf16(nt, TILE + EXTRA, d)]
        + [vmem_bf16(2, TILE + EXTRA, d) for _ in SWAPS],
        in_specs=[HBM, HBM, HBM],
        out_specs=[SMEM] + [VM] * (1 + len(SWAPS)),
        scratch_shapes=[
            pltpu.VMEM((8, n), F32),
            pltpu.SMEM(partners.shape, jnp.int32),
            pltpu.SemaphoreType.DMA((nt + 2,)),
        ],
        compiler_params=params(),
        name="prep",
    )(*(pltpu.with_memory_space_constraint(x, pltpu.HBM) for x in (partners, points, targets)))


def gate(held, arrived):
    m = len(held)

    def body(*refs):
        pass

    return pl.pallas_call(
        body,
        out_shape=[vmem_bf16(*x.shape) for x in held],
        in_specs=[VM] * m + [ANY] * len(arrived),
        out_specs=[VM] * m,
        input_output_aliases={i: i for i in range(m)},
        compiler_params=params(4),
        name="gate",
    )(*held, *arrived)


def local_first(own):
    nt, _, d = own.shape
    n = nt * TILE

    def body(a_ref, k_ref, acc_ref, na, nb, va):
        for i in range(nt):
            s = slice(i * TILE, (i + 1) * TILE)
            x = col_norms(a_ref[i, 0:TILE, :])
            na[s, :] = x
            nb[:, s] = x.T[0:8]
            va[:, s] = rhs_ones(a_ref[i, TILE:, :], 1.0)

        def step(t, carry):
            s = span(t)
            b = a_ref[t, 0:TILE, :] * jnp.asarray(-2.0, BF16)
            for i in range(nt):
                c = slice(i * TILE, (i + 1) * TILE)
                k_ref[t, c, :] = kernel_tile(a_ref[i, 0:TILE, :], b, na[c, :], nb[0:1, s])
            acc_ref[:, s] = fold_ones(mm(va[...], k_ref[t], NN))
            return carry

        lax.fori_loop(0, nt, step, 0)

    return pl.pallas_call(
        body,
        out_shape=(vmem_bf16(nt, n, TILE), f32(16, n)),
        in_specs=[VM],
        out_specs=(VM, VM),
        scratch_shapes=[pltpu.VMEM((n, 128), F32), pltpu.VMEM((8, n), F32), pltpu.VMEM((32, n), BF16)],
        compiler_params=params(),
        name="local_first",
    )(own)


def band_first(left, own, right, after):
    nt, _, d = own.shape
    n = nt * TILE
    m = len(after)

    def body(l_ref, a_ref, b_ref, *refs):
        k_ref, col_ref, rowl_ref, rowo_ref, na, nb, va, vb, acc = refs[m:]
        v = lax.axis_index("dev")
        has_left = (v > 0).astype(F32)
        has_right = (v < lax.axis_size("dev") - 1).astype(F32)
        for i in range(nt):
            s = slice(i * TILE, (i + 1) * TILE)
            e = slice(n + i * TILE, n + (i + 1) * TILE)
            na[s, :] = col_norms(l_ref[i, 0:TILE, :])
            na[e, :] = col_norms(a_ref[i, 0:TILE, :])
            nb[:, s] = col_norms(b_ref[i, 0:TILE, :]).T[0:8]
            va[:, s] = rhs_ones(l_ref[i, TILE:, :], has_left)
            va[:, e] = rhs_ones(a_ref[i, TILE:, :], 1.0)
            vb[:, s] = rhs_ones(b_ref[i, TILE:, :], has_right)
        acc[...] = jnp.zeros_like(acc)

        def step(t, carry):
            s = span(t)
            b = b_ref[t, 0:TILE, :] * jnp.asarray(-2.0, BF16)
            for j, x in enumerate((l_ref, a_ref)):
                for i in range(nt):
                    e = slice((j * nt + i) * TILE, (j * nt + i + 1) * TILE)
                    k_ref[t, e, :] = kernel_tile(x[i, 0:TILE, :], b, na[e, :], nb[0:1, s])
            k = k_ref[t]
            col_ref[:, s] = fold_ones(mm(va[...], k, NN))
            acc[...] += mm(vb[:, s], k, NT)
            return carry

        lax.fori_loop(0, nt, step, 0)
        rows = fold_ones(acc[...])
        rowl_ref[...] = rows[:, 0:n]
        rowo_ref[...] = rows[:, n:]

    return pl.pallas_call(
        body,
        out_shape=(vmem_bf16(nt, 2 * n, TILE), f32(16, n), f32(16, n), f32(16, n)),
        in_specs=[VM] * 3 + [ANY] * m,
        out_specs=(VM,) * 4,
        scratch_shapes=[
            pltpu.VMEM((2 * n, 128), F32),
            pltpu.VMEM((8, n), F32),
            pltpu.VMEM((32, 2 * n), BF16),
            pltpu.VMEM((32, n), BF16),
            pltpu.VMEM((32, 2 * n), F32),
        ],
        compiler_params=params(),
        name="band_first",
    )(left, own, right, *after)


def cross_first(ks, table, own, tiles, after, held=()):
    nt, _, d = own.shape
    n = nt * TILE
    m = len(ks)
    slots = 2 * m
    p = len(held)

    def body(q_ref, a_ref, _, *refs):
        tile_refs = refs[:m]
        k_ref, row_ref, *cols = refs[m + p : 2 * m + p + 2]
        buf, jobs, sems, na, va, acc, nb, col = refs[2 * m + 2 * p + 2 :]
        g = lax.axis_index("group")
        count = jnp.int32(0)
        for i, k in enumerate(ks):
            for c in range(2):
                live = q_ref[16 + (g ^ k) * 2 + c] >= 0

                @pl.when(live)
                def _(count=count, i=i, k=k, c=c):
                    pltpu.make_async_copy(tile_refs[i].at[c], buf.at[count], sems.at[count]).start()
                    jobs[count] = 2 * i + c

                count = count + live.astype(jnp.int32)
        for i in range(nt):
            s = slice(i * TILE, (i + 1) * TILE)
            na[s, :] = col_norms(a_ref[i, 0:TILE, :])
            va[:, s] = rhs_ones(a_ref[i, TILE:, :], 1.0)
        acc[...] = jnp.zeros_like(acc)

        def step(j, carry):
            pltpu.make_async_copy(tile_refs[0].at[0], buf.at[j], sems.at[j]).wait()
            b = buf[j, 0:TILE, :]
            nb[...] = col_norms(b).T[0:8]
            b = b * jnp.asarray(-2.0, BF16)
            vb = rhs_ones(buf[j, TILE:, :], 1.0)
            for i in range(nt):
                c = slice(i * TILE, (i + 1) * TILE)
                k_ref[j, c, :] = kernel_tile(a_ref[i, 0:TILE, :], b, na[c, :], nb[0:1, :])
            k = k_ref[j]
            col[jobs[j]] = fold_ones(mm(va[...], k, NN))
            acc[...] += mm(vb, k, NT)
            return carry

        lax.fori_loop(0, count, step, 0)
        row_ref[...] = fold_ones(acc[...])
        for i, out in enumerate(cols):
            out[...] = col[2 * i : 2 * i + 2]

    return pl.pallas_call(
        body,
        out_shape=[vmem_bf16(slots, n, TILE), f32(16, n)] + [f32(2, 16, TILE)] * (m + p),
        in_specs=[SMEM, VM, ANY] + [ANY] * m + [VM] * p,
        out_specs=[VM] * (2 + m + p),
        input_output_aliases={3 + m + i: 2 + m + i for i in range(p)},
        scratch_shapes=[
            pltpu.VMEM((slots, TILE + EXTRA, d), BF16),
            pltpu.SMEM((slots,), jnp.int32),
            pltpu.SemaphoreType.DMA((slots,)),
            pltpu.VMEM((n, 128), F32),
            pltpu.VMEM((32, n), BF16),
            pltpu.VMEM((32, n), F32),
            pltpu.VMEM((8, TILE), F32),
            pltpu.VMEM((slots, 16, TILE), F32),
        ],
        compiler_params=params(),
        name=f"cross_first_{ks[0]}",
    )(table, own, after, *tiles, *held)


def combine(table, r, parts, ret):
    n = r.shape[1]
    m = len(parts)

    def body(q_ref, r_ref, *refs):
        part_refs, (*x_refs, w_ref, deg_ref, sum_ref, acc) = refs[:m], refs[m:]
        x_refs, out_refs = x_refs[:7], x_refs[7:]
        g = lax.axis_index("group")
        total = part_refs[0][...]
        for p in part_refs[1:]:
            total = total + p[...]
        acc[...] = total
        for k, x in zip(SWAPS, x_refs):
            for c in range(2):
                t = q_ref[(g ^ k) * 2 + c]

                @pl.when(t >= 0)
                def _(x=x, c=c, t=t):
                    acc[:, span(t)] = acc[:, span(t)] + x[c]

        rv = r_ref[...]
        deg = acc[8:16, :]
        w = 0.5 * (deg * rv - acc[0:8, :])
        w_ref[...] = w
        deg_ref[...] = deg
        for k, out in zip(SWAPS, out_refs):
            for c in range(2):
                t = jnp.maximum(q_ref[(g ^ k) * 2 + c], 0)
                out[c * 8 : c * 8 + 8, :] = w_ref[:, span(t)]
        lane = lax.broadcasted_iota(jnp.int32, (8, 128), 1)
        sums = jnp.zeros((8, 128), F32)
        for k, v in enumerate((rv * rv, rv * w, w * w, 0.5 * deg * w * w)):
            sums = jnp.where(lane == k, jnp.sum(v, axis=1, keepdims=True), sums)
        sum_ref[...] = sums

    return pl.pallas_call(
        body,
        out_shape=[f32(16, TILE)] * 7 + [f32(8, n), f32(8, n), f32(8, 128)],
        in_specs=[SMEM] + [VM] * (m + 8),
        out_specs=[VM] * 10,
        scratch_shapes=[pltpu.VMEM((16, n), F32)],
        compiler_params=params(),
        name="combine",
    )(table, r, *parts, *ret)


def local_second(k_local, w):
    nt, n, _ = k_local.shape

    def body(k_ref, w_ref, out_ref):
        va = split(w_ref[...])
        for t in range(nt):
            out_ref[:, t * TILE : (t + 1) * TILE] = fold(mm(va, k_ref[t], NN))

    return pl.pallas_call(
        body,
        out_shape=f32(8, n),
        in_specs=[VM, VM],
        out_specs=VM,
        compiler_params=params(),
        name="local_second",
    )(k_local, w)


def band_second(k_band, w_left, w, w_right, after):
    nt, n2, _ = k_band.shape
    n = n2 // 2

    def body(k_ref, wl_ref, w_ref, wb_ref, _, col_ref, rowl_ref, rowo_ref, va, acc):
        va[:, 0:n] = split(wl_ref[...])
        va[:, n:] = split(w_ref[...])
        vb = split(wb_ref[...])
        for t in range(nt):
            s = slice(t * TILE, (t + 1) * TILE)
            col_ref[:, s] = fold(mm(va[...], k_ref[t], NN))
            new = mm(vb[:, s], k_ref[t], NT)
            acc[...] = new if t == 0 else acc[...] + new
        rows = fold(acc[...])
        rowl_ref[...] = rows[:, 0:n]
        rowo_ref[...] = rows[:, n:]

    return pl.pallas_call(
        body,
        out_shape=(f32(8, n), f32(8, n), f32(8, n)),
        in_specs=[VM] * 4 + [ANY],
        out_specs=(VM,) * 3,
        scratch_shapes=[pltpu.VMEM((16, n2), BF16), pltpu.VMEM((16, n2), F32)],
        compiler_params=params(),
        name="band_second",
    )(k_band, w_left, w, w_right, after)


def cross_second(table, k_caches, w, xw, sums, loc, row_left, row_own, w_left):
    n = w.shape[1]

    def body(
        q_ref, ka_ref, kb_ref, kc_ref, w_ref, sum_ref, loc_ref, rl_ref, ro_ref, wl_ref, *refs
    ):
        xw_refs, (col_ref, row_ref, va, acc, jobs, xw_ref) = refs[:7], refs[7:]
        g = lax.axis_index("group")
        for k, x in zip(SWAPS, xw_refs):
            xw_ref[g ^ k] = x[...]
        va[...] = split(w_ref[...])
        acc[...] = jnp.zeros_like(acc)
        for ks, k_ref in zip(STAGES, (ka_ref, kb_ref, kc_ref)):
            count = jnp.int32(0)
            for k in ks:
                for c in range(2):
                    live = q_ref[16 + (g ^ k) * 2 + c] >= 0

                    @pl.when(live)
                    def _(count=count, k=k, c=c):
                        jobs[count] = (g ^ k) * 2 + c

                    count = count + live.astype(jnp.int32)

            def step(j, carry, k_ref=k_ref):
                slot = jobs[j]
                h, c = slot >> 1, slot & 1
                rows = pl.ds(pl.multiple_of(c * 8, 8), 8)
                k = k_ref[j]
                col_ref[h, rows, :] = fold(mm(va[...], k, NN))
                acc[...] += mm(split(xw_ref[h, rows, :]), k, NT)
                return carry

            lax.fori_loop(0, count, step, 0)
        row = fold(acc[...])
        row_ref[...] = row
        pairs = w_ref[...] * (0.5 * loc_ref[...] + ro_ref[...] + row) + wl_ref[...] * rl_ref[...]
        lane = lax.broadcasted_iota(jnp.int32, (8, 128), 1)
        pay = jnp.where(lane == 3, sum_ref[...] - jnp.sum(pairs, axis=1, keepdims=True), sum_ref[...])
        for h in range(8):
            col_ref[h, 16:24, 0:128] = pay
            col_ref[h, 16:24, 128:] = jnp.zeros((8, 128), F32)

    return pl.pallas_call(
        body,
        out_shape=(f32(8, 24, TILE), f32(8, n)),
        in_specs=[SMEM] + [VM] * 16,
        out_specs=(VM, VM),
        scratch_shapes=[
            pltpu.VMEM((16, n), BF16),
            pltpu.VMEM((16, n), F32),
            pltpu.SMEM((16,), jnp.int32),
            pltpu.VMEM((8, 16, TILE), F32),
        ],
        compiler_params=params(),
        name="cross_second",
    )(table, *k_caches, w, sums, loc, row_left, row_own, w_left, *xw)


def group_sum(table, w, deg, parts, ret):
    n = w.shape[1]
    m = len(parts)

    def body(q_ref, w_ref, deg_ref, *refs):
        part_refs, (x_ref, w2_ref, out_ref, acc) = refs[:m], refs[m:]
        total = part_refs[0][...]
        for p in part_refs[1:]:
            total = total + p[...]
        acc[...] = total
        for h in range(8):
            for c in range(2):
                t = q_ref[h * 2 + c]

                @pl.when(t >= 0)
                def _(h=h, c=c, t=t):
                    acc[:, span(t)] = acc[:, span(t)] + x_ref[h, c * 8 : c * 8 + 8, :]

        w2_ref[...] = 0.5 * (deg_ref[...] * w_ref[...] - acc[...])
        sums = x_ref[0, 16:24, 0:128]
        for h in range(1, 8):
            sums = sums + x_ref[h, 16:24, 0:128]
        for v in range(16):
            out_ref[v] = sums

    return pl.pallas_call(
        body,
        out_shape=(f32(8, n), f32(16, 8, 128)),
        in_specs=[SMEM] + [VM] * (3 + m),
        out_specs=(VM, VM),
        scratch_shapes=[pltpu.VMEM((8, n), F32)],
        compiler_params=params(),
        name="group_sum",
    )(table, w, deg, *parts, ret)


def finish(gathered, r, w, w2):
    n = r.shape[1]

    def body(g_ref, r_ref, w_ref, w2_ref, sol_ref, res_ref):
        sums = g_ref[0]
        for v in range(1, 16):
            sums = sums + g_ref[v]
        rho, mu, nu, xi = (sums[:, k : k + 1] for k in range(4))
        rv = r_ref[...]
        wv = w_ref[...]
        first = rho / (rho + mu)
        gap = (nu - mu * (mu / rho)) * (first * first)
        beta = gap / rho
        cr = mu / (rho + mu) + beta
        curvature = cr * cr * (rho + mu) - 2.0 * cr * first * (mu + nu) + first * first * (nu + xi)
        second = gap / curvature
        sol_ref[...] = (first + second * cr) * rv - (second * first) * wv
        res_ref[...] = (
            (mu / (rho + mu) - second * cr) * rv
            + (second * (first - cr) - first) * wv
            + (second * first) * w2_ref[...]
        )

    return pl.pallas_call(
        body,
        out_shape=(f32(8, n), f32(8, n)),
        in_specs=[VM] * 4,
        out_specs=(VM, VM),
        compiler_params=params(),
        name="finish",
    )(gathered, r, w, w2)


def on_device(points, targets, partner_tiles):
    dev_count = lax.axis_size("dev")
    to_right = [(i, i + 1) for i in range(dev_count - 1)]
    to_left = [(i + 1, i) for i in range(dev_count - 1)]

    def right_of(x):
        return lax.ppermute(x, "dev", to_left)

    def left_of(x):
        return lax.ppermute(x, "dev", to_right)

    def swap(x, k):
        return lax.ppermute(x, "group", [(i, i ^ k) for i in range(8)])

    def trade(x, axis="group"):
        return lax.all_to_all(x, axis, split_axis=0, concat_axis=0, tiled=True)

    table, own, *outgoing = prep(jnp.transpose(partner_tiles, (0, 2, 3, 1)), points, targets)
    arrived = dict(zip(SWAPS[:5], [swap(x, k) for x, k in zip(outgoing, SWAPS[:5])]))
    left, right = left_of(own), right_of(own)
    k_local, acc_local = local_first(own)

    def cross(stage, after, held=()):
        return cross_first(stage, table, own, [arrived[k] for k in stage], after, held)

    k_a, row_a, *col_a = cross(STAGES[0], acc_local)
    for x, k in zip(gate(outgoing[5:], [row_a, arrived[3], arrived[7]]), STAGES[2]):
        arrived[k] = swap(x, k)
    k_b, row_b, *col_b = cross(STAGES[1], row_a, col_a)
    ret_near = [swap(x, k) for x, k in zip(col_b, STAGES[1] + STAGES[0])]
    k_band, to_r, to_l, acc_band = band_first(left, own, right, [row_b, *ret_near])
    from_left, from_right = left_of(to_r), right_of(to_l)
    k_c, row_c, *col_c = cross(STAGES[2], acc_band)
    ret = ret_near[2:] + ret_near[:2] + [swap(x, k) for x, k in zip(col_c, STAGES[2])]
    *xw_out, w, deg, sums = combine(
        table, targets, (acc_local, acc_band, from_left, from_right, row_a, row_b, row_c), ret
    )
    w_left, w_right = left_of(w), right_of(w)
    xw = [swap(x, k) for x, k in zip(xw_out, SWAPS)]
    loc2 = local_second(k_local, w)
    col_r, rowl_b, rowo_b = band_second(k_band, w_left, w, w_right, loc2)
    from_left2, from_right2 = left_of(col_r), right_of(rowl_b)
    col_x, row_x = cross_second(table, (k_a, k_b, k_c), w, xw, sums, loc2, rowl_b, rowo_b, w_left)
    w2, column = group_sum(table, w, deg, (loc2, rowo_b, row_x, from_left2, from_right2), trade(col_x))
    return finish(trade(column, "dev"), targets, w, w2)


def solution(mesh):
    return jax.shard_map(
        on_device,
        mesh=mesh,
        in_specs=(P(("group", "dev"), None), P(None, ("group", "dev")), P()),
        out_specs=(P(None, ("group", "dev")), P(None, ("group", "dev"))),
        check_vma=False,
    )
```

```python
import jax
import jax.numpy as jnp
from jax import lax
from jax.experimental import pallas as pl
from jax.experimental.pallas import tpu as pltpu
from jax.sharding import PartitionSpec as P


TILE = 256
EXTRA = 8
SCALE = 3.9
C4 = 4.0 / SCALE**5
CUT = 5.0 * SCALE / 4.0
NT = (((1,), (1,)), ((), ()))
NN = (((1,), (0,)), ((), ()))
F32 = jnp.float32
BF16 = jnp.bfloat16
STAGES = ((2, 6, 1), (3, 7), (4, 5))
SWAPS = STAGES[0] + STAGES[1] + STAGES[2]

SMEM = pl.BlockSpec(memory_space=pltpu.SMEM)
ANY = pl.BlockSpec(memory_space=pl.ANY)
HBM = pl.BlockSpec(memory_space=pltpu.HBM)
VM = pl.BlockSpec(memory_space=pltpu.VMEM)


def mm(a, b, dims):
    return lax.dot_general(a, b, dims, preferred_element_type=F32)


def col_norms(x):
    x = x.astype(F32)
    return jnp.broadcast_to(jnp.sum(x * x, axis=1, keepdims=True), (x.shape[0], 128))


def kernel_tile(a, b_scaled, na, nb):
    q = mm(a, b_scaled, NT) + (jnp.concatenate([na, na], axis=1) + nb)
    q = jnp.maximum(q, 1e-30)
    u = jnp.maximum(SCALE - q * lax.rsqrt(q), 0.0)
    t = u * u
    return (t * t * (CUT - u)).astype(BF16)


def split(v):
    hi = v.astype(BF16)
    lo = (v - hi.astype(F32)).astype(BF16)
    return jnp.concatenate([hi, lo], axis=0)


def rhs_ones(rows, one):
    v = rows.astype(F32)
    return jnp.concatenate([v[:, 0:TILE], v[:, TILE:], jnp.full((16, TILE), one, F32)], axis=0).astype(BF16)


def fold(acc):
    return (acc[0:8] + acc[8:16]) * C4


def fold_ones(acc):
    return jnp.concatenate([acc[0:8] + acc[8:16], acc[16:24]], axis=0) * C4


def span(t):
    return pl.ds(pl.multiple_of(t * TILE, TILE), TILE)


def params(mib=12):
    return pltpu.CompilerParams(vmem_limit_bytes=mib * 1024 * 1024)


def f32(*shape):
    return jax.ShapeDtypeStruct(shape, F32)


def vmem_bf16(*shape):
    return pltpu.VMEM(shape, BF16)


def prep(partners, points, targets):
    n, d = points.shape
    nt = n // TILE

    def body(p_hbm, pts_ref, r_hbm, table_ref, msg_ref, *refs):
        outs, (r_ref, p_ref, sems) = refs[:-3], refs[-3:]
        g = lax.axis_index("group")
        dev = lax.axis_index("dev")
        copies = [pltpu.make_async_copy(r_hbm, r_ref, sems.at[nt])]
        for t in range(nt):
            s = slice(t * TILE, (t + 1) * TILE)
            copies.append(pltpu.make_async_copy(pts_ref.at[s, :], msg_ref.at[t, pl.ds(0, TILE), :], sems.at[t]))
        table_copy = pltpu.make_async_copy(p_hbm, p_ref, sems.at[nt + 1])
        table_copy.start()
        for cp in copies:
            cp.start()
        table_copy.wait()
        for h in range(8):
            for c in range(2):
                table_ref[h * 2 + c] = p_ref[h, g, c, dev]
                table_ref[16 + h * 2 + c] = p_ref[g, h, c, dev]
        for cp in copies:
            cp.wait()
        for t in range(nt):
            s = slice(t * TILE, (t + 1) * TILE)
            v = r_ref[:, s]
            hi = v.astype(BF16).astype(F32)
            msg_ref[t, TILE:, :] = jnp.concatenate([hi, v - hi], axis=1).astype(BF16)
        for k, out in zip(SWAPS, outs):
            for c in range(2):
                out[c] = msg_ref[jnp.maximum(p_ref[g ^ k, g, c, dev], 0)]

    return pl.pallas_call(
        body,
        out_shape=[jax.ShapeDtypeStruct((32,), jnp.int32), vmem_bf16(nt, TILE + EXTRA, d)]
        + [vmem_bf16(2, TILE + EXTRA, d) for _ in SWAPS],
        in_specs=[HBM, HBM, HBM],
        out_specs=[SMEM] + [VM] * (1 + len(SWAPS)),
        scratch_shapes=[
            pltpu.VMEM((8, n), F32),
            pltpu.SMEM(partners.shape, jnp.int32),
            pltpu.SemaphoreType.DMA((nt + 2,)),
        ],
        compiler_params=params(),
        name="prep",
    )(*(pltpu.with_memory_space_constraint(x, pltpu.HBM) for x in (partners, points, targets)))


def gate(held, arrived):
    m = len(held)

    def body(*refs):
        pass

    return pl.pallas_call(
        body,
        out_shape=[vmem_bf16(*x.shape) for x in held],
        in_specs=[VM] * m + [ANY] * len(arrived),
        out_specs=[VM] * m,
        input_output_aliases={i: i for i in range(m)},
        compiler_params=params(4),
        name="gate",
    )(*held, *arrived)


def local_first(own):
    nt, _, _ = own.shape
    n = nt * TILE

    def body(a_ref, k_ref, acc_ref, na, nb, va):
        for i in range(nt):
            s = slice(i * TILE, (i + 1) * TILE)
            x = col_norms(a_ref[i, 0:TILE, :])
            na[s, :] = x
            nb[:, s] = x.T[0:8]
            va[:, s] = rhs_ones(a_ref[i, TILE:, :], 1.0)

        def step(t, carry):
            s = span(t)
            b = a_ref[t, 0:TILE, :] * jnp.asarray(-2.0, BF16)
            for i in range(nt):
                c = slice(i * TILE, (i + 1) * TILE)
                k_ref[t, c, :] = kernel_tile(a_ref[i, 0:TILE, :], b, na[c, :], nb[0:1, s])
            acc_ref[:, s] = fold_ones(mm(va[...], k_ref[t], NN))
            return carry

        lax.fori_loop(0, nt, step, 0)

    return pl.pallas_call(
        body,
        out_shape=(vmem_bf16(nt, n, TILE), f32(16, n)),
        in_specs=[VM],
        out_specs=(VM, VM),
        scratch_shapes=[pltpu.VMEM((n, 128), F32), pltpu.VMEM((8, n), F32), pltpu.VMEM((32, n), BF16)],
        compiler_params=params(),
        name="local_first",
    )(own)


def band_first(left, own, right, after):
    nt, _, _ = own.shape
    n = nt * TILE
    m = len(after)

    def body(l_ref, a_ref, b_ref, *refs):
        k_ref, col_ref, rowl_ref, rowo_ref, na, nb, va, vb, acc = refs[m:]
        v = lax.axis_index("dev")
        has_left = (v > 0).astype(F32)
        has_right = (v < lax.axis_size("dev") - 1).astype(F32)
        for i in range(nt):
            s = slice(i * TILE, (i + 1) * TILE)
            e = slice(n + i * TILE, n + (i + 1) * TILE)
            na[s, :] = col_norms(l_ref[i, 0:TILE, :])
            na[e, :] = col_norms(a_ref[i, 0:TILE, :])
            nb[:, s] = col_norms(b_ref[i, 0:TILE, :]).T[0:8]
            va[:, s] = rhs_ones(l_ref[i, TILE:, :], has_left)
            va[:, e] = rhs_ones(a_ref[i, TILE:, :], 1.0)
            vb[:, s] = rhs_ones(b_ref[i, TILE:, :], has_right)
        acc[...] = jnp.zeros_like(acc)

        def step(t, carry):
            s = span(t)
            b = b_ref[t, 0:TILE, :] * jnp.asarray(-2.0, BF16)
            for j, x in enumerate((l_ref, a_ref)):
                for i in range(nt):
                    e = slice((j * nt + i) * TILE, (j * nt + i + 1) * TILE)
                    k_ref[t, e, :] = kernel_tile(x[i, 0:TILE, :], b, na[e, :], nb[0:1, s])
            k = k_ref[t]
            col_ref[:, s] = fold_ones(mm(va[...], k, NN))
            acc[...] += mm(vb[:, s], k, NT)
            return carry

        lax.fori_loop(0, nt, step, 0)
        rows = fold_ones(acc[...])
        rowl_ref[...] = rows[:, 0:n]
        rowo_ref[...] = rows[:, n:]

    return pl.pallas_call(
        body,
        out_shape=(vmem_bf16(nt, 2 * n, TILE), f32(16, n), f32(16, n), f32(16, n)),
        in_specs=[VM] * 3 + [ANY] * m,
        out_specs=(VM,) * 4,
        scratch_shapes=[
            pltpu.VMEM((2 * n, 128), F32),
            pltpu.VMEM((8, n), F32),
            pltpu.VMEM((32, 2 * n), BF16),
            pltpu.VMEM((32, n), BF16),
            pltpu.VMEM((32, 2 * n), F32),
        ],
        compiler_params=params(),
        name="band_first",
    )(left, own, right, *after)


def cross_first(ks, table, own, tiles, after, held=()):
    nt, _, d = own.shape
    n = nt * TILE
    m = len(ks)
    slots = 2 * m
    p = len(held)

    def body(q_ref, a_ref, _, *refs):
        tile_refs = refs[:m]
        k_ref, row_ref, *cols = refs[m + p : 2 * m + p + 2]
        buf, jobs, sems, na, va, acc, nb, col = refs[2 * m + 2 * p + 2 :]
        g = lax.axis_index("group")
        count = jnp.int32(0)
        for i, k in enumerate(ks):
            for c in range(2):
                live = q_ref[16 + (g ^ k) * 2 + c] >= 0

                @pl.when(live)
                def _(count=count, i=i, k=k, c=c):
                    pltpu.make_async_copy(tile_refs[i].at[c], buf.at[count], sems.at[count]).start()
                    jobs[count] = 2 * i + c

                count = count + live.astype(jnp.int32)
        for i in range(nt):
            s = slice(i * TILE, (i + 1) * TILE)
            na[s, :] = col_norms(a_ref[i, 0:TILE, :])
            va[:, s] = rhs_ones(a_ref[i, TILE:, :], 1.0)
        acc[...] = jnp.zeros_like(acc)

        def step(j, carry):
            pltpu.make_async_copy(tile_refs[0].at[0], buf.at[j], sems.at[j]).wait()
            b = buf[j, 0:TILE, :]
            nb[...] = col_norms(b).T[0:8]
            b = b * jnp.asarray(-2.0, BF16)
            vb = rhs_ones(buf[j, TILE:, :], 1.0)
            for i in range(nt):
                c = slice(i * TILE, (i + 1) * TILE)
                k_ref[j, c, :] = kernel_tile(a_ref[i, 0:TILE, :], b, na[c, :], nb[0:1, :])
            k = k_ref[j]
            col[jobs[j]] = fold_ones(mm(va[...], k, NN))
            acc[...] += mm(vb, k, NT)
            return carry

        lax.fori_loop(0, count, step, 0)
        row_ref[...] = fold_ones(acc[...])
        for i, out in enumerate(cols):
            out[...] = col[2 * i : 2 * i + 2]

    return pl.pallas_call(
        body,
        out_shape=[vmem_bf16(slots, n, TILE), f32(16, n)] + [f32(2, 16, TILE)] * (m + p),
        in_specs=[SMEM, VM, ANY] + [ANY] * m + [VM] * p,
        out_specs=[VM] * (2 + m + p),
        input_output_aliases={3 + m + i: 2 + m + i for i in range(p)},
        scratch_shapes=[
            pltpu.VMEM((slots, TILE + EXTRA, d), BF16),
            pltpu.SMEM((slots,), jnp.int32),
            pltpu.SemaphoreType.DMA((slots,)),
            pltpu.VMEM((n, 128), F32),
            pltpu.VMEM((32, n), BF16),
            pltpu.VMEM((32, n), F32),
            pltpu.VMEM((8, TILE), F32),
            pltpu.VMEM((slots, 16, TILE), F32),
        ],
        compiler_params=params(),
    )(table, own, after, *tiles, *held)


def combine(table, r, parts, ret):
    n = r.shape[1]
    m = len(parts)

    def body(q_ref, r_ref, *refs):
        part_refs, (*x_refs, w_ref, deg_ref, sum_ref, acc) = refs[:m], refs[m:]
        x_refs, out_refs = x_refs[:7], x_refs[7:]
        g = lax.axis_index("group")
        total = part_refs[0][...]
        for p in part_refs[1:]:
            total = total + p[...]
        acc[...] = total
        for k, x in zip(SWAPS, x_refs):
            for c in range(2):
                t = q_ref[(g ^ k) * 2 + c]

                @pl.when(t >= 0)
                def _(x=x, c=c, t=t):
                    acc[:, span(t)] = acc[:, span(t)] + x[c]

        rv = r_ref[...]
        deg = acc[8:16, :]
        w = 0.5 * (deg * rv - acc[0:8, :])
        w_ref[...] = w
        deg_ref[...] = deg
        for k, out in zip(SWAPS, out_refs):
            for c in range(2):
                t = jnp.maximum(q_ref[(g ^ k) * 2 + c], 0)
                out[c * 8 : c * 8 + 8, :] = w_ref[:, span(t)]
        lane = lax.broadcasted_iota(jnp.int32, (8, 128), 1)
        sums = jnp.zeros((8, 128), F32)
        for k, v in enumerate((rv * rv, rv * w, w * w, 0.5 * deg * w * w)):
            sums = jnp.where(lane == k, jnp.sum(v, axis=1, keepdims=True), sums)
        sum_ref[...] = sums

    return pl.pallas_call(
        body,
        out_shape=[f32(16, TILE)] * 7 + [f32(8, n), f32(8, n), f32(8, 128)],
        in_specs=[SMEM] + [VM] * (m + 8),
        out_specs=[VM] * 10,
        scratch_shapes=[pltpu.VMEM((16, n), F32)],
        compiler_params=params(),
        name="combine",
    )(table, r, *parts, *ret)


def local_second(k_local, w):
    nt, n, _ = k_local.shape

    def body(k_ref, w_ref, out_ref):
        va = split(w_ref[...])
        for t in range(nt):
            out_ref[:, t * TILE : (t + 1) * TILE] = fold(mm(va, k_ref[t], NN))

    return pl.pallas_call(
        body,
        out_shape=f32(8, n),
        in_specs=[VM, VM],
        out_specs=VM,
        compiler_params=params(),
        name="local_second",
    )(k_local, w)


def band_second(k_band, w_left, w, w_right, after):
    nt, n2, _ = k_band.shape
    n = n2 // 2

    def body(k_ref, wl_ref, w_ref, wb_ref, _, col_ref, rowl_ref, rowo_ref, va, acc):
        va[:, 0:n] = split(wl_ref[...])
        va[:, n:] = split(w_ref[...])
        vb = split(wb_ref[...])
        for t in range(nt):
            s = slice(t * TILE, (t + 1) * TILE)
            col_ref[:, s] = fold(mm(va[...], k_ref[t], NN))
            new = mm(vb[:, s], k_ref[t], NT)
            acc[...] = new if t == 0 else acc[...] + new
        rows = fold(acc[...])
        rowl_ref[...] = rows[:, 0:n]
        rowo_ref[...] = rows[:, n:]

    return pl.pallas_call(
        body,
        out_shape=(f32(8, n), f32(8, n), f32(8, n)),
        in_specs=[VM] * 4 + [ANY],
        out_specs=(VM,) * 3,
        scratch_shapes=[pltpu.VMEM((16, n2), BF16), pltpu.VMEM((16, n2), F32)],
        compiler_params=params(),
        name="band_second",
    )(k_band, w_left, w, w_right, after)


def cross_second(table, k_caches, w, xw, sums, loc, row_left, row_own, w_left):
    n = w.shape[1]

    def body(
        q_ref, ka_ref, kb_ref, kc_ref, w_ref, sum_ref, loc_ref, rl_ref, ro_ref, wl_ref, *refs
    ):
        xw_refs, (col_ref, row_ref, va, acc, jobs, xw_ref) = refs[:7], refs[7:]
        g = lax.axis_index("group")
        for k, x in zip(SWAPS, xw_refs):
            xw_ref[g ^ k] = x[...]
        va[...] = split(w_ref[...])
        acc[...] = jnp.zeros_like(acc)
        for ks, k_ref in zip(STAGES, (ka_ref, kb_ref, kc_ref)):
            count = jnp.int32(0)
            for k in ks:
                for c in range(2):
                    live = q_ref[16 + (g ^ k) * 2 + c] >= 0

                    @pl.when(live)
                    def _(count=count, k=k, c=c):
                        jobs[count] = (g ^ k) * 2 + c

                    count = count + live.astype(jnp.int32)

            def step(j, carry, k_ref=k_ref):
                slot = jobs[j]
                h, c = slot >> 1, slot & 1
                rows = pl.ds(pl.multiple_of(c * 8, 8), 8)
                k = k_ref[j]
                col_ref[h, rows, :] = fold(mm(va[...], k, NN))
                acc[...] += mm(split(xw_ref[h, rows, :]), k, NT)
                return carry

            lax.fori_loop(0, count, step, 0)
        row = fold(acc[...])
        row_ref[...] = row
        pairs = w_ref[...] * (0.5 * loc_ref[...] + ro_ref[...] + row) + wl_ref[...] * rl_ref[...]
        lane = lax.broadcasted_iota(jnp.int32, (8, 128), 1)
        pay = jnp.where(lane == 3, sum_ref[...] - jnp.sum(pairs, axis=1, keepdims=True), sum_ref[...])
        for h in range(8):
            col_ref[h, 16:24, 0:128] = pay
            col_ref[h, 16:24, 128:] = jnp.zeros((8, 128), F32)

    return pl.pallas_call(
        body,
        out_shape=(f32(8, 24, TILE), f32(8, n)),
        in_specs=[SMEM] + [VM] * 16,
        out_specs=(VM, VM),
        scratch_shapes=[
            pltpu.VMEM((16, n), BF16),
            pltpu.VMEM((16, n), F32),
            pltpu.SMEM((16,), jnp.int32),
            pltpu.VMEM((8, 16, TILE), F32),
        ],
        compiler_params=params(),
        name="cross_second",
    )(table, *k_caches, w, sums, loc, row_left, row_own, w_left, *xw)


def group_sum(table, w, deg, parts, ret):
    n = w.shape[1]
    m = len(parts)

    def body(q_ref, w_ref, deg_ref, *refs):
        part_refs, (x_ref, w2_ref, out_ref, acc) = refs[:m], refs[m:]
        total = part_refs[0][...]
        for p in part_refs[1:]:
            total = total + p[...]
        acc[...] = total
        for h in range(8):
            for c in range(2):
                t = q_ref[h * 2 + c]

                @pl.when(t >= 0)
                def _(h=h, c=c, t=t):
                    acc[:, span(t)] = acc[:, span(t)] + x_ref[h, c * 8 : c * 8 + 8, :]

        w2_ref[...] = 0.5 * (deg_ref[...] * w_ref[...] - acc[...])
        sums = x_ref[0, 16:24, 0:128]
        for h in range(1, 8):
            sums = sums + x_ref[h, 16:24, 0:128]
        for v in range(16):
            out_ref[v] = sums

    return pl.pallas_call(
        body,
        out_shape=(f32(8, n), f32(16, 8, 128)),
        in_specs=[SMEM] + [VM] * (3 + m),
        out_specs=(VM, VM),
        scratch_shapes=[pltpu.VMEM((8, n), F32)],
        compiler_params=params(),
        name="group_sum",
    )(table, w, deg, *parts, ret)


def finish(gathered, r, w, w2):
    n = r.shape[1]

    def body(g_ref, r_ref, w_ref, w2_ref, sol_ref, res_ref):
        sums = g_ref[0]
        for v in range(1, 16):
            sums = sums + g_ref[v]
        rho, mu, nu, xi = (sums[:, k : k + 1] for k in range(4))
        rv = r_ref[...]
        wv = w_ref[...]
        first = rho / (rho + mu)
        gap = (nu - mu * (mu / rho)) * (first * first)
        beta = gap / rho
        cr = mu / (rho + mu) + beta
        curvature = cr * cr * (rho + mu) - 2.0 * cr * first * (mu + nu) + first * first * (nu + xi)
        second = gap / curvature
        sol_ref[...] = (first + second * cr) * rv - (second * first) * wv
        res_ref[...] = (
            (mu / (rho + mu) - second * cr) * rv
            + (second * (first - cr) - first) * wv
            + (second * first) * w2_ref[...]
        )

    return pl.pallas_call(
        body,
        out_shape=(f32(8, n), f32(8, n)),
        in_specs=[VM] * 4,
        out_specs=(VM, VM),
        compiler_params=params(),
        name="finish",
    )(gathered, r, w, w2)


def on_device(points, targets, partner_tiles):
    dev_count = lax.axis_size("dev")
    to_right = [(i, i + 1) for i in range(dev_count - 1)]
    to_left = [(i + 1, i) for i in range(dev_count - 1)]

    def right_of(x):
        return lax.ppermute(x, "dev", to_left)

    def left_of(x):
        return lax.ppermute(x, "dev", to_right)

    def swap(x, k):
        return lax.ppermute(x, "group", [(i, i ^ k) for i in range(8)])

    def trade(x, axis="group"):
        return lax.all_to_all(x, axis, split_axis=0, concat_axis=0, tiled=True)

    table, own, *outgoing = prep(jnp.transpose(partner_tiles, (0, 2, 3, 1)), points, targets)
    arrived = {}
    for x, k in zip(outgoing, SWAPS[:5]):
        arrived[k] = swap(x, k)
    left = left_of(own)
    right = right_of(own)
    k_local, acc_local = local_first(own)

    def cross(stage, after, held=()):
        return cross_first(stage, table, own, [arrived[k] for k in stage], after, held)

    k_a, row_a, *col_a = cross(STAGES[0], acc_local)
    for x, k in zip(gate(outgoing[5:], [row_a, arrived[3], arrived[7]]), STAGES[2]):
        arrived[k] = swap(x, k)
    k_b, row_b, *col_b = cross(STAGES[1], row_a, col_a)
    ret_near = []
    for x, k in zip(col_b, STAGES[1] + STAGES[0]):
        ret_near.append(swap(x, k))
    k_band, to_r, to_l, acc_band = band_first(left, own, right, [row_b])
    from_left, from_right = left_of(to_r), right_of(to_l)
    k_c, row_c, *col_c = cross(STAGES[2], acc_band)
    ret = ret_near[2:] + ret_near[:2] + [swap(x, k) for x, k in zip(col_c, STAGES[2])]
    *xw_out, w, deg, sums = combine(
        table, targets, (acc_local, acc_band, from_left, from_right, row_a, row_b, row_c), ret
    )
    w_left, w_right = left_of(w), right_of(w)
    xw = [swap(x, k) for x, k in zip(xw_out, SWAPS)]
    loc2 = local_second(k_local, w)
    col_r, rowl_b, rowo_b = band_second(k_band, w_left, w, w_right, loc2)
    from_left2 = left_of(col_r)
    from_right2 = right_of(rowl_b)
    col_x, row_x = cross_second(table, (k_a, k_b, k_c), w, xw, sums, loc2, rowl_b, rowo_b, w_left)
    w2, column = group_sum(table, w, deg, (loc2, rowo_b, row_x, from_left2, from_right2), trade(col_x))
    return finish(trade(column, "dev"), targets, w, w2)


def solution(mesh):
    return jax.shard_map(
        on_device,
        mesh=mesh,
        in_specs=(P(("group", "dev"), None), P(None, ("group", "dev")), P()),
        out_specs=(P(None, ("group", "dev")), P(None, ("group", "dev"))),
        check_vma=False,
    )
```

```python
import jax
import jax.numpy as jnp
from jax import lax
from jax.experimental import pallas as pl
from jax.experimental.pallas import tpu as pltpu
from jax.sharding import PartitionSpec as P


TILE = 256
EXTRA = 8
SCALE = 3.9
C4 = 4.0 / SCALE**5
CUT = 5.0 * SCALE / 4.0
NT = (((1,), (1,)), ((), ()))
NN = (((1,), (0,)), ((), ()))
F32 = jnp.float32
BF16 = jnp.bfloat16
STAGES = ((2, 6, 1), (3, 7), (4, 5))
SWAPS = STAGES[0] + STAGES[1] + STAGES[2]

SMEM = pl.BlockSpec(memory_space=pltpu.SMEM)
ANY = pl.BlockSpec(memory_space=pl.ANY)
HBM = pl.BlockSpec(memory_space=pltpu.HBM)
VM = pl.BlockSpec(memory_space=pltpu.VMEM)


def mm(a, b, dims):
    return lax.dot_general(a, b, dims, preferred_element_type=F32)


def col_norms(x):
    x = x.astype(F32)
    return jnp.broadcast_to(jnp.sum(x * x, axis=1, keepdims=True), (x.shape[0], 128))


def kernel_tile(a, b_scaled, na, nb):
    q = mm(a, b_scaled, NT) + (jnp.concatenate([na, na], axis=1) + nb)
    q = jnp.maximum(q, 1e-30)
    u = jnp.maximum(SCALE - q * lax.rsqrt(q), 0.0)
    t = u * u
    return (t * t * (CUT - u)).astype(BF16)


def split(v):
    hi = v.astype(BF16)
    lo = (v - hi.astype(F32)).astype(BF16)
    return jnp.concatenate([hi, lo], axis=0)


def rhs_ones(rows, one):
    v = rows.astype(F32)
    return jnp.concatenate([v[:, 0:TILE], v[:, TILE:], jnp.full((16, TILE), one, F32)], axis=0).astype(BF16)


def fold(acc):
    return (acc[0:8] + acc[8:16]) * C4


def fold_ones(acc):
    return jnp.concatenate([acc[0:8] + acc[8:16], acc[16:24]], axis=0) * C4


def span(t):
    return pl.ds(pl.multiple_of(t * TILE, TILE), TILE)


def params(mib=12):
    return pltpu.CompilerParams(vmem_limit_bytes=mib * 1024 * 1024)


def f32(*shape):
    return jax.ShapeDtypeStruct(shape, F32)


def vmem_bf16(*shape):
    return pltpu.VMEM(shape, BF16)


def prep(partners, points, targets):
    n, d = points.shape
    nt = n // TILE

    def body(p_hbm, pts_ref, r_hbm, table_ref, msg_ref, *refs):
        outs, (r_ref, p_ref, sems) = refs[:-3], refs[-3:]
        g = lax.axis_index("group")
        dev = lax.axis_index("dev")
        copies = [pltpu.make_async_copy(r_hbm, r_ref, sems.at[nt])]
        for t in range(nt):
            s = slice(t * TILE, (t + 1) * TILE)
            copies.append(pltpu.make_async_copy(pts_ref.at[s, :], msg_ref.at[t, pl.ds(0, TILE), :], sems.at[t]))
        table_copy = pltpu.make_async_copy(p_hbm, p_ref, sems.at[nt + 1])
        table_copy.start()
        for cp in copies:
            cp.start()
        table_copy.wait()
        for h in range(8):
            for c in range(2):
                table_ref[h * 2 + c] = p_ref[h, g, c, dev]
                table_ref[16 + h * 2 + c] = p_ref[g, h, c, dev]
        for cp in copies:
            cp.wait()
        for t in range(nt):
            s = slice(t * TILE, (t + 1) * TILE)
            v = r_ref[:, s]
            hi = v.astype(BF16).astype(F32)
            msg_ref[t, TILE:, :] = jnp.concatenate([hi, v - hi], axis=1).astype(BF16)
        for k, out in zip(SWAPS, outs):
            for c in range(2):
                out[c] = msg_ref[jnp.maximum(p_ref[g ^ k, g, c, dev], 0)]

    return pl.pallas_call(
        body,
        out_shape=[jax.ShapeDtypeStruct((32,), jnp.int32), vmem_bf16(nt, TILE + EXTRA, d)]
        + [vmem_bf16(2, TILE + EXTRA, d) for _ in SWAPS],
        in_specs=[HBM, HBM, HBM],
        out_specs=[SMEM] + [VM] * (1 + len(SWAPS)),
        scratch_shapes=[
            pltpu.VMEM((8, n), F32),
            pltpu.SMEM(partners.shape, jnp.int32),
            pltpu.SemaphoreType.DMA((nt + 2,)),
        ],
        compiler_params=params(),
        name="prep",
    )(*(pltpu.with_memory_space_constraint(x, pltpu.HBM) for x in (partners, points, targets)))


def gate(held, arrived):
    m = len(held)

    def body(*refs):
        pass

    return pl.pallas_call(
        body,
        out_shape=[vmem_bf16(*x.shape) for x in held],
        in_specs=[VM] * m + [ANY] * len(arrived),
        out_specs=[VM] * m,
        input_output_aliases={i: i for i in range(m)},
        compiler_params=params(4),
        name="gate",
    )(*held, *arrived)


def local_first(own):
    nt, _, _ = own.shape
    n = nt * TILE

    def body(a_ref, k_ref, acc_ref, na, nb, va):
        for i in range(nt):
            s = slice(i * TILE, (i + 1) * TILE)
            x = col_norms(a_ref[i, 0:TILE, :])
            na[s, :] = x
            nb[:, s] = x.T[0:8]
            va[:, s] = rhs_ones(a_ref[i, TILE:, :], 1.0)

        def step(t, carry):
            s = span(t)
            b = a_ref[t, 0:TILE, :] * jnp.asarray(-2.0, BF16)
            for i in range(nt):
                c = slice(i * TILE, (i + 1) * TILE)
                k_ref[t, c, :] = kernel_tile(a_ref[i, 0:TILE, :], b, na[c, :], nb[0:1, s])
            acc_ref[:, s] = fold_ones(mm(va[...], k_ref[t], NN))
            return carry

        lax.fori_loop(0, nt, step, 0, unroll=2)

    return pl.pallas_call(
        body,
        out_shape=(vmem_bf16(nt, n, TILE), f32(16, n)),
        in_specs=[VM],
        out_specs=(VM, VM),
        scratch_shapes=[pltpu.VMEM((n, 128), F32), pltpu.VMEM((8, n), F32), pltpu.VMEM((32, n), BF16)],
        compiler_params=params(),
        name="local_first",
    )(own)


def band_first(left, own, right, after):
    nt, _, _ = own.shape
    n = nt * TILE
    m = len(after)

    def body(l_ref, a_ref, b_ref, *refs):
        k_ref, col_ref, rowl_ref, rowo_ref, na, nb, va, vb, acc = refs[m:]
        v = lax.axis_index("dev")
        has_left = (v > 0).astype(F32)
        has_right = (v < lax.axis_size("dev") - 1).astype(F32)
        for i in range(nt):
            s = slice(i * TILE, (i + 1) * TILE)
            e = slice(n + i * TILE, n + (i + 1) * TILE)
            na[s, :] = col_norms(l_ref[i, 0:TILE, :])
            na[e, :] = col_norms(a_ref[i, 0:TILE, :])
            nb[:, s] = col_norms(b_ref[i, 0:TILE, :]).T[0:8]
            va[:, s] = rhs_ones(l_ref[i, TILE:, :], has_left)
            va[:, e] = rhs_ones(a_ref[i, TILE:, :], 1.0)
            vb[:, s] = rhs_ones(b_ref[i, TILE:, :], has_right)
        acc[...] = jnp.zeros_like(acc)

        def step(t, carry):
            s = span(t)
            b = b_ref[t, 0:TILE, :] * jnp.asarray(-2.0, BF16)
            for j, x in enumerate((l_ref, a_ref)):
                for i in range(nt):
                    e = slice((j * nt + i) * TILE, (j * nt + i + 1) * TILE)
                    k_ref[t, e, :] = kernel_tile(x[i, 0:TILE, :], b, na[e, :], nb[0:1, s])
            k = k_ref[t]
            col_ref[:, s] = fold_ones(mm(va[...], k, NN))
            acc[...] += mm(vb[:, s], k, NT)
            return carry

        lax.fori_loop(0, nt, step, 0, unroll=2)
        rows = fold_ones(acc[...])
        rowl_ref[...] = rows[:, 0:n]
        rowo_ref[...] = rows[:, n:]

    return pl.pallas_call(
        body,
        out_shape=(vmem_bf16(nt, 2 * n, TILE), f32(16, n), f32(16, n), f32(16, n)),
        in_specs=[VM] * 3 + [ANY] * m,
        out_specs=(VM,) * 4,
        scratch_shapes=[
            pltpu.VMEM((2 * n, 128), F32),
            pltpu.VMEM((8, n), F32),
            pltpu.VMEM((32, 2 * n), BF16),
            pltpu.VMEM((32, n), BF16),
            pltpu.VMEM((32, 2 * n), F32),
        ],
        compiler_params=params(),
        name="band_first",
    )(left, own, right, *after)


def cross_first(ks, table, own, tiles, after, held=()):
    nt, _, d = own.shape
    n = nt * TILE
    m = len(ks)
    slots = 2 * m
    p = len(held)

    def body(q_ref, a_ref, _, *refs):
        tile_refs = refs[:m]
        k_ref, row_ref, *cols = refs[m + p : 2 * m + p + 2]
        buf, jobs, sems, na, va, acc, nb, col = refs[2 * m + 2 * p + 2 :]
        g = lax.axis_index("group")
        count = jnp.int32(0)
        for i, k in enumerate(ks):
            for c in range(2):
                live = q_ref[16 + (g ^ k) * 2 + c] >= 0

                @pl.when(live)
                def _(count=count, i=i, k=k, c=c):
                    pltpu.make_async_copy(tile_refs[i].at[c], buf.at[count], sems.at[count]).start()
                    jobs[count] = 2 * i + c

                count = count + live.astype(jnp.int32)
        for i in range(nt):
            s = slice(i * TILE, (i + 1) * TILE)
            na[s, :] = col_norms(a_ref[i, 0:TILE, :])
            va[:, s] = rhs_ones(a_ref[i, TILE:, :], 1.0)
        acc[...] = jnp.zeros_like(acc)

        def step(j, carry):
            pltpu.make_async_copy(tile_refs[0].at[0], buf.at[j], sems.at[j]).wait()
            b = buf[j, 0:TILE, :]
            nb[...] = col_norms(b).T[0:8]
            b = b * jnp.asarray(-2.0, BF16)
            vb = rhs_ones(buf[j, TILE:, :], 1.0)
            for i in range(nt):
                c = slice(i * TILE, (i + 1) * TILE)
                k_ref[j, c, :] = kernel_tile(a_ref[i, 0:TILE, :], b, na[c, :], nb[0:1, :])
            k = k_ref[j]
            col[jobs[j]] = fold_ones(mm(va[...], k, NN))
            acc[...] += mm(vb, k, NT)
            return carry

        lax.fori_loop(0, count, step, 0)
        row_ref[...] = fold_ones(acc[...])
        for i, out in enumerate(cols):
            out[...] = col[2 * i : 2 * i + 2]

    return pl.pallas_call(
        body,
        out_shape=[vmem_bf16(slots, n, TILE), f32(16, n)] + [f32(2, 16, TILE)] * (m + p),
        in_specs=[SMEM, VM, ANY] + [ANY] * m + [VM] * p,
        out_specs=[VM] * (2 + m + p),
        input_output_aliases={3 + m + i: 2 + m + i for i in range(p)},
        scratch_shapes=[
            pltpu.VMEM((slots, TILE + EXTRA, d), BF16),
            pltpu.SMEM((slots,), jnp.int32),
            pltpu.SemaphoreType.DMA((slots,)),
            pltpu.VMEM((n, 128), F32),
            pltpu.VMEM((32, n), BF16),
            pltpu.VMEM((32, n), F32),
            pltpu.VMEM((8, TILE), F32),
            pltpu.VMEM((slots, 16, TILE), F32),
        ],
        compiler_params=params(),
    )(table, own, after, *tiles, *held)


def combine(table, r, parts, ret):
    n = r.shape[1]
    m = len(parts)

    def body(q_ref, r_ref, *refs):
        part_refs, (*x_refs, w_ref, deg_ref, sum_ref, acc) = refs[:m], refs[m:]
        x_refs, xw_ref = x_refs[:7], x_refs[7]
        g = lax.axis_index("group")
        total = part_refs[0][...]
        for p in part_refs[1:]:
            total = total + p[...]
        acc[...] = total
        for k, x in zip(SWAPS, x_refs):
            for c in range(2):
                t = q_ref[(g ^ k) * 2 + c]

                @pl.when(t >= 0)
                def _(x=x, c=c, t=t):
                    acc[:, span(t)] = acc[:, span(t)] + x[c]

        rv = r_ref[...]
        deg = acc[8:16, :]
        w = 0.5 * (deg * rv - acc[0:8, :])
        w_ref[...] = w
        deg_ref[...] = deg
        for h in range(8):
            for c in range(2):
                t = jnp.maximum(q_ref[h * 2 + c], 0)
                xw_ref[h, c * 8 : c * 8 + 8, :] = w_ref[:, span(t)]
        lane = lax.broadcasted_iota(jnp.int32, (8, 128), 1)
        sums = jnp.zeros((8, 128), F32)
        for k, v in enumerate((rv * rv, rv * w, w * w, 0.5 * deg * w * w)):
            sums = jnp.where(lane == k, jnp.sum(v, axis=1, keepdims=True), sums)
        sum_ref[...] = sums

    return pl.pallas_call(
        body,
        out_shape=[f32(8, 16, TILE), f32(8, n), f32(8, n), f32(8, 128)],
        in_specs=[SMEM] + [VM] * (m + 8),
        out_specs=[VM] * 4,
        scratch_shapes=[pltpu.VMEM((16, n), F32)],
        compiler_params=params(),
        name="combine",
    )(table, r, *parts, *ret)


def local_second(k_local, w, after):
    nt, n, _ = k_local.shape

    def body(k_ref, w_ref, _, out_ref):
        va = split(w_ref[...])
        for t in range(nt):
            out_ref[:, t * TILE : (t + 1) * TILE] = fold(mm(va, k_ref[t], NN))

    return pl.pallas_call(
        body,
        out_shape=f32(8, n),
        in_specs=[VM, VM, ANY],
        out_specs=VM,
        compiler_params=params(),
        name="local_second",
    )(k_local, w, after)


def band_second(k_band, w_left, w, w_right, after):
    nt, n2, _ = k_band.shape
    n = n2 // 2

    def body(k_ref, wl_ref, w_ref, wb_ref, _, col_ref, rowl_ref, rowo_ref, va, acc):
        va[:, 0:n] = split(wl_ref[...])
        va[:, n:] = split(w_ref[...])
        vb = split(wb_ref[...])
        for t in range(nt):
            s = slice(t * TILE, (t + 1) * TILE)
            col_ref[:, s] = fold(mm(va[...], k_ref[t], NN))
            new = mm(vb[:, s], k_ref[t], NT)
            acc[...] = new if t == 0 else acc[...] + new
        rows = fold(acc[...])
        rowl_ref[...] = rows[:, 0:n]
        rowo_ref[...] = rows[:, n:]

    return pl.pallas_call(
        body,
        out_shape=(f32(8, n), f32(8, n), f32(8, n)),
        in_specs=[VM] * 4 + [ANY],
        out_specs=(VM,) * 3,
        scratch_shapes=[pltpu.VMEM((16, n2), BF16), pltpu.VMEM((16, n2), F32)],
        compiler_params=params(),
        name="band_second",
    )(k_band, w_left, w, w_right, after)


def cross_second(table, k_caches, w, xw, sums, loc, row_left, row_own, w_left):
    n = w.shape[1]

    def body(
        q_ref, ka_ref, kb_ref, kc_ref, w_ref, sum_ref, loc_ref, rl_ref, ro_ref, wl_ref, *refs
    ):
        xw_ref, col_ref, row_ref, va, acc, jobs = refs
        g = lax.axis_index("group")
        va[...] = split(w_ref[...])
        acc[...] = jnp.zeros_like(acc)
        for ks, k_ref in zip(STAGES, (ka_ref, kb_ref, kc_ref)):
            count = jnp.int32(0)
            for k in ks:
                for c in range(2):
                    live = q_ref[16 + (g ^ k) * 2 + c] >= 0

                    @pl.when(live)
                    def _(count=count, k=k, c=c):
                        jobs[count] = (g ^ k) * 2 + c

                    count = count + live.astype(jnp.int32)

            def step(j, carry, k_ref=k_ref):
                slot = jobs[j]
                h, c = slot >> 1, slot & 1
                rows = pl.ds(pl.multiple_of(c * 8, 8), 8)
                k = k_ref[j]
                col_ref[h, rows, :] = fold(mm(va[...], k, NN))
                acc[...] += mm(split(xw_ref[h, rows, :]), k, NT)
                return carry

            lax.fori_loop(0, count, step, 0)
        row = fold(acc[...])
        row_ref[...] = row
        pairs = w_ref[...] * (0.5 * loc_ref[...] + ro_ref[...] + row) + wl_ref[...] * rl_ref[...]
        lane = lax.broadcasted_iota(jnp.int32, (8, 128), 1)
        pay = jnp.where(lane == 3, sum_ref[...] - jnp.sum(pairs, axis=1, keepdims=True), sum_ref[...])
        for h in range(8):
            col_ref[h, 16:24, 0:128] = pay
            col_ref[h, 16:24, 128:] = jnp.zeros((8, 128), F32)

    return pl.pallas_call(
        body,
        out_shape=(f32(8, 24, TILE), f32(8, n)),
        in_specs=[SMEM] + [VM] * 10,
        out_specs=(VM, VM),
        scratch_shapes=[
            pltpu.VMEM((16, n), BF16),
            pltpu.VMEM((16, n), F32),
            pltpu.SMEM((16,), jnp.int32),
        ],
        compiler_params=params(),
        name="cross_second",
    )(table, *k_caches, w, sums, loc, row_left, row_own, w_left, xw)


def group_sum(table, w, deg, parts, ret):
    n = w.shape[1]
    m = len(parts)

    def body(q_ref, w_ref, deg_ref, *refs):
        part_refs, (x_ref, w2_ref, out_ref, acc) = refs[:m], refs[m:]
        total = part_refs[0][...]
        for p in part_refs[1:]:
            total = total + p[...]
        acc[...] = total
        for h in range(8):
            for c in range(2):
                t = q_ref[h * 2 + c]

                @pl.when(t >= 0)
                def _(h=h, c=c, t=t):
                    acc[:, span(t)] = acc[:, span(t)] + x_ref[h, c * 8 : c * 8 + 8, :]

        w2_ref[...] = 0.5 * (deg_ref[...] * w_ref[...] - acc[...])
        sums = x_ref[0, 16:24, 0:128]
        for h in range(1, 8):
            sums = sums + x_ref[h, 16:24, 0:128]
        for v in range(16):
            out_ref[v] = sums

    return pl.pallas_call(
        body,
        out_shape=(f32(8, n), f32(16, 8, 128)),
        in_specs=[SMEM] + [VM] * (3 + m),
        out_specs=(VM, VM),
        scratch_shapes=[pltpu.VMEM((8, n), F32)],
        compiler_params=params(),
        name="group_sum",
    )(table, w, deg, *parts, ret)


def finish(gathered, r, w, w2):
    n = r.shape[1]

    def body(g_ref, r_ref, w_ref, w2_ref, sol_ref, res_ref):
        sums = g_ref[0]
        for v in range(1, 16):
            sums = sums + g_ref[v]
        rho, mu, nu, xi = (sums[:, k : k + 1] for k in range(4))
        rv = r_ref[...]
        wv = w_ref[...]
        first = rho / (rho + mu)
        gap = (nu - mu * (mu / rho)) * (first * first)
        beta = gap / rho
        cr = mu / (rho + mu) + beta
        curvature = cr * cr * (rho + mu) - 2.0 * cr * first * (mu + nu) + first * first * (nu + xi)
        second = gap / curvature
        sol_ref[...] = (first + second * cr) * rv - (second * first) * wv
        res_ref[...] = (
            (mu / (rho + mu) - second * cr) * rv
            + (second * (first - cr) - first) * wv
            + (second * first) * w2_ref[...]
        )

    return pl.pallas_call(
        body,
        out_shape=(f32(8, n), f32(8, n)),
        in_specs=[VM] * 4,
        out_specs=(VM, VM),
        compiler_params=params(),
        name="finish",
    )(gathered, r, w, w2)


def on_device(points, targets, partner_tiles):
    dev_count = lax.axis_size("dev")
    to_right = [(i, i + 1) for i in range(dev_count - 1)]
    to_left = [(i + 1, i) for i in range(dev_count - 1)]

    def right_of(x):
        return lax.ppermute(x, "dev", to_left)

    def left_of(x):
        return lax.ppermute(x, "dev", to_right)

    def swap(x, k):
        return lax.ppermute(x, "group", [(i, i ^ k) for i in range(8)])

    def trade(x, axis="group"):
        return lax.all_to_all(x, axis, split_axis=0, concat_axis=0, tiled=True)

    table, own, *outgoing = prep(jnp.transpose(partner_tiles, (0, 2, 3, 1)), points, targets)
    arrived = {}
    for x, k in zip(outgoing, SWAPS[:5]):
        arrived[k] = swap(x, k)
    left = left_of(own)
    right = right_of(own)
    k_local, acc_local = local_first(own)

    def cross(stage, after, held=()):
        return cross_first(stage, table, own, [arrived[k] for k in stage], after, held)

    k_a, row_a, *col_a = cross(STAGES[0], acc_local)
    for x, k in zip(gate(outgoing[5:], [row_a, arrived[3], arrived[7]]), STAGES[2]):
        arrived[k] = swap(x, k)
    k_b, row_b, *col_b = cross(STAGES[1], row_a, col_a)
    ret_near = []
    for x, k in zip(col_b, STAGES[1] + STAGES[0]):
        ret_near.append(swap(x, k))
    k_band, to_r, to_l, acc_band = band_first(left, own, right, [row_b])
    from_left, from_right = left_of(to_r), right_of(to_l)
    k_c, row_c, *col_c = cross(STAGES[2], acc_band)
    ret = ret_near[2:] + ret_near[:2] + [swap(x, k) for x, k in zip(col_c, STAGES[2])]
    xw_out, w, deg, sums = combine(
        table, targets, (acc_local, acc_band, from_left, from_right, row_a, row_b, row_c), ret
    )
    w_left = left_of(w)
    w_right = right_of(w)
    xw = trade(xw_out)
    loc2 = local_second(k_local, w, xw)
    col_r, rowl_b, rowo_b = band_second(k_band, w_left, w, w_right, loc2)
    from_left2 = left_of(col_r)
    from_right2 = right_of(rowl_b)
    col_x, row_x = cross_second(table, (k_a, k_b, k_c), w, xw, sums, loc2, rowl_b, rowo_b, w_left)
    w2, column = group_sum(table, w, deg, (loc2, rowo_b, row_x, from_left2, from_right2), trade(col_x))
    return finish(trade(column, "dev"), targets, w, w2)


def solution(mesh):
    return jax.shard_map(
        on_device,
        mesh=mesh,
        in_specs=(P(("group", "dev"), None), P(None, ("group", "dev")), P()),
        out_specs=(P(None, ("group", "dev")), P(None, ("group", "dev"))),
        check_vma=False,
    )
```

```python
import jax
import jax.numpy as jnp
from jax import lax
from jax.experimental import pallas as pl
from jax.experimental.pallas import tpu as pltpu
from jax.sharding import PartitionSpec as P


TILE = 256
EXTRA = 8
SCALE = 3.9
C4 = 4.0 / SCALE**5
CUT = 5.0 * SCALE / 4.0
NT = (((1,), (1,)), ((), ()))
NN = (((1,), (0,)), ((), ()))
F32 = jnp.float32
BF16 = jnp.bfloat16
STAGES = ((2, 6, 1), (3, 7), (4, 5))
SWAPS = STAGES[0] + STAGES[1] + STAGES[2]

SMEM = pl.BlockSpec(memory_space=pltpu.SMEM)
ANY = pl.BlockSpec(memory_space=pl.ANY)
HBM = pl.BlockSpec(memory_space=pltpu.HBM)
VM = pl.BlockSpec(memory_space=pltpu.VMEM)


def mm(a, b, dims):
    return lax.dot_general(a, b, dims, preferred_element_type=F32)


def col_norms(x):
    x = x.astype(F32)
    return jnp.broadcast_to(jnp.sum(x * x, axis=1, keepdims=True), (x.shape[0], 128))


def kernel_tile(a, b_scaled, na, nb):
    q = mm(a, b_scaled, NT) + (jnp.concatenate([na, na], axis=1) + nb)
    q = jnp.maximum(q, 1e-30)
    u = jnp.maximum(SCALE - q * lax.rsqrt(q), 0.0)
    t = u * u
    return (t * t * (CUT - u)).astype(BF16)


def split(v):
    hi = v.astype(BF16)
    lo = (v - hi.astype(F32)).astype(BF16)
    return jnp.concatenate([hi, lo], axis=0)


def rhs_ones(rows, one):
    v = rows.astype(F32)
    return jnp.concatenate([v[:, 0:TILE], v[:, TILE:], jnp.full((16, TILE), one, F32)], axis=0).astype(BF16)


def fold(acc):
    return (acc[0:8] + acc[8:16]) * C4


def fold_ones(acc):
    return jnp.concatenate([acc[0:8] + acc[8:16], acc[16:24]], axis=0) * C4


def span(t):
    return pl.ds(pl.multiple_of(t * TILE, TILE), TILE)


def params(mib=12):
    return pltpu.CompilerParams(vmem_limit_bytes=mib * 1024 * 1024)


def f32(*shape):
    return jax.ShapeDtypeStruct(shape, F32)


def vmem_bf16(*shape):
    return pltpu.VMEM(shape, BF16)


def prep(partners, points, targets):
    n, d = points.shape
    nt = n // TILE

    def body(p_hbm, pts_ref, r_hbm, table_ref, msg_ref, *refs):
        outs, (r_ref, p_ref, sems) = refs[:-3], refs[-3:]
        g = lax.axis_index("group")
        dev = lax.axis_index("dev")
        copies = [pltpu.make_async_copy(r_hbm, r_ref, sems.at[nt])]
        for t in range(nt):
            s = slice(t * TILE, (t + 1) * TILE)
            copies.append(pltpu.make_async_copy(pts_ref.at[s, :], msg_ref.at[t, pl.ds(0, TILE), :], sems.at[t]))
        table_copy = pltpu.make_async_copy(p_hbm, p_ref, sems.at[nt + 1])
        table_copy.start()
        for cp in copies:
            cp.start()
        table_copy.wait()
        for h in range(8):
            for c in range(2):
                table_ref[h * 2 + c] = p_ref[h, g, c, dev]
                table_ref[16 + h * 2 + c] = p_ref[g, h, c, dev]
        for cp in copies:
            cp.wait()
        for t in range(nt):
            s = slice(t * TILE, (t + 1) * TILE)
            v = r_ref[:, s]
            hi = v.astype(BF16).astype(F32)
            msg_ref[t, TILE:, :] = jnp.concatenate([hi, v - hi], axis=1).astype(BF16)
        for k, out in zip(SWAPS, outs):
            for c in range(2):
                out[c] = msg_ref[jnp.maximum(p_ref[g ^ k, g, c, dev], 0)]

    return pl.pallas_call(
        body,
        out_shape=[jax.ShapeDtypeStruct((32,), jnp.int32), vmem_bf16(nt, TILE + EXTRA, d)]
        + [vmem_bf16(2, TILE + EXTRA, d) for _ in SWAPS],
        in_specs=[HBM, HBM, HBM],
        out_specs=[SMEM] + [VM] * (1 + len(SWAPS)),
        scratch_shapes=[
            pltpu.VMEM((8, n), F32),
            pltpu.SMEM(partners.shape, jnp.int32),
            pltpu.SemaphoreType.DMA((nt + 2,)),
        ],
        compiler_params=params(),
        name="prep",
    )(*(pltpu.with_memory_space_constraint(x, pltpu.HBM) for x in (partners, points, targets)))


def gate(held, arrived):
    m = len(held)

    def body(*refs):
        pass

    return pl.pallas_call(
        body,
        out_shape=[vmem_bf16(*x.shape) for x in held],
        in_specs=[VM] * m + [ANY] * len(arrived),
        out_specs=[VM] * m,
        input_output_aliases={i: i for i in range(m)},
        compiler_params=params(4),
        name="gate",
    )(*held, *arrived)


def local_first(own):
    nt, _, _ = own.shape
    n = nt * TILE

    def body(a_ref, k_ref, acc_ref, na, nb, va):
        for i in range(nt):
            s = slice(i * TILE, (i + 1) * TILE)
            x = col_norms(a_ref[i, 0:TILE, :])
            na[s, :] = x
            nb[:, s] = x.T[0:8]
            va[:, s] = rhs_ones(a_ref[i, TILE:, :], 1.0)

        def step(t, carry):
            s = span(t)
            b = a_ref[t, 0:TILE, :] * jnp.asarray(-2.0, BF16)
            for i in range(nt):
                c = slice(i * TILE, (i + 1) * TILE)
                k_ref[t, c, :] = kernel_tile(a_ref[i, 0:TILE, :], b, na[c, :], nb[0:1, s])
            acc_ref[:, s] = fold_ones(mm(va[...], k_ref[t], NN))
            return carry

        lax.fori_loop(0, nt, step, 0, unroll=2)

    return pl.pallas_call(
        body,
        out_shape=(vmem_bf16(nt, n, TILE), f32(16, n)),
        in_specs=[VM],
        out_specs=(VM, VM),
        scratch_shapes=[pltpu.VMEM((n, 128), F32), pltpu.VMEM((8, n), F32), pltpu.VMEM((32, n), BF16)],
        compiler_params=params(),
        name="local_first",
    )(own)


def band_first(left, own, right, after):
    nt, _, _ = own.shape
    n = nt * TILE
    m = len(after)

    def body(l_ref, a_ref, b_ref, *refs):
        k_ref, col_ref, rowl_ref, rowo_ref, na, nb, va, vb, acc = refs[m:]
        v = lax.axis_index("dev")
        has_left = (v > 0).astype(F32)
        has_right = (v < lax.axis_size("dev") - 1).astype(F32)
        for i in range(nt):
            s = slice(i * TILE, (i + 1) * TILE)
            e = slice(n + i * TILE, n + (i + 1) * TILE)
            na[s, :] = col_norms(l_ref[i, 0:TILE, :])
            na[e, :] = col_norms(a_ref[i, 0:TILE, :])
            nb[:, s] = col_norms(b_ref[i, 0:TILE, :]).T[0:8]
            va[:, s] = rhs_ones(l_ref[i, TILE:, :], has_left)
            va[:, e] = rhs_ones(a_ref[i, TILE:, :], 1.0)
            vb[:, s] = rhs_ones(b_ref[i, TILE:, :], has_right)
        acc[...] = jnp.zeros_like(acc)

        def step(t, carry):
            s = span(t)
            b = b_ref[t, 0:TILE, :] * jnp.asarray(-2.0, BF16)
            for j, x in enumerate((l_ref, a_ref)):
                for i in range(nt):
                    e = slice((j * nt + i) * TILE, (j * nt + i + 1) * TILE)
                    k_ref[t, e, :] = kernel_tile(x[i, 0:TILE, :], b, na[e, :], nb[0:1, s])
            k = k_ref[t]
            col_ref[:, s] = fold_ones(mm(va[...], k, NN))
            acc[...] += mm(vb[:, s], k, NT)
            return carry

        lax.fori_loop(0, nt, step, 0, unroll=2)
        rows = fold_ones(acc[...])
        rowl_ref[...] = rows[:, 0:n]
        rowo_ref[...] = rows[:, n:]

    return pl.pallas_call(
        body,
        out_shape=(vmem_bf16(nt, 2 * n, TILE), f32(16, n), f32(16, n), f32(16, n)),
        in_specs=[VM] * 3 + [ANY] * m,
        out_specs=(VM,) * 4,
        scratch_shapes=[
            pltpu.VMEM((2 * n, 128), F32),
            pltpu.VMEM((8, n), F32),
            pltpu.VMEM((32, 2 * n), BF16),
            pltpu.VMEM((32, n), BF16),
            pltpu.VMEM((32, 2 * n), F32),
        ],
        compiler_params=params(),
        name="band_first",
    )(left, own, right, *after)


def cross_first(ks, table, own, tiles, after, held=()):
    nt, _, d = own.shape
    n = nt * TILE
    m = len(ks)
    slots = 2 * m
    p = len(held)

    def body(q_ref, a_ref, _, *refs):
        tile_refs = refs[:m]
        k_ref, row_ref, *cols = refs[m + p : 2 * m + p + 2]
        buf, jobs, sems, na, va, acc, nb, col = refs[2 * m + 2 * p + 2 :]
        g = lax.axis_index("group")
        count = jnp.int32(0)
        for i, k in enumerate(ks):
            for c in range(2):
                live = q_ref[16 + (g ^ k) * 2 + c] >= 0

                @pl.when(live)
                def _(count=count, i=i, k=k, c=c):
                    pltpu.make_async_copy(tile_refs[i].at[c], buf.at[count], sems.at[count]).start()
                    jobs[count] = 2 * i + c

                count = count + live.astype(jnp.int32)
        for i in range(nt):
            s = slice(i * TILE, (i + 1) * TILE)
            na[s, :] = col_norms(a_ref[i, 0:TILE, :])
            va[:, s] = rhs_ones(a_ref[i, TILE:, :], 1.0)
        acc[...] = jnp.zeros_like(acc)

        def step(j, carry):
            pltpu.make_async_copy(tile_refs[0].at[0], buf.at[j], sems.at[j]).wait()
            b = buf[j, 0:TILE, :]
            nb[...] = col_norms(b).T[0:8]
            b = b * jnp.asarray(-2.0, BF16)
            vb = rhs_ones(buf[j, TILE:, :], 1.0)
            for i in range(nt):
                c = slice(i * TILE, (i + 1) * TILE)
                k_ref[j, c, :] = kernel_tile(a_ref[i, 0:TILE, :], b, na[c, :], nb[0:1, :])
            k = k_ref[j]
            col[jobs[j]] = fold_ones(mm(va[...], k, NN))
            acc[...] += mm(vb, k, NT)
            return carry

        lax.fori_loop(0, count, step, 0)
        row_ref[...] = fold_ones(acc[...])
        for i, out in enumerate(cols):
            out[...] = col[2 * i : 2 * i + 2]

    return pl.pallas_call(
        body,
        out_shape=[vmem_bf16(slots, n, TILE), f32(16, n)] + [f32(2, 16, TILE)] * (m + p),
        in_specs=[SMEM, VM, ANY] + [ANY] * m + [VM] * p,
        out_specs=[VM] * (2 + m + p),
        input_output_aliases={3 + m + i: 2 + m + i for i in range(p)},
        scratch_shapes=[
            pltpu.VMEM((slots, TILE + EXTRA, d), BF16),
            pltpu.SMEM((slots,), jnp.int32),
            pltpu.SemaphoreType.DMA((slots,)),
            pltpu.VMEM((n, 128), F32),
            pltpu.VMEM((32, n), BF16),
            pltpu.VMEM((32, n), F32),
            pltpu.VMEM((8, TILE), F32),
            pltpu.VMEM((slots, 16, TILE), F32),
        ],
        compiler_params=params(),
    )(table, own, after, *tiles, *held)


def combine(table, r, parts, ret):
    n = r.shape[1]
    m = len(parts)

    def body(q_ref, r_ref, *refs):
        part_refs, (*x_refs, w_ref, deg_ref, sum_ref, acc) = refs[:m], refs[m:]
        x_refs, (own_ref, relay_ref) = x_refs[:7], x_refs[7:]
        g = lax.axis_index("group")
        total = part_refs[0][...]
        for p in part_refs[1:]:
            total = total + p[...]
        acc[...] = total
        for k, x in zip(SWAPS, x_refs):
            for c in range(2):
                t = q_ref[(g ^ k) * 2 + c]

                @pl.when(t >= 0)
                def _(x=x, c=c, t=t):
                    acc[:, span(t)] = acc[:, span(t)] + x[c]

        rv = r_ref[...]
        deg = acc[8:16, :]
        w = 0.5 * (deg * rv - acc[0:8, :])
        w_ref[...] = w
        deg_ref[...] = deg
        for j in range(4):
            for out, k in ((own_ref, 2 * j), (relay_ref, 2 * j + 1)):
                for c in range(2):
                    t = jnp.maximum(q_ref[(g ^ k) * 2 + c], 0)
                    out[j, c * 8 : c * 8 + 8, :] = w_ref[:, span(t)]
        lane = lax.broadcasted_iota(jnp.int32, (8, 128), 1)
        sums = jnp.zeros((8, 128), F32)
        for k, v in enumerate((rv * rv, rv * w, w * w, 0.5 * deg * w * w)):
            sums = jnp.where(lane == k, jnp.sum(v, axis=1, keepdims=True), sums)
        sum_ref[...] = sums

    return pl.pallas_call(
        body,
        out_shape=[f32(4, 16, TILE), f32(4, 16, TILE), f32(8, n), f32(8, n), f32(8, 128)],
        in_specs=[SMEM] + [VM] * (m + 8),
        out_specs=[VM] * 5,
        scratch_shapes=[pltpu.VMEM((16, n), F32)],
        compiler_params=params(),
        name="combine",
    )(table, r, *parts, *ret)


def relay(own, partner):
    def body(own_ref, partner_ref, *outs):
        for j, out in enumerate(outs):
            out[0] = own_ref[j + 1]
            out[1] = partner_ref[j + 1]

    return pl.pallas_call(
        body,
        out_shape=[f32(2, 16, TILE)] * 3,
        in_specs=[VM, VM],
        out_specs=[VM] * 3,
        compiler_params=params(4),
        name="relay",
    )(own, partner)


def local_second(k_local, w):
    nt, n, _ = k_local.shape

    def body(k_ref, w_ref, out_ref):
        va = split(w_ref[...])
        for t in range(nt):
            out_ref[:, t * TILE : (t + 1) * TILE] = fold(mm(va, k_ref[t], NN))

    return pl.pallas_call(
        body,
        out_shape=f32(8, n),
        in_specs=[VM, VM],
        out_specs=VM,
        compiler_params=params(),
        name="local_second",
    )(k_local, w)


def band_second(k_band, w_left, w, w_right, after):
    nt, n2, _ = k_band.shape
    n = n2 // 2

    def body(k_ref, wl_ref, w_ref, wb_ref, _, col_ref, rowl_ref, rowo_ref, va, acc):
        va[:, 0:n] = split(wl_ref[...])
        va[:, n:] = split(w_ref[...])
        vb = split(wb_ref[...])
        for t in range(nt):
            s = slice(t * TILE, (t + 1) * TILE)
            col_ref[:, s] = fold(mm(va[...], k_ref[t], NN))
            new = mm(vb[:, s], k_ref[t], NT)
            acc[...] = new if t == 0 else acc[...] + new
        rows = fold(acc[...])
        rowl_ref[...] = rows[:, 0:n]
        rowo_ref[...] = rows[:, n:]

    return pl.pallas_call(
        body,
        out_shape=(f32(8, n), f32(8, n), f32(8, n)),
        in_specs=[VM] * 4 + [ANY],
        out_specs=(VM,) * 3,
        scratch_shapes=[pltpu.VMEM((16, n2), BF16), pltpu.VMEM((16, n2), F32)],
        compiler_params=params(),
        name="band_second",
    )(k_band, w_left, w, w_right, after)


def cross_second(table, k_caches, w, xw, sums, loc, row_left, row_own, w_left):
    n = w.shape[1]

    def body(
        q_ref, ka_ref, kb_ref, kc_ref, w_ref, sum_ref, loc_ref, rl_ref, ro_ref, wl_ref, *refs
    ):
        near_ref, *chip_refs, col_ref, row_ref, va, acc, jobs, xw_ref = refs
        g = lax.axis_index("group")
        xw_ref[g ^ 1] = near_ref[0]
        for j, x in enumerate(chip_refs):
            for i in range(2):
                xw_ref[g ^ (2 * j + 2 + i)] = x[i]
        va[...] = split(w_ref[...])
        acc[...] = jnp.zeros_like(acc)
        for ks, k_ref in zip(STAGES, (ka_ref, kb_ref, kc_ref)):
            count = jnp.int32(0)
            for k in ks:
                for c in range(2):
                    live = q_ref[16 + (g ^ k) * 2 + c] >= 0

                    @pl.when(live)
                    def _(count=count, k=k, c=c):
                        jobs[count] = (g ^ k) * 2 + c

                    count = count + live.astype(jnp.int32)

            def step(j, carry, k_ref=k_ref):
                slot = jobs[j]
                h, c = slot >> 1, slot & 1
                rows = pl.ds(pl.multiple_of(c * 8, 8), 8)
                k = k_ref[j]
                col_ref[h, rows, :] = fold(mm(va[...], k, NN))
                acc[...] += mm(split(xw_ref[h, rows, :]), k, NT)
                return carry

            lax.fori_loop(0, count, step, 0)
        row = fold(acc[...])
        row_ref[...] = row
        pairs = w_ref[...] * (0.5 * loc_ref[...] + ro_ref[...] + row) + wl_ref[...] * rl_ref[...]
        lane = lax.broadcasted_iota(jnp.int32, (8, 128), 1)
        pay = jnp.where(lane == 3, sum_ref[...] - jnp.sum(pairs, axis=1, keepdims=True), sum_ref[...])
        for h in range(8):
            col_ref[h, 16:24, 0:128] = pay
            col_ref[h, 16:24, 128:] = jnp.zeros((8, 128), F32)

    return pl.pallas_call(
        body,
        out_shape=(f32(8, 24, TILE), f32(8, n)),
        in_specs=[SMEM] + [VM] * 13,
        out_specs=(VM, VM),
        scratch_shapes=[
            pltpu.VMEM((16, n), BF16),
            pltpu.VMEM((16, n), F32),
            pltpu.SMEM((16,), jnp.int32),
            pltpu.VMEM((8, 16, TILE), F32),
        ],
        compiler_params=params(),
        name="cross_second",
    )(table, *k_caches, w, sums, loc, row_left, row_own, w_left, *xw)


def group_sum(table, w, deg, parts, ret):
    n = w.shape[1]
    m = len(parts)

    def body(q_ref, w_ref, deg_ref, *refs):
        part_refs, (x_ref, w2_ref, out_ref, acc) = refs[:m], refs[m:]
        total = part_refs[0][...]
        for p in part_refs[1:]:
            total = total + p[...]
        acc[...] = total
        for h in range(8):
            for c in range(2):
                t = q_ref[h * 2 + c]

                @pl.when(t >= 0)
                def _(h=h, c=c, t=t):
                    acc[:, span(t)] = acc[:, span(t)] + x_ref[h, c * 8 : c * 8 + 8, :]

        w2_ref[...] = 0.5 * (deg_ref[...] * w_ref[...] - acc[...])
        sums = x_ref[0, 16:24, 0:128]
        for h in range(1, 8):
            sums = sums + x_ref[h, 16:24, 0:128]
        for v in range(16):
            out_ref[v] = sums

    return pl.pallas_call(
        body,
        out_shape=(f32(8, n), f32(16, 8, 128)),
        in_specs=[SMEM] + [VM] * (3 + m),
        out_specs=(VM, VM),
        scratch_shapes=[pltpu.VMEM((8, n), F32)],
        compiler_params=params(),
        name="group_sum",
    )(table, w, deg, *parts, ret)


def finish(gathered, r, w, w2):
    n = r.shape[1]

    def body(g_ref, r_ref, w_ref, w2_ref, sol_ref, res_ref):
        sums = g_ref[0]
        for v in range(1, 16):
            sums = sums + g_ref[v]
        rho, mu, nu, xi = (sums[:, k : k + 1] for k in range(4))
        rv = r_ref[...]
        wv = w_ref[...]
        first = rho / (rho + mu)
        gap = (nu - mu * (mu / rho)) * (first * first)
        beta = gap / rho
        cr = mu / (rho + mu) + beta
        curvature = cr * cr * (rho + mu) - 2.0 * cr * first * (mu + nu) + first * first * (nu + xi)
        second = gap / curvature
        sol_ref[...] = (first + second * cr) * rv - (second * first) * wv
        res_ref[...] = (
            (mu / (rho + mu) - second * cr) * rv
            + (second * (first - cr) - first) * wv
            + (second * first) * w2_ref[...]
        )

    return pl.pallas_call(
        body,
        out_shape=(f32(8, n), f32(8, n)),
        in_specs=[VM] * 4,
        out_specs=(VM, VM),
        compiler_params=params(),
        name="finish",
    )(gathered, r, w, w2)


def on_device(points, targets, partner_tiles):
    dev_count = lax.axis_size("dev")
    to_right = [(i, i + 1) for i in range(dev_count - 1)]
    to_left = [(i + 1, i) for i in range(dev_count - 1)]

    def right_of(x):
        return lax.ppermute(x, "dev", to_left)

    def left_of(x):
        return lax.ppermute(x, "dev", to_right)

    def swap(x, k):
        return lax.ppermute(x, "group", [(i, i ^ k) for i in range(8)])

    def trade(x, axis="group"):
        return lax.all_to_all(x, axis, split_axis=0, concat_axis=0, tiled=True)

    table, own, *outgoing = prep(jnp.transpose(partner_tiles, (0, 2, 3, 1)), points, targets)
    arrived = {}
    for x, k in zip(outgoing, SWAPS[:5]):
        arrived[k] = swap(x, k)
    left = left_of(own)
    right = right_of(own)
    k_local, acc_local = local_first(own)

    def cross(stage, after, held=()):
        return cross_first(stage, table, own, [arrived[k] for k in stage], after, held)

    k_a, row_a, *col_a = cross(STAGES[0], acc_local)
    for x, k in zip(gate(outgoing[5:], [row_a, arrived[3], arrived[7]]), STAGES[2]):
        arrived[k] = swap(x, k)
    k_b, row_b, *col_b = cross(STAGES[1], row_a, col_a)
    ret_near = []
    for x, k in zip(col_b, STAGES[1] + STAGES[0]):
        ret_near.append(swap(x, k))
    k_band, to_r, to_l, acc_band = band_first(left, own, right, [row_b])
    from_left, from_right = left_of(to_r), right_of(to_l)
    k_c, row_c, *col_c = cross(STAGES[2], acc_band)
    ret = ret_near[2:] + ret_near[:2] + [swap(x, k) for x, k in zip(col_c, STAGES[2])]
    w_own, w_relay, w, deg, sums = combine(
        table, targets, (acc_local, acc_band, from_left, from_right, row_a, row_b, row_c), ret
    )
    w_left = left_of(w)
    w_right = right_of(w)
    partner = swap(w_relay, 1)
    xw = [partner] + [swap(x, 2 * j + 2) for j, x in enumerate(relay(w_own, partner))]
    loc2 = local_second(k_local, w)
    col_r, rowl_b, rowo_b = band_second(k_band, w_left, w, w_right, loc2)
    from_left2, from_right2 = left_of(col_r), right_of(rowl_b)
    col_x, row_x = cross_second(table, (k_a, k_b, k_c), w, xw, sums, loc2, rowl_b, rowo_b, w_left)
    w2, column = group_sum(table, w, deg, (loc2, rowo_b, row_x, from_left2, from_right2), trade(col_x))
    return finish(trade(column, "dev"), targets, w, w2)


def solution(mesh):
    return jax.shard_map(
        on_device,
        mesh=mesh,
        in_specs=(P(("group", "dev"), None), P(None, ("group", "dev")), P()),
        out_specs=(P(None, ("group", "dev")), P(None, ("group", "dev"))),
        check_vma=False,
    )
```

```python
import jax
import jax.numpy as jnp
from jax import lax
from jax.experimental import pallas as pl
from jax.experimental.pallas import tpu as pltpu
from jax.sharding import PartitionSpec as P


TILE = 256
EXTRA = 8
SCALE = 3.9
C4 = 4.0 / SCALE**5
CUT = 5.0 * SCALE / 4.0
NT = (((1,), (1,)), ((), ()))
NN = (((1,), (0,)), ((), ()))
F32 = jnp.float32
BF16 = jnp.bfloat16
STAGES = ((2, 6, 1), (3, 7), (4, 5))
SWAPS = STAGES[0] + STAGES[1] + STAGES[2]

SMEM = pl.BlockSpec(memory_space=pltpu.SMEM)
ANY = pl.BlockSpec(memory_space=pl.ANY)
HBM = pl.BlockSpec(memory_space=pltpu.HBM)
VM = pl.BlockSpec(memory_space=pltpu.VMEM)


def mm(a, b, dims):
    return lax.dot_general(a, b, dims, preferred_element_type=F32)


def col_norms(x):
    x = x.astype(F32)
    return jnp.broadcast_to(jnp.sum(x * x, axis=1, keepdims=True), (x.shape[0], 128))


def kernel_tile(a, b_scaled, na, nb):
    q = mm(a, b_scaled, NT) + (jnp.concatenate([na, na], axis=1) + nb)
    q = jnp.maximum(q, 1e-30)
    u = jnp.maximum(SCALE - q * lax.rsqrt(q), 0.0)
    t = u * u
    return (t * t * (CUT - u)).astype(BF16)


def split(v):
    hi = v.astype(BF16)
    lo = (v - hi.astype(F32)).astype(BF16)
    return jnp.concatenate([hi, lo], axis=0)


def rhs_ones(rows, one):
    v = rows.astype(F32)
    return jnp.concatenate([v[:, 0:TILE], v[:, TILE:], jnp.full((16, TILE), one, F32)], axis=0).astype(BF16)


def fold(acc):
    return (acc[0:8] + acc[8:16]) * C4


def fold_ones(acc):
    return jnp.concatenate([acc[0:8] + acc[8:16], acc[16:24]], axis=0) * C4


def span(t):
    return pl.ds(pl.multiple_of(t * TILE, TILE), TILE)


def params(mib=12):
    return pltpu.CompilerParams(vmem_limit_bytes=mib * 1024 * 1024)


def f32(*shape):
    return jax.ShapeDtypeStruct(shape, F32)


def vmem_bf16(*shape):
    return pltpu.VMEM(shape, BF16)


def prep(partners, points, targets):
    n, d = points.shape
    nt = n // TILE

    def body(p_hbm, pts_ref, r_hbm, table_ref, msg_ref, *refs):
        outs, (r_ref, p_ref, sems) = refs[:-3], refs[-3:]
        g = lax.axis_index("group")
        dev = lax.axis_index("dev")
        copies = [pltpu.make_async_copy(r_hbm, r_ref, sems.at[nt])]
        for t in range(nt):
            s = slice(t * TILE, (t + 1) * TILE)
            copies.append(pltpu.make_async_copy(pts_ref.at[s, :], msg_ref.at[t, pl.ds(0, TILE), :], sems.at[t]))
        table_copy = pltpu.make_async_copy(p_hbm, p_ref, sems.at[nt + 1])
        table_copy.start()
        for cp in copies:
            cp.start()
        table_copy.wait()
        for h in range(8):
            for c in range(2):
                table_ref[h * 2 + c] = p_ref[h, g, c, dev]
                table_ref[16 + h * 2 + c] = p_ref[g, h, c, dev]
        for cp in copies:
            cp.wait()
        for t in range(nt):
            s = slice(t * TILE, (t + 1) * TILE)
            v = r_ref[:, s]
            hi = v.astype(BF16).astype(F32)
            msg_ref[t, TILE:, :] = jnp.concatenate([hi, v - hi], axis=1).astype(BF16)
        for k, out in zip(SWAPS, outs):
            for c in range(2):
                out[c] = msg_ref[jnp.maximum(p_ref[g ^ k, g, c, dev], 0)]

    return pl.pallas_call(
        body,
        out_shape=[jax.ShapeDtypeStruct((32,), jnp.int32), vmem_bf16(nt, TILE + EXTRA, d)]
        + [vmem_bf16(2, TILE + EXTRA, d) for _ in SWAPS],
        in_specs=[HBM, HBM, HBM],
        out_specs=[SMEM] + [VM] * (1 + len(SWAPS)),
        scratch_shapes=[
            pltpu.VMEM((8, n), F32),
            pltpu.SMEM(partners.shape, jnp.int32),
            pltpu.SemaphoreType.DMA((nt + 2,)),
        ],
        compiler_params=params(),
        name="prep",
    )(*(pltpu.with_memory_space_constraint(x, pltpu.HBM) for x in (partners, points, targets)))


def gate(held, arrived):
    m = len(held)

    def body(*refs):
        pass

    return pl.pallas_call(
        body,
        out_shape=[vmem_bf16(*x.shape) for x in held],
        in_specs=[VM] * m + [ANY] * len(arrived),
        out_specs=[VM] * m,
        input_output_aliases={i: i for i in range(m)},
        compiler_params=params(4),
        name="gate",
    )(*held, *arrived)


def local_first(own, after):
    nt, _, _ = own.shape
    n = nt * TILE

    def body(a_ref, _, k_ref, acc_ref, na, nb, va):
        for i in range(nt):
            s = slice(i * TILE, (i + 1) * TILE)
            x = col_norms(a_ref[i, 0:TILE, :])
            na[s, :] = x
            nb[:, s] = x.T[0:8]
            va[:, s] = rhs_ones(a_ref[i, TILE:, :], 1.0)

        def step(t, carry):
            s = span(t)
            b = a_ref[t, 0:TILE, :] * jnp.asarray(-2.0, BF16)
            for i in range(nt):
                c = slice(i * TILE, (i + 1) * TILE)
                k_ref[t, c, :] = kernel_tile(a_ref[i, 0:TILE, :], b, na[c, :], nb[0:1, s])
            acc_ref[:, s] = fold_ones(mm(va[...], k_ref[t], NN))
            return carry

        lax.fori_loop(0, nt, step, 0, unroll=2)

    return pl.pallas_call(
        body,
        out_shape=(vmem_bf16(nt, n, TILE), f32(16, n)),
        in_specs=[VM, ANY],
        out_specs=(VM, VM),
        scratch_shapes=[pltpu.VMEM((n, 128), F32), pltpu.VMEM((8, n), F32), pltpu.VMEM((32, n), BF16)],
        compiler_params=params(),
        name="local_first",
    )(own, after)


def band_first(left, own, right, after):
    nt, _, _ = own.shape
    n = nt * TILE
    m = len(after)

    def body(l_ref, a_ref, b_ref, *refs):
        k_ref, col_ref, rowl_ref, rowo_ref, na, nb, va, vb, acc = refs[m:]
        v = lax.axis_index("dev")
        has_left = (v > 0).astype(F32)
        has_right = (v < lax.axis_size("dev") - 1).astype(F32)
        for i in range(nt):
            s = slice(i * TILE, (i + 1) * TILE)
            e = slice(n + i * TILE, n + (i + 1) * TILE)
            na[s, :] = col_norms(l_ref[i, 0:TILE, :])
            na[e, :] = col_norms(a_ref[i, 0:TILE, :])
            nb[:, s] = col_norms(b_ref[i, 0:TILE, :]).T[0:8]
            va[:, s] = rhs_ones(l_ref[i, TILE:, :], has_left)
            va[:, e] = rhs_ones(a_ref[i, TILE:, :], 1.0)
            vb[:, s] = rhs_ones(b_ref[i, TILE:, :], has_right)
        acc[...] = jnp.zeros_like(acc)

        def step(t, carry):
            s = span(t)
            b = b_ref[t, 0:TILE, :] * jnp.asarray(-2.0, BF16)
            for j, x in enumerate((l_ref, a_ref)):
                for i in range(nt):
                    e = slice((j * nt + i) * TILE, (j * nt + i + 1) * TILE)
                    k_ref[t, e, :] = kernel_tile(x[i, 0:TILE, :], b, na[e, :], nb[0:1, s])
            k = k_ref[t]
            col_ref[:, s] = fold_ones(mm(va[...], k, NN))
            acc[...] += mm(vb[:, s], k, NT)
            return carry

        lax.fori_loop(0, nt, step, 0, unroll=2)
        rows = fold_ones(acc[...])
        rowl_ref[...] = rows[:, 0:n]
        rowo_ref[...] = rows[:, n:]

    return pl.pallas_call(
        body,
        out_shape=(vmem_bf16(nt, 2 * n, TILE), f32(16, n), f32(16, n), f32(16, n)),
        in_specs=[VM] * 3 + [ANY] * m,
        out_specs=(VM,) * 4,
        scratch_shapes=[
            pltpu.VMEM((2 * n, 128), F32),
            pltpu.VMEM((8, n), F32),
            pltpu.VMEM((32, 2 * n), BF16),
            pltpu.VMEM((32, n), BF16),
            pltpu.VMEM((32, 2 * n), F32),
        ],
        compiler_params=params(),
        name="band_first",
    )(left, own, right, *after)


def cross_first(ks, table, own, tiles, after):
    nt, _, d = own.shape
    n = nt * TILE
    m = len(ks)
    slots = 2 * m

    def body(q_ref, a_ref, _, *refs):
        tile_refs = refs[:m]
        k_ref, row_ref, *cols = refs[m : 2 * m + 2]
        buf, jobs, sems, na, va, acc, nb, col = refs[2 * m + 2 :]
        g = lax.axis_index("group")
        count = jnp.int32(0)
        for i, k in enumerate(ks):
            for c in range(2):
                live = q_ref[16 + (g ^ k) * 2 + c] >= 0

                @pl.when(live)
                def _(count=count, i=i, k=k, c=c):
                    pltpu.make_async_copy(tile_refs[i].at[c], buf.at[count], sems.at[count]).start()
                    jobs[count] = 2 * i + c

                count = count + live.astype(jnp.int32)
        for i in range(nt):
            s = slice(i * TILE, (i + 1) * TILE)
            na[s, :] = col_norms(a_ref[i, 0:TILE, :])
            va[:, s] = rhs_ones(a_ref[i, TILE:, :], 1.0)
        acc[...] = jnp.zeros_like(acc)

        def step(j, carry):
            pltpu.make_async_copy(tile_refs[0].at[0], buf.at[j], sems.at[j]).wait()
            b = buf[j, 0:TILE, :]
            nb[...] = col_norms(b).T[0:8]
            b = b * jnp.asarray(-2.0, BF16)
            vb = rhs_ones(buf[j, TILE:, :], 1.0)
            for i in range(nt):
                c = slice(i * TILE, (i + 1) * TILE)
                k_ref[j, c, :] = kernel_tile(a_ref[i, 0:TILE, :], b, na[c, :], nb[0:1, :])
            k = k_ref[j]
            col[jobs[j]] = fold_ones(mm(va[...], k, NN))
            acc[...] += mm(vb, k, NT)
            return carry

        lax.fori_loop(0, count, step, 0)
        row_ref[...] = fold_ones(acc[...])
        for i, out in enumerate(cols):
            out[...] = col[2 * i : 2 * i + 2]

    return pl.pallas_call(
        body,
        out_shape=[vmem_bf16(slots, n, TILE), f32(16, n)] + [f32(2, 16, TILE)] * m,
        in_specs=[SMEM, VM, ANY] + [ANY] * m,
        out_specs=[VM] * (2 + m),
        scratch_shapes=[
            pltpu.VMEM((slots, TILE + EXTRA, d), BF16),
            pltpu.SMEM((slots,), jnp.int32),
            pltpu.SemaphoreType.DMA((slots,)),
            pltpu.VMEM((n, 128), F32),
            pltpu.VMEM((32, n), BF16),
            pltpu.VMEM((32, n), F32),
            pltpu.VMEM((8, TILE), F32),
            pltpu.VMEM((slots, 16, TILE), F32),
        ],
        compiler_params=params(),
    )(table, own, after, *tiles)


def combine(table, r, parts, ret):
    n = r.shape[1]
    m = len(parts)

    def body(q_ref, r_ref, *refs):
        part_refs, (*x_refs, w_ref, deg_ref, sum_ref, acc) = refs[:m], refs[m:]
        x_refs, (own_ref, relay_ref) = x_refs[:7], x_refs[7:]
        g = lax.axis_index("group")
        total = part_refs[0][...]
        for p in part_refs[1:]:
            total = total + p[...]
        acc[...] = total
        for k, x in zip(SWAPS, x_refs):
            for c in range(2):
                t = q_ref[(g ^ k) * 2 + c]

                @pl.when(t >= 0)
                def _(x=x, c=c, t=t):
                    acc[:, span(t)] = acc[:, span(t)] + x[c]

        rv = r_ref[...]
        deg = acc[8:16, :]
        w = 0.5 * (deg * rv - acc[0:8, :])
        w_ref[...] = w
        deg_ref[...] = deg
        for j in range(4):
            for out, k in ((own_ref, 2 * j), (relay_ref, 2 * j + 1)):
                for c in range(2):
                    t = jnp.maximum(q_ref[(g ^ k) * 2 + c], 0)
                    out[j, c * 8 : c * 8 + 8, :] = w_ref[:, span(t)]
        lane = lax.broadcasted_iota(jnp.int32, (8, 128), 1)
        sums = jnp.zeros((8, 128), F32)
        for k, v in enumerate((rv * rv, rv * w, w * w, 0.5 * deg * w * w)):
            sums = jnp.where(lane == k, jnp.sum(v, axis=1, keepdims=True), sums)
        sum_ref[...] = sums

    return pl.pallas_call(
        body,
        out_shape=[f32(4, 16, TILE), f32(4, 16, TILE), f32(8, n), f32(8, n), f32(8, 128)],
        in_specs=[SMEM] + [VM] * (m + 8),
        out_specs=[VM] * 5,
        scratch_shapes=[pltpu.VMEM((16, n), F32)],
        compiler_params=params(),
        name="combine",
    )(table, r, *parts, *ret)


def relay(own, partner):
    summed = own.shape[0] == 5

    def body(own_ref, partner_ref, *outs):
        for j, out in enumerate(outs):
            out[0] = own_ref[j + 1]
            out[1] = partner_ref[j + 1]
            if summed:
                out[2] = own_ref[4] + partner_ref[4]

    return pl.pallas_call(
        body,
        out_shape=[f32(2 + summed, 16, TILE)] * 3,
        in_specs=[VM, VM],
        out_specs=[VM] * 3,
        compiler_params=params(4),
        name="relay",
    )(own, partner)


def local_second(k_local, w):
    nt, n, _ = k_local.shape

    def body(k_ref, w_ref, out_ref):
        va = split(w_ref[...])
        for t in range(nt):
            out_ref[:, t * TILE : (t + 1) * TILE] = fold(mm(va, k_ref[t], NN))

    return pl.pallas_call(
        body,
        out_shape=f32(8, n),
        in_specs=[VM, VM],
        out_specs=VM,
        compiler_params=params(),
        name="local_second",
    )(k_local, w)


def band_second(k_band, w_left, w, w_right, after):
    nt, n2, _ = k_band.shape
    n = n2 // 2

    def body(k_ref, wl_ref, w_ref, wb_ref, _, col_ref, rowl_ref, rowo_ref, va, acc):
        va[:, 0:n] = split(wl_ref[...])
        va[:, n:] = split(w_ref[...])
        vb = split(wb_ref[...])
        for t in range(nt):
            s = slice(t * TILE, (t + 1) * TILE)
            col_ref[:, s] = fold(mm(va[...], k_ref[t], NN))
            new = mm(vb[:, s], k_ref[t], NT)
            acc[...] = new if t == 0 else acc[...] + new
        rows = fold(acc[...])
        rowl_ref[...] = rows[:, 0:n]
        rowo_ref[...] = rows[:, n:]

    return pl.pallas_call(
        body,
        out_shape=(f32(8, n), f32(8, n), f32(8, n)),
        in_specs=[VM] * 4 + [ANY],
        out_specs=(VM,) * 3,
        scratch_shapes=[pltpu.VMEM((16, n2), BF16), pltpu.VMEM((16, n2), F32)],
        compiler_params=params(),
        name="band_second",
    )(k_band, w_left, w, w_right, after)


def cross_second(table, k_caches, w, xw, sums, loc, row_left, row_own, w_left):
    n = w.shape[1]

    def body(
        q_ref, ka_ref, kb_ref, kc_ref, w_ref, sum_ref, loc_ref, rl_ref, ro_ref, wl_ref, *refs
    ):
        near_ref, *chip_refs, own_ref, relay_ref, row_ref, va, acc, jobs, xw_ref, col_ref = refs
        g = lax.axis_index("group")
        xw_ref[g ^ 1] = near_ref[0]
        for j, x in enumerate(chip_refs):
            for i in range(2):
                xw_ref[g ^ (2 * j + 2 + i)] = x[i]
        va[...] = split(w_ref[...])
        acc[...] = jnp.zeros_like(acc)
        for ks, k_ref in zip(STAGES, (ka_ref, kb_ref, kc_ref)):
            count = jnp.int32(0)
            for k in ks:
                for c in range(2):
                    live = q_ref[16 + (g ^ k) * 2 + c] >= 0

                    @pl.when(live)
                    def _(count=count, k=k, c=c):
                        jobs[count] = (g ^ k) * 2 + c

                    count = count + live.astype(jnp.int32)

            def step(j, carry, k_ref=k_ref):
                slot = jobs[j]
                h, c = slot >> 1, slot & 1
                rows = pl.ds(pl.multiple_of(c * 8, 8), 8)
                k = k_ref[j]
                col_ref[h, rows, :] = fold(mm(va[...], k, NN))
                acc[...] += mm(split(xw_ref[h, rows, :]), k, NT)
                return carry

            lax.fori_loop(0, count, step, 0)
        row = fold(acc[...])
        row_ref[...] = row
        pairs = w_ref[...] * (0.5 * loc_ref[...] + ro_ref[...] + row) + wl_ref[...] * rl_ref[...]
        lane = lax.broadcasted_iota(jnp.int32, (8, 128), 1)
        pay = jnp.where(lane == 3, sum_ref[...] - jnp.sum(pairs, axis=1, keepdims=True), sum_ref[...])
        for j in range(4):
            own_ref[j] = col_ref[g ^ (2 * j)]
            relay_ref[j] = col_ref[g ^ (2 * j + 1)]
        for out in (own_ref, relay_ref):
            out[4] = jnp.zeros((16, TILE), F32)
            out[4, 0:8, 0:128] = pay

    return pl.pallas_call(
        body,
        out_shape=(f32(5, 16, TILE), f32(5, 16, TILE), f32(8, n)),
        in_specs=[SMEM] + [VM] * 13,
        out_specs=(VM, VM, VM),
        scratch_shapes=[
            pltpu.VMEM((16, n), BF16),
            pltpu.VMEM((16, n), F32),
            pltpu.SMEM((16,), jnp.int32),
            pltpu.VMEM((8, 16, TILE), F32),
            pltpu.VMEM((8, 16, TILE), F32),
        ],
        compiler_params=params(),
        name="cross_second",
    )(table, *k_caches, w, sums, loc, row_left, row_own, w_left, *xw)


def group_sum(table, w, deg, parts, own, partner, chips):
    n = w.shape[1]
    m = len(parts)

    def body(q_ref, w_ref, deg_ref, *refs):
        part_refs, (own_ref, partner_ref, *chip_refs, w2_ref, out_ref, acc) = refs[:m], refs[m:]
        g = lax.axis_index("group")
        total = part_refs[0][...]
        for p in part_refs[1:]:
            total = total + p[...]
        acc[...] = total
        for k in range(1, 8):
            for c in range(2):
                t = q_ref[(g ^ k) * 2 + c]

                @pl.when(t >= 0)
                def _(k=k, c=c, t=t):
                    x = partner_ref.at[0] if k == 1 else chip_refs[k // 2 - 1].at[k % 2]
                    acc[:, span(t)] = acc[:, span(t)] + x[c * 8 : c * 8 + 8, :]

        w2_ref[...] = 0.5 * (deg_ref[...] * w_ref[...] - acc[...])
        sums = own_ref[4, 0:8, 0:128] + partner_ref[4, 0:8, 0:128]
        for x in chip_refs:
            sums = sums + x[2, 0:8, 0:128]
        for v in range(16):
            out_ref[v] = sums

    return pl.pallas_call(
        body,
        out_shape=(f32(8, n), f32(16, 8, 128)),
        in_specs=[SMEM] + [VM] * (2 + m + 5),
        out_specs=(VM, VM),
        scratch_shapes=[pltpu.VMEM((8, n), F32)],
        compiler_params=params(),
        name="group_sum",
    )(table, w, deg, *parts, own, partner, *chips)


def finish(gathered, r, w, w2):
    n = r.shape[1]

    def body(g_ref, r_ref, w_ref, w2_ref, sol_ref, res_ref):
        sums = g_ref[0]
        for v in range(1, 16):
            sums = sums + g_ref[v]
        rho, mu, nu, xi = (sums[:, k : k + 1] for k in range(4))
        rv = r_ref[...]
        wv = w_ref[...]
        first = rho / (rho + mu)
        gap = (nu - mu * (mu / rho)) * (first * first)
        beta = gap / rho
        cr = mu / (rho + mu) + beta
        curvature = cr * cr * (rho + mu) - 2.0 * cr * first * (mu + nu) + first * first * (nu + xi)
        second = gap / curvature
        sol_ref[...] = (first + second * cr) * rv - (second * first) * wv
        res_ref[...] = (
            (mu / (rho + mu) - second * cr) * rv
            + (second * (first - cr) - first) * wv
            + (second * first) * w2_ref[...]
        )

    return pl.pallas_call(
        body,
        out_shape=(f32(8, n), f32(8, n)),
        in_specs=[VM] * 4,
        out_specs=(VM, VM),
        compiler_params=params(),
        name="finish",
    )(gathered, r, w, w2)


def on_device(points, targets, partner_tiles):
    dev_count = lax.axis_size("dev")
    to_right = [(i, i + 1) for i in range(dev_count - 1)]
    to_left = [(i + 1, i) for i in range(dev_count - 1)]

    def right_of(x):
        return lax.ppermute(x, "dev", to_left)

    def left_of(x):
        return lax.ppermute(x, "dev", to_right)

    def swap(x, k):
        return lax.ppermute(x, "group", [(i, i ^ k) for i in range(8)])

    def trade(x, axis="group"):
        return lax.all_to_all(x, axis, split_axis=0, concat_axis=0, tiled=True)

    table, own, *outgoing = prep(jnp.transpose(partner_tiles, (0, 2, 3, 1)), points, targets)
    arrived = {}
    for x, k in zip(outgoing, SWAPS[:5]):
        arrived[k] = swap(x, k)
    left = left_of(own)
    right = right_of(own)

    def cross(stage, after):
        return cross_first(stage, table, own, [arrived[k] for k in stage], after)

    ret = {}

    def give_back(cols, stage):
        for x, k in zip(cols, stage):
            ret[k] = swap(x, k)

    k_a, row_a, *col_a = cross(STAGES[0], table)
    give_back(col_a, STAGES[0])
    for x, k in zip(gate(outgoing[5:], [row_a, arrived[3], arrived[7]]), STAGES[2]):
        arrived[k] = swap(x, k)
    k_b, row_b, *col_b = cross(STAGES[1], row_a)
    give_back(col_b, STAGES[1])
    k_band, to_r, to_l, acc_band = band_first(left, own, right, [row_b])
    from_left, from_right = left_of(to_r), right_of(to_l)
    k_c, row_c, *col_c = cross(STAGES[2], acc_band)
    give_back(col_c, STAGES[2])
    k_local, acc_local = local_first(own, row_c)
    w_own, w_relay, w, deg, sums = combine(
        table, targets, (acc_local, acc_band, from_left, from_right, row_a, row_b, row_c), [ret[k] for k in SWAPS]
    )
    w_left = left_of(w)
    w_right = right_of(w)
    partner = swap(w_relay, 1)
    xw = [partner] + [swap(x, 2 * j + 2) for j, x in enumerate(relay(w_own, partner))]
    loc2 = local_second(k_local, w)
    col_r, rowl_b, rowo_b = band_second(k_band, w_left, w, w_right, loc2)
    from_left2 = left_of(col_r)
    from_right2 = right_of(rowl_b)
    x_own, x_relay, row_x = cross_second(table, (k_a, k_b, k_c), w, xw, sums, loc2, rowl_b, rowo_b, w_left)
    x_partner = swap(x_relay, 1)
    chips = [swap(x, 2 * j + 2) for j, x in enumerate(relay(x_own, x_partner))]
    parts = (loc2, rowo_b, row_x, from_left2, from_right2)
    w2, column = group_sum(table, w, deg, parts, x_own, x_partner, chips)
    return finish(trade(column, "dev"), targets, w, w2)


def solution(mesh):
    return jax.shard_map(
        on_device,
        mesh=mesh,
        in_specs=(P(("group", "dev"), None), P(None, ("group", "dev")), P()),
        out_specs=(P(None, ("group", "dev")), P(None, ("group", "dev"))),
        check_vma=False,
    )
```

```python
import jax
import jax.numpy as jnp
from jax import lax
from jax.experimental import pallas as pl
from jax.experimental.pallas import tpu as pltpu
from jax.sharding import PartitionSpec as P


TILE = 256
EXTRA = 8
SCALE = 3.9
C4 = 4.0 / SCALE**5
CUT = 5.0 * SCALE / 4.0
NT = (((1,), (1,)), ((), ()))
NN = (((1,), (0,)), ((), ()))
F32 = jnp.float32
BF16 = jnp.bfloat16
STAGES = ((2, 6, 1), (3, 7), (4, 5))
SWAPS = STAGES[0] + STAGES[1] + STAGES[2]

SMEM = pl.BlockSpec(memory_space=pltpu.SMEM)
ANY = pl.BlockSpec(memory_space=pl.ANY)
HBM = pl.BlockSpec(memory_space=pltpu.HBM)
VM = pl.BlockSpec(memory_space=pltpu.VMEM)


def mm(a, b, dims):
    return lax.dot_general(a, b, dims, preferred_element_type=F32)


def col_norms(x):
    x = x.astype(F32)
    return jnp.broadcast_to(jnp.sum(x * x, axis=1, keepdims=True), (x.shape[0], 128))


def kernel_tile(a, b_scaled, na, nb):
    q = mm(a, b_scaled, NT) + (jnp.concatenate([na, na], axis=1) + nb)
    q = jnp.maximum(q, 1e-30)
    u = jnp.maximum(SCALE - q * lax.rsqrt(q), 0.0)
    t = u * u
    return (t * t * (CUT - u)).astype(BF16)


def split(v):
    hi = v.astype(BF16)
    lo = (v - hi.astype(F32)).astype(BF16)
    return jnp.concatenate([hi, lo], axis=0)


def rhs_ones(rows, one):
    v = rows.astype(F32)
    return jnp.concatenate([v[:, 0:TILE], v[:, TILE:], jnp.full((16, TILE), one, F32)], axis=0).astype(BF16)


def fold(acc):
    return (acc[0:8] + acc[8:16]) * C4


def fold_ones(acc):
    return jnp.concatenate([acc[0:8] + acc[8:16], acc[16:24]], axis=0) * C4


def span(t):
    return pl.ds(pl.multiple_of(t * TILE, TILE), TILE)


def params(mib=12):
    return pltpu.CompilerParams(vmem_limit_bytes=mib * 1024 * 1024)


def f32(*shape):
    return jax.ShapeDtypeStruct(shape, F32)


def vmem_bf16(*shape):
    return pltpu.VMEM(shape, BF16)


def prep(partners, points, targets):
    n, d = points.shape
    nt = n // TILE

    def body(p_hbm, pts_ref, r_hbm, table_ref, msg_ref, *refs):
        outs, (r_ref, p_ref, sems) = refs[:-3], refs[-3:]
        g = lax.axis_index("group")
        dev = lax.axis_index("dev")
        copies = [pltpu.make_async_copy(r_hbm, r_ref, sems.at[nt])]
        for t in range(nt):
            s = slice(t * TILE, (t + 1) * TILE)
            copies.append(pltpu.make_async_copy(pts_ref.at[s, :], msg_ref.at[t, pl.ds(0, TILE), :], sems.at[t]))
        table_copy = pltpu.make_async_copy(p_hbm, p_ref, sems.at[nt + 1])
        table_copy.start()
        for cp in copies:
            cp.start()
        table_copy.wait()
        for h in range(8):
            for c in range(2):
                table_ref[h * 2 + c] = p_ref[h, g, c, dev]
                table_ref[16 + h * 2 + c] = p_ref[g, h, c, dev]
        for cp in copies:
            cp.wait()
        for t in range(nt):
            s = slice(t * TILE, (t + 1) * TILE)
            v = r_ref[:, s]
            hi = v.astype(BF16).astype(F32)
            msg_ref[t, TILE:, :] = jnp.concatenate([hi, v - hi], axis=1).astype(BF16)
        for k, out in zip(SWAPS, outs):
            for c in range(2):
                out[c] = msg_ref[jnp.maximum(p_ref[g ^ k, g, c, dev], 0)]

    return pl.pallas_call(
        body,
        out_shape=[jax.ShapeDtypeStruct((32,), jnp.int32), vmem_bf16(nt, TILE + EXTRA, d)]
        + [vmem_bf16(2, TILE + EXTRA, d) for _ in SWAPS],
        in_specs=[HBM, HBM, HBM],
        out_specs=[SMEM] + [VM] * (1 + len(SWAPS)),
        scratch_shapes=[
            pltpu.VMEM((8, n), F32),
            pltpu.SMEM(partners.shape, jnp.int32),
            pltpu.SemaphoreType.DMA((nt + 2,)),
        ],
        compiler_params=params(),
        name="prep",
    )(*(pltpu.with_memory_space_constraint(x, pltpu.HBM) for x in (partners, points, targets)))


def gate(held, arrived):
    m = len(held)

    def body(*refs):
        pass

    return pl.pallas_call(
        body,
        out_shape=[vmem_bf16(*x.shape) for x in held],
        in_specs=[VM] * m + [ANY] * len(arrived),
        out_specs=[VM] * m,
        input_output_aliases={i: i for i in range(m)},
        compiler_params=params(4),
        name="gate",
    )(*held, *arrived)


def local_first(own):
    nt, _, _ = own.shape
    n = nt * TILE

    def body(a_ref, k_ref, acc_ref, na, nb, va):
        for i in range(nt):
            s = slice(i * TILE, (i + 1) * TILE)
            x = col_norms(a_ref[i, 0:TILE, :])
            na[s, :] = x
            nb[:, s] = x.T[0:8]
            va[:, s] = rhs_ones(a_ref[i, TILE:, :], 1.0)

        def step(t, carry):
            s = span(t)
            b = a_ref[t, 0:TILE, :] * jnp.asarray(-2.0, BF16)
            for i in range(nt):
                c = slice(i * TILE, (i + 1) * TILE)
                k_ref[t, c, :] = kernel_tile(a_ref[i, 0:TILE, :], b, na[c, :], nb[0:1, s])
            acc_ref[:, s] = fold_ones(mm(va[...], k_ref[t], NN))
            return carry

        lax.fori_loop(0, nt, step, 0, unroll=2)

    return pl.pallas_call(
        body,
        out_shape=(vmem_bf16(nt, n, TILE), f32(16, n)),
        in_specs=[VM],
        out_specs=(VM, VM),
        scratch_shapes=[pltpu.VMEM((n, 128), F32), pltpu.VMEM((8, n), F32), pltpu.VMEM((32, n), BF16)],
        compiler_params=params(),
        name="local_first",
    )(own)


def band_first(left, own, right, after):
    nt, _, _ = own.shape
    n = nt * TILE
    m = len(after)

    def body(l_ref, a_ref, b_ref, *refs):
        k_ref, col_ref, rowl_ref, rowo_ref, na, nb, va, vb, acc = refs[m:]
        v = lax.axis_index("dev")
        has_left = (v > 0).astype(F32)
        has_right = (v < lax.axis_size("dev") - 1).astype(F32)
        for i in range(nt):
            s = slice(i * TILE, (i + 1) * TILE)
            e = slice(n + i * TILE, n + (i + 1) * TILE)
            na[s, :] = col_norms(l_ref[i, 0:TILE, :])
            na[e, :] = col_norms(a_ref[i, 0:TILE, :])
            nb[:, s] = col_norms(b_ref[i, 0:TILE, :]).T[0:8]
            va[:, s] = rhs_ones(l_ref[i, TILE:, :], has_left)
            va[:, e] = rhs_ones(a_ref[i, TILE:, :], 1.0)
            vb[:, s] = rhs_ones(b_ref[i, TILE:, :], has_right)
        acc[...] = jnp.zeros_like(acc)

        def step(t, carry):
            s = span(t)
            b = b_ref[t, 0:TILE, :] * jnp.asarray(-2.0, BF16)
            for j, x in enumerate((l_ref, a_ref)):
                for i in range(nt):
                    e = slice((j * nt + i) * TILE, (j * nt + i + 1) * TILE)
                    k_ref[t, e, :] = kernel_tile(x[i, 0:TILE, :], b, na[e, :], nb[0:1, s])
            k = k_ref[t]
            col_ref[:, s] = fold_ones(mm(va[...], k, NN))
            acc[...] += mm(vb[:, s], k, NT)
            return carry

        lax.fori_loop(0, nt, step, 0, unroll=2)
        rows = fold_ones(acc[...])
        rowl_ref[...] = rows[:, 0:n]
        rowo_ref[...] = rows[:, n:]

    return pl.pallas_call(
        body,
        out_shape=(vmem_bf16(nt, 2 * n, TILE), f32(16, n), f32(16, n), f32(16, n)),
        in_specs=[VM] * 3 + [ANY] * m,
        out_specs=(VM,) * 4,
        scratch_shapes=[
            pltpu.VMEM((2 * n, 128), F32),
            pltpu.VMEM((8, n), F32),
            pltpu.VMEM((32, 2 * n), BF16),
            pltpu.VMEM((32, n), BF16),
            pltpu.VMEM((32, 2 * n), F32),
        ],
        compiler_params=params(),
        name="band_first",
    )(left, own, right, *after)


def cross_first(ks, table, own, tiles, after):
    nt, _, d = own.shape
    n = nt * TILE
    m = len(ks)
    slots = 2 * m

    def body(q_ref, a_ref, _, *refs):
        tile_refs = refs[:m]
        k_ref, row_ref, *cols = refs[m : 2 * m + 2]
        buf, jobs, sems, na, va, acc, nb, col = refs[2 * m + 2 :]
        g = lax.axis_index("group")
        count = jnp.int32(0)
        for i, k in enumerate(ks):
            for c in range(2):
                live = q_ref[16 + (g ^ k) * 2 + c] >= 0

                @pl.when(live)
                def _(count=count, i=i, k=k, c=c):
                    pltpu.make_async_copy(tile_refs[i].at[c], buf.at[count], sems.at[count]).start()
                    jobs[count] = 2 * i + c

                count = count + live.astype(jnp.int32)
        for i in range(nt):
            s = slice(i * TILE, (i + 1) * TILE)
            na[s, :] = col_norms(a_ref[i, 0:TILE, :])
            va[:, s] = rhs_ones(a_ref[i, TILE:, :], 1.0)
        acc[...] = jnp.zeros_like(acc)

        def arrive(j, carry):
            pltpu.make_async_copy(tile_refs[0].at[0], buf.at[j], sems.at[j]).wait()
            return carry

        lax.fori_loop(0, count, arrive, 0)

        def step(pair, carry):
            for u in range(2):
                j = jnp.minimum(2 * pair + u, count - 1)
                live = (2 * pair + u < count).astype(F32)
                b = buf[j, 0:TILE, :]
                nb[u] = col_norms(b).T[0:8]
                b = b * jnp.asarray(-2.0, BF16)
                vb = rhs_ones(buf[j, TILE:, :].astype(F32) * live, live)
                for i in range(nt):
                    c = slice(i * TILE, (i + 1) * TILE)
                    k_ref[j, c, :] = kernel_tile(a_ref[i, 0:TILE, :], b, na[c, :], nb[u, 0:1, :])
                k = k_ref[j]
                col[jobs[j]] = fold_ones(mm(va[...], k, NN))
                acc[...] += mm(vb, k, NT)
            return carry

        lax.fori_loop(0, (count + 1) // 2, step, 0)
        row_ref[...] = fold_ones(acc[...])
        for i, out in enumerate(cols):
            out[...] = col[2 * i : 2 * i + 2]

    return pl.pallas_call(
        body,
        out_shape=[vmem_bf16(slots, n, TILE), f32(16, n)] + [f32(2, 16, TILE)] * m,
        in_specs=[SMEM, VM, ANY] + [ANY] * m,
        out_specs=[VM] * (2 + m),
        scratch_shapes=[
            pltpu.VMEM((slots, TILE + EXTRA, d), BF16),
            pltpu.SMEM((slots,), jnp.int32),
            pltpu.SemaphoreType.DMA((slots,)),
            pltpu.VMEM((n, 128), F32),
            pltpu.VMEM((32, n), BF16),
            pltpu.VMEM((32, n), F32),
            pltpu.VMEM((2, 8, TILE), F32),
            pltpu.VMEM((slots, 16, TILE), F32),
        ],
        compiler_params=params(),
    )(table, own, after, *tiles)


def combine(table, r, parts, ret):
    n = r.shape[1]
    m = len(parts)

    def body(q_ref, r_ref, *refs):
        part_refs, (*x_refs, w_ref, deg_ref, sum_ref, acc) = refs[:m], refs[m:]
        x_refs, (own_ref, relay_ref) = x_refs[:7], x_refs[7:]
        g = lax.axis_index("group")
        total = part_refs[0][...]
        for p in part_refs[1:]:
            total = total + p[...]
        acc[...] = total
        for k, x in zip(SWAPS, x_refs):
            for c in range(2):
                t = q_ref[(g ^ k) * 2 + c]

                @pl.when(t >= 0)
                def _(x=x, c=c, t=t):
                    acc[:, span(t)] = acc[:, span(t)] + x[c]

        rv = r_ref[...]
        deg = acc[8:16, :]
        w = 0.5 * (deg * rv - acc[0:8, :])
        w_ref[...] = w
        deg_ref[...] = deg
        for j in range(4):
            for out, k in ((own_ref, 2 * j), (relay_ref, 2 * j + 1)):
                for c in range(2):
                    t = jnp.maximum(q_ref[(g ^ k) * 2 + c], 0)
                    out[j, c * 8 : c * 8 + 8, :] = w_ref[:, span(t)]
        lane = lax.broadcasted_iota(jnp.int32, (8, 128), 1)
        sums = jnp.zeros((8, 128), F32)
        for k, v in enumerate((rv * rv, rv * w, w * w, 0.5 * deg * w * w)):
            sums = jnp.where(lane == k, jnp.sum(v, axis=1, keepdims=True), sums)
        sum_ref[...] = sums

    return pl.pallas_call(
        body,
        out_shape=[f32(4, 16, TILE), f32(4, 16, TILE), f32(8, n), f32(8, n), f32(8, 128)],
        in_specs=[SMEM] + [VM] * (m + 8),
        out_specs=[VM] * 5,
        scratch_shapes=[pltpu.VMEM((16, n), F32)],
        compiler_params=params(),
        name="combine",
    )(table, r, *parts, *ret)


def relay(own, partner):
    def body(own_ref, partner_ref, *outs):
        for j, out in enumerate(outs):
            out[0] = own_ref[j + 1]
            out[1] = partner_ref[j + 1]

    return pl.pallas_call(
        body,
        out_shape=[f32(2, 16, TILE)] * 3,
        in_specs=[VM, VM],
        out_specs=[VM] * 3,
        compiler_params=params(4),
        name="relay",
    )(own, partner)


def local_second(k_local, w):
    nt, n, _ = k_local.shape

    def body(k_ref, w_ref, out_ref):
        va = split(w_ref[...])
        for t in range(nt):
            out_ref[:, t * TILE : (t + 1) * TILE] = fold(mm(va, k_ref[t], NN))

    return pl.pallas_call(
        body,
        out_shape=f32(8, n),
        in_specs=[VM, VM],
        out_specs=VM,
        compiler_params=params(),
        name="local_second",
    )(k_local, w)


def band_second(k_band, w_left, w, w_right, after):
    nt, n2, _ = k_band.shape
    n = n2 // 2

    def body(k_ref, wl_ref, w_ref, wb_ref, _, col_ref, rowl_ref, rowo_ref, va, acc):
        va[:, 0:n] = split(wl_ref[...])
        va[:, n:] = split(w_ref[...])
        vb = split(wb_ref[...])
        for t in range(nt):
            s = slice(t * TILE, (t + 1) * TILE)
            col_ref[:, s] = fold(mm(va[...], k_ref[t], NN))
            new = mm(vb[:, s], k_ref[t], NT)
            acc[...] = new if t == 0 else acc[...] + new
        rows = fold(acc[...])
        rowl_ref[...] = rows[:, 0:n]
        rowo_ref[...] = rows[:, n:]

    return pl.pallas_call(
        body,
        out_shape=(f32(8, n), f32(8, n), f32(8, n)),
        in_specs=[VM] * 4 + [ANY],
        out_specs=(VM,) * 3,
        scratch_shapes=[pltpu.VMEM((16, n2), BF16), pltpu.VMEM((16, n2), F32)],
        compiler_params=params(),
        name="band_second",
    )(k_band, w_left, w, w_right, after)


def cross_second(table, k_caches, w, xw, sums, loc, row_left, row_own, w_left):
    n = w.shape[1]

    def body(
        q_ref, ka_ref, kb_ref, kc_ref, w_ref, sum_ref, loc_ref, rl_ref, ro_ref, wl_ref, *refs
    ):
        near_ref, *chip_refs, col_ref, row_ref, va, acc, jobs, xw_ref = refs
        g = lax.axis_index("group")
        xw_ref[g ^ 1] = near_ref[0]
        for j, x in enumerate(chip_refs):
            for i in range(2):
                xw_ref[g ^ (2 * j + 2 + i)] = x[i]
        va[...] = split(w_ref[...])
        acc[...] = jnp.zeros_like(acc)
        for ks, k_ref in zip(STAGES, (ka_ref, kb_ref, kc_ref)):
            count = jnp.int32(0)
            for k in ks:
                for c in range(2):
                    live = q_ref[16 + (g ^ k) * 2 + c] >= 0

                    @pl.when(live)
                    def _(count=count, k=k, c=c):
                        jobs[count] = (g ^ k) * 2 + c

                    count = count + live.astype(jnp.int32)

            def step(pair, carry, k_ref=k_ref, count=count):
                for u in range(2):
                    j = jnp.minimum(2 * pair + u, count - 1)
                    live = (2 * pair + u < count).astype(F32)
                    slot = jobs[j]
                    h, c = slot >> 1, slot & 1
                    rows = pl.ds(pl.multiple_of(c * 8, 8), 8)
                    k = k_ref[j]
                    col_ref[h, rows, :] = fold(mm(va[...], k, NN))
                    acc[...] += mm(split(xw_ref[h, rows, :] * live), k, NT)
                return carry

            lax.fori_loop(0, (count + 1) // 2, step, 0)
        row = fold(acc[...])
        row_ref[...] = row
        pairs = w_ref[...] * (0.5 * loc_ref[...] + ro_ref[...] + row) + wl_ref[...] * rl_ref[...]
        lane = lax.broadcasted_iota(jnp.int32, (8, 128), 1)
        pay = jnp.where(lane == 3, sum_ref[...] - jnp.sum(pairs, axis=1, keepdims=True), sum_ref[...])
        for h in range(8):
            col_ref[h, 16:24, 0:128] = pay
            col_ref[h, 16:24, 128:] = jnp.zeros((8, 128), F32)

    return pl.pallas_call(
        body,
        out_shape=(f32(8, 24, TILE), f32(8, n)),
        in_specs=[SMEM] + [VM] * 13,
        out_specs=(VM, VM),
        scratch_shapes=[
            pltpu.VMEM((16, n), BF16),
            pltpu.VMEM((16, n), F32),
            pltpu.SMEM((16,), jnp.int32),
            pltpu.VMEM((8, 16, TILE), F32),
        ],
        compiler_params=params(),
        name="cross_second",
    )(table, *k_caches, w, sums, loc, row_left, row_own, w_left, *xw)


def group_sum(table, w, deg, parts, ret):
    n = w.shape[1]
    m = len(parts)

    def body(q_ref, w_ref, deg_ref, *refs):
        part_refs, (x_ref, w2_ref, out_ref, acc) = refs[:m], refs[m:]
        total = part_refs[0][...]
        for p in part_refs[1:]:
            total = total + p[...]
        acc[...] = total
        for h in range(8):
            for c in range(2):
                t = q_ref[h * 2 + c]

                @pl.when(t >= 0)
                def _(h=h, c=c, t=t):
                    acc[:, span(t)] = acc[:, span(t)] + x_ref[h, c * 8 : c * 8 + 8, :]

        w2_ref[...] = 0.5 * (deg_ref[...] * w_ref[...] - acc[...])
        sums = x_ref[0, 16:24, 0:128]
        for h in range(1, 8):
            sums = sums + x_ref[h, 16:24, 0:128]
        for v in range(16):
            out_ref[v] = sums

    return pl.pallas_call(
        body,
        out_shape=(f32(8, n), f32(16, 8, 128)),
        in_specs=[SMEM] + [VM] * (3 + m),
        out_specs=(VM, VM),
        scratch_shapes=[pltpu.VMEM((8, n), F32)],
        compiler_params=params(),
        name="group_sum",
    )(table, w, deg, *parts, ret)


def finish(gathered, r, w, w2):
    n = r.shape[1]

    def body(g_ref, r_ref, w_ref, w2_ref, sol_ref, res_ref):
        sums = g_ref[0]
        for v in range(1, 16):
            sums = sums + g_ref[v]
        rho, mu, nu, xi = (sums[:, k : k + 1] for k in range(4))
        rv = r_ref[...]
        wv = w_ref[...]
        first = rho / (rho + mu)
        gap = (nu - mu * (mu / rho)) * (first * first)
        beta = gap / rho
        cr = mu / (rho + mu) + beta
        curvature = cr * cr * (rho + mu) - 2.0 * cr * first * (mu + nu) + first * first * (nu + xi)
        second = gap / curvature
        sol_ref[...] = (first + second * cr) * rv - (second * first) * wv
        res_ref[...] = (
            (mu / (rho + mu) - second * cr) * rv
            + (second * (first - cr) - first) * wv
            + (second * first) * w2_ref[...]
        )

    return pl.pallas_call(
        body,
        out_shape=(f32(8, n), f32(8, n)),
        in_specs=[VM] * 4,
        out_specs=(VM, VM),
        compiler_params=params(),
        name="finish",
    )(gathered, r, w, w2)


def on_device(points, targets, partner_tiles):
    dev_count = lax.axis_size("dev")
    to_right = [(i, i + 1) for i in range(dev_count - 1)]
    to_left = [(i + 1, i) for i in range(dev_count - 1)]

    def right_of(x):
        return lax.ppermute(x, "dev", to_left)

    def left_of(x):
        return lax.ppermute(x, "dev", to_right)

    def swap(x, k):
        return lax.ppermute(x, "group", [(i, i ^ k) for i in range(8)])

    def trade(x, axis="group"):
        return lax.all_to_all(x, axis, split_axis=0, concat_axis=0, tiled=True)

    table, own, *outgoing = prep(jnp.transpose(partner_tiles, (0, 2, 3, 1)), points, targets)
    arrived = {}
    for x, k in zip(outgoing, SWAPS[:5]):
        arrived[k] = swap(x, k)
    left = left_of(own)
    right = right_of(own)
    k_local, acc_local = local_first(own)

    def cross(stage, after):
        return cross_first(stage, table, own, [arrived[k] for k in stage], after)

    ret = {}

    def give_back(cols, stage):
        for x, k in zip(cols, stage):
            ret[k] = swap(x, k)

    k_a, row_a, *col_a = cross(STAGES[0], acc_local)
    give_back(col_a, STAGES[0])
    for x, k in zip(gate(outgoing[5:], [row_a, arrived[3], arrived[7]]), STAGES[2]):
        arrived[k] = swap(x, k)
    k_b, row_b, *col_b = cross(STAGES[1], row_a)
    give_back(col_b, STAGES[1])
    k_band, to_r, to_l, acc_band = band_first(left, own, right, [row_b])
    from_left, from_right = left_of(to_r), right_of(to_l)
    k_c, row_c, *col_c = cross(STAGES[2], acc_band)
    give_back(col_c, STAGES[2])
    w_own, w_relay, w, deg, sums = combine(
        table, targets, (acc_local, acc_band, from_left, from_right, row_a, row_b, row_c), [ret[k] for k in SWAPS]
    )
    w_left = left_of(w)
    w_right = right_of(w)
    partner = swap(w_relay, 1)
    xw = [partner] + [swap(x, 2 * j + 2) for j, x in enumerate(relay(w_own, partner))]
    loc2 = local_second(k_local, w)
    col_r, rowl_b, rowo_b = band_second(k_band, w_left, w, w_right, loc2)
    from_left2 = left_of(col_r)
    from_right2 = right_of(rowl_b)
    col_x, row_x = cross_second(table, (k_a, k_b, k_c), w, xw, sums, loc2, rowl_b, rowo_b, w_left)
    w2, column = group_sum(table, w, deg, (loc2, rowo_b, row_x, from_left2, from_right2), trade(col_x))
    return finish(trade(column, "dev"), targets, w, w2)


def solution(mesh):
    return jax.shard_map(
        on_device,
        mesh=mesh,
        in_specs=(P(("group", "dev"), None), P(None, ("group", "dev")), P()),
        out_specs=(P(None, ("group", "dev")), P(None, ("group", "dev"))),
        check_vma=False,
    )
```

```python
import jax
import jax.numpy as jnp
from jax import lax
from jax.experimental import pallas as pl
from jax.experimental.pallas import tpu as pltpu
from jax.sharding import PartitionSpec as P


TILE = 256
EXTRA = 8
SCALE = 3.9
C4 = 4.0 / SCALE**5
CUT = 5.0 * SCALE / 4.0
NT = (((1,), (1,)), ((), ()))
NN = (((1,), (0,)), ((), ()))
F32 = jnp.float32
BF16 = jnp.bfloat16
STAGES = ((2, 6, 1), (3, 7), (4, 5))
SWAPS = STAGES[0] + STAGES[1] + STAGES[2]

SMEM = pl.BlockSpec(memory_space=pltpu.SMEM)
ANY = pl.BlockSpec(memory_space=pl.ANY)
HBM = pl.BlockSpec(memory_space=pltpu.HBM)
VM = pl.BlockSpec(memory_space=pltpu.VMEM)


def mm(a, b, dims):
    return lax.dot_general(a, b, dims, preferred_element_type=F32)


def col_norms(x):
    x = x.astype(F32)
    return jnp.broadcast_to(jnp.sum(x * x, axis=1, keepdims=True), (x.shape[0], 128))


def kernel_tile(a, b_scaled, na, nb):
    q = mm(a, b_scaled, NT) + (jnp.concatenate([na, na], axis=1) + nb)
    q = jnp.maximum(q, 1e-30)
    u = jnp.maximum(SCALE - q * lax.rsqrt(q), 0.0)
    t = u * u
    return (t * t * (CUT - u)).astype(BF16)


def split(v):
    hi = v.astype(BF16)
    lo = (v - hi.astype(F32)).astype(BF16)
    return jnp.concatenate([hi, lo], axis=0)


def rhs_ones(rows, one):
    v = rows.astype(F32)
    return jnp.concatenate([v[:, 0:TILE], v[:, TILE:], jnp.full((16, TILE), one, F32)], axis=0).astype(BF16)


def fold(acc):
    return (acc[0:8] + acc[8:16]) * C4


def fold_ones(acc):
    return jnp.concatenate([acc[0:8] + acc[8:16], acc[16:24]], axis=0) * C4


def span(t):
    return pl.ds(pl.multiple_of(t * TILE, TILE), TILE)


def params(mib=12):
    return pltpu.CompilerParams(vmem_limit_bytes=mib * 1024 * 1024)


def f32(*shape):
    return jax.ShapeDtypeStruct(shape, F32)


def vmem_bf16(*shape):
    return pltpu.VMEM(shape, BF16)


def prep(partners, points, targets):
    n, d = points.shape
    nt = n // TILE

    def body(p_hbm, pts_ref, r_hbm, table_ref, msg_ref, *refs):
        outs, (r_ref, p_ref, sems) = refs[:-3], refs[-3:]
        g = lax.axis_index("group")
        dev = lax.axis_index("dev")
        copies = [pltpu.make_async_copy(r_hbm, r_ref, sems.at[nt])]
        for t in range(nt):
            s = slice(t * TILE, (t + 1) * TILE)
            copies.append(pltpu.make_async_copy(pts_ref.at[s, :], msg_ref.at[t, pl.ds(0, TILE), :], sems.at[t]))
        table_copy = pltpu.make_async_copy(p_hbm, p_ref, sems.at[nt + 1])
        table_copy.start()
        for cp in copies:
            cp.start()
        table_copy.wait()
        for h in range(8):
            for c in range(2):
                table_ref[h * 2 + c] = p_ref[h, g, c, dev]
                table_ref[16 + h * 2 + c] = p_ref[g, h, c, dev]
        for cp in copies:
            cp.wait()
        for t in range(nt):
            s = slice(t * TILE, (t + 1) * TILE)
            v = r_ref[:, s]
            hi = v.astype(BF16).astype(F32)
            msg_ref[t, TILE:, :] = jnp.concatenate([hi, v - hi], axis=1).astype(BF16)
        for k, out in zip(SWAPS, outs):
            for c in range(2):
                out[c] = msg_ref[jnp.maximum(p_ref[g ^ k, g, c, dev], 0)]

    return pl.pallas_call(
        body,
        out_shape=[jax.ShapeDtypeStruct((32,), jnp.int32), vmem_bf16(nt, TILE + EXTRA, d)]
        + [vmem_bf16(2, TILE + EXTRA, d) for _ in SWAPS],
        in_specs=[HBM, HBM, HBM],
        out_specs=[SMEM] + [VM] * (1 + len(SWAPS)),
        scratch_shapes=[
            pltpu.VMEM((8, n), F32),
            pltpu.SMEM(partners.shape, jnp.int32),
            pltpu.SemaphoreType.DMA((nt + 2,)),
        ],
        compiler_params=params(),
        name="prep",
    )(*(pltpu.with_memory_space_constraint(x, pltpu.HBM) for x in (partners, points, targets)))


def gate(held, arrived):
    m = len(held)

    def body(*refs):
        pass

    return pl.pallas_call(
        body,
        out_shape=[vmem_bf16(*x.shape) for x in held],
        in_specs=[VM] * m + [ANY] * len(arrived),
        out_specs=[VM] * m,
        input_output_aliases={i: i for i in range(m)},
        compiler_params=params(4),
        name="gate",
    )(*held, *arrived)


def local_first(own):
    nt, _, _ = own.shape
    n = nt * TILE

    def body(a_ref, k_ref, acc_ref, na, nb, va):
        for i in range(nt):
            s = slice(i * TILE, (i + 1) * TILE)
            x = col_norms(a_ref[i, 0:TILE, :])
            na[s, :] = x
            nb[:, s] = x.T[0:8]
            va[:, s] = rhs_ones(a_ref[i, TILE:, :], 1.0)

        def step(t, carry):
            s = span(t)
            b = a_ref[t, 0:TILE, :] * jnp.asarray(-2.0, BF16)
            for i in range(nt):
                c = slice(i * TILE, (i + 1) * TILE)
                k_ref[t, c, :] = kernel_tile(a_ref[i, 0:TILE, :], b, na[c, :], nb[0:1, s])
            acc_ref[:, s] = fold_ones(mm(va[...], k_ref[t], NN))
            return carry

        lax.fori_loop(0, nt, step, 0, unroll=2)

    return pl.pallas_call(
        body,
        out_shape=(vmem_bf16(nt, n, TILE), f32(16, n)),
        in_specs=[VM],
        out_specs=(VM, VM),
        scratch_shapes=[pltpu.VMEM((n, 128), F32), pltpu.VMEM((8, n), F32), pltpu.VMEM((32, n), BF16)],
        compiler_params=params(),
        name="local_first",
    )(own)


def band_first(rows, right, after, left_side):
    nt, _, _ = rows.shape
    n = nt * TILE

    def body(a_ref, b_ref, before_ref, k_ref, col_ref, row_ref, na, nb, va, vb, acc):
        v = lax.axis_index("dev")
        has_rows = (v > 0).astype(F32) if left_side else 1.0
        has_right = (v < lax.axis_size("dev") - 1).astype(F32)
        for i in range(nt):
            s = slice(i * TILE, (i + 1) * TILE)
            na[s, :] = col_norms(a_ref[i, 0:TILE, :])
            nb[:, s] = col_norms(b_ref[i, 0:TILE, :]).T[0:8]
            va[:, s] = rhs_ones(a_ref[i, TILE:, :], has_rows)
            vb[:, s] = rhs_ones(b_ref[i, TILE:, :], has_right)
        acc[...] = jnp.zeros_like(acc)

        def step(t, carry):
            s = span(t)
            b = b_ref[t, 0:TILE, :] * jnp.asarray(-2.0, BF16)
            for i in range(nt):
                c = slice(i * TILE, (i + 1) * TILE)
                k_ref[t, c, :] = kernel_tile(a_ref[i, 0:TILE, :], b, na[c, :], nb[0:1, s])
            k = k_ref[t]
            col = fold_ones(mm(va[...], k, NN))
            col_ref[:, s] = before_ref[:, s] + col if left_side else col
            acc[...] += mm(vb[:, s], k, NT)
            return carry

        lax.fori_loop(0, nt, step, 0, unroll=2)
        row_ref[...] = fold_ones(acc[...])

    return pl.pallas_call(
        body,
        out_shape=(vmem_bf16(nt, n, TILE), f32(16, n), f32(16, n)),
        in_specs=[VM, VM, VM if left_side else ANY],
        out_specs=(VM,) * 3,
        scratch_shapes=[
            pltpu.VMEM((n, 128), F32),
            pltpu.VMEM((8, n), F32),
            pltpu.VMEM((32, n), BF16),
            pltpu.VMEM((32, n), BF16),
            pltpu.VMEM((32, n), F32),
        ],
        compiler_params=params(),
        name="band_left" if left_side else "band_own",
    )(rows, right, after)


def cross_first(ks, table, own, tiles, after):
    nt, _, d = own.shape
    n = nt * TILE
    m = len(ks)
    slots = 2 * m

    def body(q_ref, a_ref, _, *refs):
        tile_refs = refs[:m]
        k_ref, row_ref, *cols = refs[m : 2 * m + 2]
        buf, jobs, sems, na, va, acc, nb, col = refs[2 * m + 2 :]
        g = lax.axis_index("group")
        count = jnp.int32(0)
        for i, k in enumerate(ks):
            for c in range(2):
                live = q_ref[16 + (g ^ k) * 2 + c] >= 0

                @pl.when(live)
                def _(count=count, i=i, k=k, c=c):
                    pltpu.make_async_copy(tile_refs[i].at[c], buf.at[count], sems.at[count]).start()
                    jobs[count] = 2 * i + c

                count = count + live.astype(jnp.int32)
        for i in range(nt):
            s = slice(i * TILE, (i + 1) * TILE)
            na[s, :] = col_norms(a_ref[i, 0:TILE, :])
            va[:, s] = rhs_ones(a_ref[i, TILE:, :], 1.0)
        acc[...] = jnp.zeros_like(acc)

        def arrive(j, carry):
            pltpu.make_async_copy(tile_refs[0].at[0], buf.at[j], sems.at[j]).wait()
            return carry

        lax.fori_loop(0, count, arrive, 0)

        def step(pair, carry):
            for u in range(2):
                j = jnp.minimum(2 * pair + u, count - 1)
                live = (2 * pair + u < count).astype(F32)
                b = buf[j, 0:TILE, :]
                nb[u] = col_norms(b).T[0:8]
                b = b * jnp.asarray(-2.0, BF16)
                vb = rhs_ones(buf[j, TILE:, :].astype(F32) * live, live)
                for i in range(nt):
                    c = slice(i * TILE, (i + 1) * TILE)
                    k_ref[j, c, :] = kernel_tile(a_ref[i, 0:TILE, :], b, na[c, :], nb[u, 0:1, :])
                k = k_ref[j]
                col[jobs[j]] = fold_ones(mm(va[...], k, NN))
                acc[...] += mm(vb, k, NT)
            return carry

        lax.fori_loop(0, (count + 1) // 2, step, 0)
        row_ref[...] = fold_ones(acc[...])
        for i, out in enumerate(cols):
            out[...] = col[2 * i : 2 * i + 2]

    return pl.pallas_call(
        body,
        out_shape=[vmem_bf16(slots, n, TILE), f32(16, n)] + [f32(2, 16, TILE)] * m,
        in_specs=[SMEM, VM, ANY] + [ANY] * m,
        out_specs=[VM] * (2 + m),
        scratch_shapes=[
            pltpu.VMEM((slots, TILE + EXTRA, d), BF16),
            pltpu.SMEM((slots,), jnp.int32),
            pltpu.SemaphoreType.DMA((slots,)),
            pltpu.VMEM((n, 128), F32),
            pltpu.VMEM((32, n), BF16),
            pltpu.VMEM((32, n), F32),
            pltpu.VMEM((2, 8, TILE), F32),
            pltpu.VMEM((slots, 16, TILE), F32),
        ],
        compiler_params=params(),
    )(table, own, after, *tiles)


def combine(table, r, parts, ret):
    n = r.shape[1]
    m = len(parts)

    def body(q_ref, r_ref, *refs):
        part_refs, (*x_refs, w_ref, deg_ref, sum_ref, acc) = refs[:m], refs[m:]
        x_refs, (own_ref, relay_ref) = x_refs[:7], x_refs[7:]
        g = lax.axis_index("group")
        total = part_refs[0][...]
        for p in part_refs[1:]:
            total = total + p[...]
        acc[...] = total
        for k, x in zip(SWAPS, x_refs):
            for c in range(2):
                t = q_ref[(g ^ k) * 2 + c]

                @pl.when(t >= 0)
                def _(x=x, c=c, t=t):
                    acc[:, span(t)] = acc[:, span(t)] + x[c]

        rv = r_ref[...]
        deg = acc[8:16, :]
        w = 0.5 * (deg * rv - acc[0:8, :])
        w_ref[...] = w
        deg_ref[...] = deg
        for j in range(4):
            for out, k in ((own_ref, 2 * j), (relay_ref, 2 * j + 1)):
                for c in range(2):
                    t = jnp.maximum(q_ref[(g ^ k) * 2 + c], 0)
                    out[j, c * 8 : c * 8 + 8, :] = w_ref[:, span(t)]
        lane = lax.broadcasted_iota(jnp.int32, (8, 128), 1)
        sums = jnp.zeros((8, 128), F32)
        for k, v in enumerate((rv * rv, rv * w, w * w, 0.5 * deg * w * w)):
            sums = jnp.where(lane == k, jnp.sum(v, axis=1, keepdims=True), sums)
        sum_ref[...] = sums

    return pl.pallas_call(
        body,
        out_shape=[f32(4, 16, TILE), f32(4, 16, TILE), f32(8, n), f32(8, n), f32(8, 128)],
        in_specs=[SMEM] + [VM] * (m + 8),
        out_specs=[VM] * 5,
        scratch_shapes=[pltpu.VMEM((16, n), F32)],
        compiler_params=params(),
        name="combine",
    )(table, r, *parts, *ret)


def relay(own, partner):
    def body(own_ref, partner_ref, *outs):
        for j, out in enumerate(outs):
            out[0] = own_ref[j + 1]
            out[1] = partner_ref[j + 1]

    return pl.pallas_call(
        body,
        out_shape=[f32(2, 16, TILE)] * 3,
        in_specs=[VM, VM],
        out_specs=[VM] * 3,
        compiler_params=params(4),
        name="relay",
    )(own, partner)


def local_second(k_local, w):
    nt, n, _ = k_local.shape

    def body(k_ref, w_ref, out_ref):
        va = split(w_ref[...])
        for t in range(nt):
            out_ref[:, t * TILE : (t + 1) * TILE] = fold(mm(va, k_ref[t], NN))

    return pl.pallas_call(
        body,
        out_shape=f32(8, n),
        in_specs=[VM, VM],
        out_specs=VM,
        compiler_params=params(),
        name="local_second",
    )(k_local, w)


def band_second(k_left, k_own, w_left, w, w_right, after):
    nt, n, _ = k_own.shape

    def body(kl_ref, ko_ref, wl_ref, w_ref, wb_ref, _, col_ref, rowl_ref, rowo_ref, acc_l, acc_o):
        va_l = split(wl_ref[...])
        va_o = split(w_ref[...])
        vb = split(wb_ref[...])
        for t in range(nt):
            s = slice(t * TILE, (t + 1) * TILE)
            col_ref[:, s] = fold(mm(va_l, kl_ref[t], NN) + mm(va_o, ko_ref[t], NN))
            for acc, k_ref in ((acc_l, kl_ref), (acc_o, ko_ref)):
                new = mm(vb[:, s], k_ref[t], NT)
                acc[...] = new if t == 0 else acc[...] + new
        rowl_ref[...] = fold(acc_l[...])
        rowo_ref[...] = fold(acc_o[...])

    return pl.pallas_call(
        body,
        out_shape=(f32(8, n), f32(8, n), f32(8, n)),
        in_specs=[VM] * 5 + [ANY],
        out_specs=(VM,) * 3,
        scratch_shapes=[pltpu.VMEM((16, n), F32), pltpu.VMEM((16, n), F32)],
        compiler_params=params(),
        name="band_second",
    )(k_left, k_own, w_left, w, w_right, after)


def cross_second(table, k_caches, w, xw, sums, loc, row_left, row_own, w_left):
    n = w.shape[1]

    def body(
        q_ref, ka_ref, kb_ref, kc_ref, w_ref, sum_ref, loc_ref, rl_ref, ro_ref, wl_ref, *refs
    ):
        near_ref, *chip_refs, col_ref, row_ref, va, acc, jobs, xw_ref = refs
        g = lax.axis_index("group")
        xw_ref[g ^ 1] = near_ref[0]
        for j, x in enumerate(chip_refs):
            for i in range(2):
                xw_ref[g ^ (2 * j + 2 + i)] = x[i]
        va[...] = split(w_ref[...])
        acc[...] = jnp.zeros_like(acc)
        for ks, k_ref in zip(STAGES, (ka_ref, kb_ref, kc_ref)):
            count = jnp.int32(0)
            for k in ks:
                for c in range(2):
                    live = q_ref[16 + (g ^ k) * 2 + c] >= 0

                    @pl.when(live)
                    def _(count=count, k=k, c=c):
                        jobs[count] = (g ^ k) * 2 + c

                    count = count + live.astype(jnp.int32)

            def step(pair, carry, k_ref=k_ref, count=count):
                for u in range(2):
                    j = jnp.minimum(2 * pair + u, count - 1)
                    live = (2 * pair + u < count).astype(F32)
                    slot = jobs[j]
                    h, c = slot >> 1, slot & 1
                    rows = pl.ds(pl.multiple_of(c * 8, 8), 8)
                    k = k_ref[j]
                    col_ref[h, rows, :] = fold(mm(va[...], k, NN))
                    acc[...] += mm(split(xw_ref[h, rows, :] * live), k, NT)
                return carry

            lax.fori_loop(0, (count + 1) // 2, step, 0)
        row = fold(acc[...])
        row_ref[...] = row
        pairs = w_ref[...] * (0.5 * loc_ref[...] + ro_ref[...] + row) + wl_ref[...] * rl_ref[...]
        lane = lax.broadcasted_iota(jnp.int32, (8, 128), 1)
        pay = jnp.where(lane == 3, sum_ref[...] - jnp.sum(pairs, axis=1, keepdims=True), sum_ref[...])
        for h in range(8):
            col_ref[h, 16:24, 0:128] = pay
            col_ref[h, 16:24, 128:] = jnp.zeros((8, 128), F32)

    return pl.pallas_call(
        body,
        out_shape=(f32(8, 24, TILE), f32(8, n)),
        in_specs=[SMEM] + [VM] * 13,
        out_specs=(VM, VM),
        scratch_shapes=[
            pltpu.VMEM((16, n), BF16),
            pltpu.VMEM((16, n), F32),
            pltpu.SMEM((16,), jnp.int32),
            pltpu.VMEM((8, 16, TILE), F32),
        ],
        compiler_params=params(),
        name="cross_second",
    )(table, *k_caches, w, sums, loc, row_left, row_own, w_left, *xw)


def group_sum(table, w, deg, parts, ret):
    n = w.shape[1]
    m = len(parts)

    def body(q_ref, w_ref, deg_ref, *refs):
        part_refs, (x_ref, w2_ref, out_ref, acc) = refs[:m], refs[m:]
        total = part_refs[0][...]
        for p in part_refs[1:]:
            total = total + p[...]
        acc[...] = total
        for h in range(8):
            for c in range(2):
                t = q_ref[h * 2 + c]

                @pl.when(t >= 0)
                def _(h=h, c=c, t=t):
                    acc[:, span(t)] = acc[:, span(t)] + x_ref[h, c * 8 : c * 8 + 8, :]

        w2_ref[...] = 0.5 * (deg_ref[...] * w_ref[...] - acc[...])
        sums = x_ref[0, 16:24, 0:128]
        for h in range(1, 8):
            sums = sums + x_ref[h, 16:24, 0:128]
        for v in range(16):
            out_ref[v] = sums

    return pl.pallas_call(
        body,
        out_shape=(f32(8, n), f32(16, 8, 128)),
        in_specs=[SMEM] + [VM] * (3 + m),
        out_specs=(VM, VM),
        scratch_shapes=[pltpu.VMEM((8, n), F32)],
        compiler_params=params(),
        name="group_sum",
    )(table, w, deg, *parts, ret)


def finish(gathered, r, w, w2):
    n = r.shape[1]

    def body(g_ref, r_ref, w_ref, w2_ref, sol_ref, res_ref):
        sums = g_ref[0]
        for v in range(1, 16):
            sums = sums + g_ref[v]
        rho, mu, nu, xi = (sums[:, k : k + 1] for k in range(4))
        rv = r_ref[...]
        wv = w_ref[...]
        first = rho / (rho + mu)
        gap = (nu - mu * (mu / rho)) * (first * first)
        beta = gap / rho
        cr = mu / (rho + mu) + beta
        curvature = cr * cr * (rho + mu) - 2.0 * cr * first * (mu + nu) + first * first * (nu + xi)
        second = gap / curvature
        sol_ref[...] = (first + second * cr) * rv - (second * first) * wv
        res_ref[...] = (
            (mu / (rho + mu) - second * cr) * rv
            + (second * (first - cr) - first) * wv
            + (second * first) * w2_ref[...]
        )

    return pl.pallas_call(
        body,
        out_shape=(f32(8, n), f32(8, n)),
        in_specs=[VM] * 4,
        out_specs=(VM, VM),
        compiler_params=params(),
        name="finish",
    )(gathered, r, w, w2)


def on_device(points, targets, partner_tiles):
    dev_count = lax.axis_size("dev")
    to_right = [(i, i + 1) for i in range(dev_count - 1)]
    to_left = [(i + 1, i) for i in range(dev_count - 1)]

    def right_of(x):
        return lax.ppermute(x, "dev", to_left)

    def left_of(x):
        return lax.ppermute(x, "dev", to_right)

    def swap(x, k):
        return lax.ppermute(x, "group", [(i, i ^ k) for i in range(8)])

    def trade(x, axis="group"):
        return lax.all_to_all(x, axis, split_axis=0, concat_axis=0, tiled=True)

    table, own, *outgoing = prep(jnp.transpose(partner_tiles, (0, 2, 3, 1)), points, targets)
    arrived = {}
    for x, k in zip(outgoing, SWAPS[:5]):
        arrived[k] = swap(x, k)
    left = left_of(own)
    right = right_of(own)
    k_local, acc_local = local_first(own)

    def cross(stage, after):
        return cross_first(stage, table, own, [arrived[k] for k in stage], after)

    ret = {}

    def give_back(cols, stage):
        for x, k in zip(cols, stage):
            ret[k] = swap(x, k)

    k_a, row_a, *col_a = cross(STAGES[0], acc_local)
    give_back(col_a, STAGES[0])
    for x, k in zip(gate(outgoing[5:], [row_a, arrived[3], arrived[7]]), STAGES[2]):
        arrived[k] = swap(x, k)
    k_b, row_b, *col_b = cross(STAGES[1], row_a)
    give_back(col_b, STAGES[1])
    k_own, col_own, acc_band = band_first(own, right, row_b, False)
    k_left, to_r, to_l = band_first(left, right, col_own, True)
    from_left, from_right = left_of(to_r), right_of(to_l)
    k_c, row_c, *col_c = cross(STAGES[2], to_l)
    give_back(col_c, STAGES[2])
    w_own, w_relay, w, deg, sums = combine(
        table, targets, (acc_local, acc_band, from_left, from_right, row_a, row_b, row_c), [ret[k] for k in SWAPS]
    )
    w_left = left_of(w)
    w_right = right_of(w)
    partner = swap(w_relay, 1)
    xw = [partner] + [swap(x, 2 * j + 2) for j, x in enumerate(relay(w_own, partner))]
    loc2 = local_second(k_local, w)
    col_r, rowl_b, rowo_b = band_second(k_left, k_own, w_left, w, w_right, loc2)
    from_left2 = left_of(col_r)
    from_right2 = right_of(rowl_b)
    col_x, row_x = cross_second(table, (k_a, k_b, k_c), w, xw, sums, loc2, rowl_b, rowo_b, w_left)
    w2, column = group_sum(table, w, deg, (loc2, rowo_b, row_x, from_left2, from_right2), trade(col_x))
    return finish(trade(column, "dev"), targets, w, w2)


def solution(mesh):
    return jax.shard_map(
        on_device,
        mesh=mesh,
        in_specs=(P(("group", "dev"), None), P(None, ("group", "dev")), P()),
        out_specs=(P(None, ("group", "dev")), P(None, ("group", "dev"))),
        check_vma=False,
    )
```

```python
import jax
import jax.numpy as jnp
from jax import lax
from jax.experimental import pallas as pl
from jax.experimental.pallas import tpu as pltpu
from jax.sharding import PartitionSpec as P


TILE = 256
EXTRA = 8
SCALE = 3.9
C4 = 4.0 / SCALE**5
CUT = 5.0 * SCALE / 4.0
NT = (((1,), (1,)), ((), ()))
NN = (((1,), (0,)), ((), ()))
F32 = jnp.float32
BF16 = jnp.bfloat16
STAGES = ((2, 6, 1), (3, 7), (4, 5))
SWAPS = STAGES[0] + STAGES[1] + STAGES[2]

SMEM = pl.BlockSpec(memory_space=pltpu.SMEM)
ANY = pl.BlockSpec(memory_space=pl.ANY)
HBM = pl.BlockSpec(memory_space=pltpu.HBM)
VM = pl.BlockSpec(memory_space=pltpu.VMEM)


def mm(a, b, dims):
    return lax.dot_general(a, b, dims, preferred_element_type=F32)


def col_norms(x):
    x = x.astype(F32)
    return jnp.broadcast_to(jnp.sum(x * x, axis=1, keepdims=True), (x.shape[0], 128))


def kernel_tile(a, b_scaled, na, nb):
    q = mm(a, b_scaled, NT) + (jnp.concatenate([na, na], axis=1) + nb)
    q = jnp.maximum(q, 1e-30)
    u = jnp.maximum(SCALE - q * lax.rsqrt(q), 0.0)
    t = u * u
    return (t * t * (CUT - u)).astype(BF16)


def split(v):
    hi = v.astype(BF16)
    lo = (v - hi.astype(F32)).astype(BF16)
    return jnp.concatenate([hi, lo], axis=0)


def rhs_ones(rows, one):
    v = rows.astype(F32)
    return jnp.concatenate([v[:, 0:TILE], v[:, TILE:], jnp.full((16, TILE), one, F32)], axis=0).astype(BF16)


def fold(acc):
    return (acc[0:8] + acc[8:16]) * C4


def fold_ones(acc):
    return jnp.concatenate([acc[0:8] + acc[8:16], acc[16:24]], axis=0) * C4


def span(t):
    return pl.ds(pl.multiple_of(t * TILE, TILE), TILE)


def params(mib=12):
    return pltpu.CompilerParams(vmem_limit_bytes=mib * 1024 * 1024)


def f32(*shape):
    return jax.ShapeDtypeStruct(shape, F32)


def vmem_bf16(*shape):
    return pltpu.VMEM(shape, BF16)


def prep(partners, points, targets):
    n, d = points.shape
    nt = n // TILE

    def body(p_hbm, pts_ref, r_hbm, table_ref, msg_ref, *refs):
        outs, (r_ref, p_ref, sems) = refs[:-3], refs[-3:]
        g = lax.axis_index("group")
        dev = lax.axis_index("dev")
        copies = [pltpu.make_async_copy(r_hbm, r_ref, sems.at[nt])]
        for t in range(nt):
            s = slice(t * TILE, (t + 1) * TILE)
            copies.append(pltpu.make_async_copy(pts_ref.at[s, :], msg_ref.at[t, pl.ds(0, TILE), :], sems.at[t]))
        table_copy = pltpu.make_async_copy(p_hbm, p_ref, sems.at[nt + 1])
        table_copy.start()
        for cp in copies:
            cp.start()
        table_copy.wait()
        for h in range(8):
            for c in range(2):
                table_ref[h * 2 + c] = p_ref[h, g, c, dev]
                table_ref[16 + h * 2 + c] = p_ref[g, h, c, dev]
        for cp in copies:
            cp.wait()
        for t in range(nt):
            s = slice(t * TILE, (t + 1) * TILE)
            v = r_ref[:, s]
            hi = v.astype(BF16).astype(F32)
            msg_ref[t, TILE:, :] = jnp.concatenate([hi, v - hi], axis=1).astype(BF16)
        for k, out in zip(SWAPS, outs):
            for c in range(2):
                out[c] = msg_ref[jnp.maximum(p_ref[g ^ k, g, c, dev], 0)]

    return pl.pallas_call(
        body,
        out_shape=[jax.ShapeDtypeStruct((32,), jnp.int32), vmem_bf16(nt, TILE + EXTRA, d)]
        + [vmem_bf16(2, TILE + EXTRA, d) for _ in SWAPS],
        in_specs=[HBM, HBM, HBM],
        out_specs=[SMEM] + [VM] * (1 + len(SWAPS)),
        scratch_shapes=[
            pltpu.VMEM((8, n), F32),
            pltpu.SMEM(partners.shape, jnp.int32),
            pltpu.SemaphoreType.DMA((nt + 2,)),
        ],
        compiler_params=params(),
        name="prep",
    )(*(pltpu.with_memory_space_constraint(x, pltpu.HBM) for x in (partners, points, targets)))


def gate(held, arrived):
    m = len(held)

    def body(*refs):
        pass

    return pl.pallas_call(
        body,
        out_shape=[vmem_bf16(*x.shape) for x in held],
        in_specs=[VM] * m + [ANY] * len(arrived),
        out_specs=[VM] * m,
        input_output_aliases={i: i for i in range(m)},
        compiler_params=params(4),
        name="gate",
    )(*held, *arrived)


def local_first(own):
    nt, _, _ = own.shape
    n = nt * TILE

    def body(a_ref, k_ref, acc_ref, na, va, nb):
        for i in range(nt):
            s = slice(i * TILE, (i + 1) * TILE)
            x = col_norms(a_ref[i, 0:TILE, :])
            na[s, :] = x
            nb[:, s] = x.T[0:8]
            va[:, s] = rhs_ones(a_ref[i, TILE:, :], 1.0)

        def step(t, carry):
            s = span(t)
            b = a_ref[t, 0:TILE, :] * jnp.asarray(-2.0, BF16)
            for i in range(nt):
                c = slice(i * TILE, (i + 1) * TILE)
                k_ref[t, c, :] = kernel_tile(a_ref[i, 0:TILE, :], b, na[c, :], nb[0:1, s])
            acc_ref[:, s] = fold_ones(mm(va[...], k_ref[t], NN))
            return carry

        lax.fori_loop(0, nt, step, 0, unroll=2)

    return pl.pallas_call(
        body,
        out_shape=(vmem_bf16(nt, n, TILE), f32(16, n), pltpu.VMEM((n, 128), F32), vmem_bf16(32, n)),
        in_specs=[VM],
        out_specs=(VM,) * 4,
        scratch_shapes=[pltpu.VMEM((8, n), F32)],
        compiler_params=params(),
        name="local_first",
    )(own)


def band_step(nt, a_ref, b_ref, na, va, nb, vb, before_ref, k_ref, col_ref, row_ref, acc):
    acc[...] = jnp.zeros_like(acc)

    def step(t, carry):
        s = span(t)
        b = b_ref[t, 0:TILE, :] * jnp.asarray(-2.0, BF16)
        for i in range(nt):
            c = slice(i * TILE, (i + 1) * TILE)
            k_ref[t, c, :] = kernel_tile(a_ref[i, 0:TILE, :], b, na[c, :], nb[0:1, s])
        k = k_ref[t]
        col = fold_ones(mm(va[...], k, NN))
        col_ref[:, s] = col if before_ref is None else before_ref[:, s] + col
        acc[...] += mm(vb[:, s], k, NT)
        return carry

    lax.fori_loop(0, nt, step, 0, unroll=3)
    row_ref[...] = fold_ones(acc[...])


def band_own(own, norms, rhs, right, after):
    nt, _, _ = own.shape
    n = nt * TILE

    def body(a_ref, na, va, b_ref, _, k_ref, col_ref, row_ref, nb, vb, acc):
        has_right = (lax.axis_index("dev") < lax.axis_size("dev") - 1).astype(F32)
        for i in range(nt):
            s = slice(i * TILE, (i + 1) * TILE)
            nb[:, s] = col_norms(b_ref[i, 0:TILE, :]).T[0:8]
            vb[:, s] = rhs_ones(b_ref[i, TILE:, :], has_right)
        band_step(nt, a_ref, b_ref, na, va, nb, vb, None, k_ref, col_ref, row_ref, acc)

    return pl.pallas_call(
        body,
        out_shape=(vmem_bf16(nt, n, TILE), f32(16, n), f32(16, n), pltpu.VMEM((8, n), F32), vmem_bf16(32, n)),
        in_specs=[VM] * 4 + [ANY],
        out_specs=(VM,) * 5,
        scratch_shapes=[pltpu.VMEM((32, n), F32)],
        compiler_params=params(),
        name="band_own",
    )(own, norms, rhs, right, after)


def band_left(left, right, right_norms, right_rhs, before):
    nt, _, _ = left.shape
    n = nt * TILE

    def body(a_ref, b_ref, nb, vb, before_ref, k_ref, col_ref, row_ref, na, va, acc):
        has_left = (lax.axis_index("dev") > 0).astype(F32)
        for i in range(nt):
            s = slice(i * TILE, (i + 1) * TILE)
            na[s, :] = col_norms(a_ref[i, 0:TILE, :])
            va[:, s] = rhs_ones(a_ref[i, TILE:, :], has_left)
        band_step(nt, a_ref, b_ref, na, va, nb, vb, before_ref, k_ref, col_ref, row_ref, acc)

    return pl.pallas_call(
        body,
        out_shape=(vmem_bf16(nt, n, TILE), f32(16, n), f32(16, n)),
        in_specs=[VM] * 5,
        out_specs=(VM,) * 3,
        scratch_shapes=[pltpu.VMEM((n, 128), F32), pltpu.VMEM((32, n), BF16), pltpu.VMEM((32, n), F32)],
        compiler_params=params(),
        name="band_left",
    )(left, right, right_norms, right_rhs, before)


def cross_first(ks, table, own, norms, rhs, tiles, after):
    nt, _, d = own.shape
    n = nt * TILE
    m = len(ks)
    slots = 2 * m

    def body(q_ref, a_ref, na, va, _, *refs):
        tile_refs = refs[:m]
        k_ref, row_ref, *cols = refs[m : 2 * m + 2]
        buf, jobs, sems, acc, nb, col = refs[2 * m + 2 :]
        g = lax.axis_index("group")
        count = jnp.int32(0)
        for i, k in enumerate(ks):
            for c in range(2):
                live = q_ref[16 + (g ^ k) * 2 + c] >= 0

                @pl.when(live)
                def _(count=count, i=i, k=k, c=c):
                    pltpu.make_async_copy(tile_refs[i].at[c], buf.at[count], sems.at[count]).start()
                    jobs[count] = 2 * i + c

                count = count + live.astype(jnp.int32)
        acc[...] = jnp.zeros_like(acc)

        def arrive(j, carry):
            pltpu.make_async_copy(tile_refs[0].at[0], buf.at[j], sems.at[j]).wait()
            return carry

        lax.fori_loop(0, count, arrive, 0)

        def step(pair, carry):
            for u in range(2):
                j = jnp.minimum(2 * pair + u, count - 1)
                live = (2 * pair + u < count).astype(F32)
                b = buf[j, 0:TILE, :]
                nb[u] = col_norms(b).T[0:8]
                b = b * jnp.asarray(-2.0, BF16)
                vb = rhs_ones(buf[j, TILE:, :].astype(F32) * live, live)
                for i in range(nt):
                    c = slice(i * TILE, (i + 1) * TILE)
                    k_ref[j, c, :] = kernel_tile(a_ref[i, 0:TILE, :], b, na[c, :], nb[u, 0:1, :])
                k = k_ref[j]
                col[jobs[j]] = fold_ones(mm(va[...], k, NN))
                acc[...] += mm(vb, k, NT)
            return carry

        lax.fori_loop(0, (count + 1) // 2, step, 0)
        row_ref[...] = fold_ones(acc[...])
        for i, out in enumerate(cols):
            out[...] = col[2 * i : 2 * i + 2]

    return pl.pallas_call(
        body,
        out_shape=[vmem_bf16(slots, n, TILE), f32(16, n)] + [f32(2, 16, TILE)] * m,
        in_specs=[SMEM, VM, VM, VM, ANY] + [ANY] * m,
        out_specs=[VM] * (2 + m),
        scratch_shapes=[
            pltpu.VMEM((slots, TILE + EXTRA, d), BF16),
            pltpu.SMEM((slots,), jnp.int32),
            pltpu.SemaphoreType.DMA((slots,)),
            pltpu.VMEM((32, n), F32),
            pltpu.VMEM((2, 8, TILE), F32),
            pltpu.VMEM((slots, 16, TILE), F32),
        ],
        compiler_params=params(),
    )(table, own, norms, rhs, after, *tiles)


def combine(table, r, parts, ret):
    n = r.shape[1]
    m = len(parts)

    def body(q_ref, r_ref, *refs):
        part_refs, (*x_refs, w_ref, deg_ref, sum_ref, acc) = refs[:m], refs[m:]
        x_refs, (own_ref, relay_ref) = x_refs[:7], x_refs[7:]
        g = lax.axis_index("group")
        total = part_refs[0][...]
        for p in part_refs[1:]:
            total = total + p[...]
        acc[...] = total
        for k, x in zip(SWAPS, x_refs):
            for c in range(2):
                t = q_ref[(g ^ k) * 2 + c]

                @pl.when(t >= 0)
                def _(x=x, c=c, t=t):
                    acc[:, span(t)] = acc[:, span(t)] + x[c]

        rv = r_ref[...]
        deg = acc[8:16, :]
        w = 0.5 * (deg * rv - acc[0:8, :])
        w_ref[...] = w
        deg_ref[...] = deg
        for j in range(4):
            for out, k in ((own_ref, 2 * j), (relay_ref, 2 * j + 1)):
                for c in range(2):
                    t = jnp.maximum(q_ref[(g ^ k) * 2 + c], 0)
                    out[j, c * 8 : c * 8 + 8, :] = w_ref[:, span(t)]
        lane = lax.broadcasted_iota(jnp.int32, (8, 128), 1)
        sums = jnp.zeros((8, 128), F32)
        for k, v in enumerate((rv * rv, rv * w, w * w, 0.5 * deg * w * w)):
            sums = jnp.where(lane == k, jnp.sum(v, axis=1, keepdims=True), sums)
        sum_ref[...] = sums

    return pl.pallas_call(
        body,
        out_shape=[f32(4, 16, TILE), f32(4, 16, TILE), f32(8, n), f32(8, n), f32(8, 128)],
        in_specs=[SMEM] + [VM] * (m + 8),
        out_specs=[VM] * 5,
        scratch_shapes=[pltpu.VMEM((16, n), F32)],
        compiler_params=params(),
        name="combine",
    )(table, r, *parts, *ret)


def relay(own, partner):
    def body(own_ref, partner_ref, *outs):
        for j, out in enumerate(outs):
            out[0] = own_ref[j + 1]
            out[1] = partner_ref[j + 1]

    return pl.pallas_call(
        body,
        out_shape=[f32(2, 16, TILE)] * 3,
        in_specs=[VM, VM],
        out_specs=[VM] * 3,
        compiler_params=params(4),
        name="relay",
    )(own, partner)


def local_second(k_local, w):
    nt, n, _ = k_local.shape

    def body(k_ref, w_ref, out_ref):
        va = split(w_ref[...])
        for t in range(nt):
            out_ref[:, t * TILE : (t + 1) * TILE] = fold(mm(va, k_ref[t], NN))

    return pl.pallas_call(
        body,
        out_shape=f32(8, n),
        in_specs=[VM, VM],
        out_specs=VM,
        compiler_params=params(),
        name="local_second",
    )(k_local, w)


def band_second(k_left, k_own, w_left, w, w_right, after):
    nt, n, _ = k_own.shape

    def body(kl_ref, ko_ref, wl_ref, w_ref, wb_ref, _, col_ref, rowl_ref, rowo_ref, acc_l, acc_o):
        va_l = split(wl_ref[...])
        va_o = split(w_ref[...])
        vb = split(wb_ref[...])
        for t in range(nt):
            s = slice(t * TILE, (t + 1) * TILE)
            col_ref[:, s] = fold(mm(va_l, kl_ref[t], NN) + mm(va_o, ko_ref[t], NN))
            for acc, k_ref in ((acc_l, kl_ref), (acc_o, ko_ref)):
                new = mm(vb[:, s], k_ref[t], NT)
                acc[...] = new if t == 0 else acc[...] + new
        rowl_ref[...] = fold(acc_l[...])
        rowo_ref[...] = fold(acc_o[...])

    return pl.pallas_call(
        body,
        out_shape=(f32(8, n), f32(8, n), f32(8, n)),
        in_specs=[VM] * 5 + [ANY],
        out_specs=(VM,) * 3,
        scratch_shapes=[pltpu.VMEM((16, n), F32), pltpu.VMEM((16, n), F32)],
        compiler_params=params(),
        name="band_second",
    )(k_left, k_own, w_left, w, w_right, after)


def cross_second(table, k_caches, w, xw, sums, loc, row_left, row_own, w_left):
    n = w.shape[1]

    def body(
        q_ref, ka_ref, kb_ref, kc_ref, w_ref, sum_ref, loc_ref, rl_ref, ro_ref, wl_ref, *refs
    ):
        near_ref, *chip_refs, col_ref, row_ref, va, acc, jobs, xw_ref = refs
        g = lax.axis_index("group")
        xw_ref[g ^ 1] = near_ref[0]
        for j, x in enumerate(chip_refs):
            for i in range(2):
                xw_ref[g ^ (2 * j + 2 + i)] = x[i]
        va[...] = split(w_ref[...])
        acc[...] = jnp.zeros_like(acc)
        for ks, k_ref in zip(STAGES, (ka_ref, kb_ref, kc_ref)):
            count = jnp.int32(0)
            for k in ks:
                for c in range(2):
                    live = q_ref[16 + (g ^ k) * 2 + c] >= 0

                    @pl.when(live)
                    def _(count=count, k=k, c=c):
                        jobs[count] = (g ^ k) * 2 + c

                    count = count + live.astype(jnp.int32)

            def step(pair, carry, k_ref=k_ref, count=count):
                for u in range(2):
                    j = jnp.minimum(2 * pair + u, count - 1)
                    live = (2 * pair + u < count).astype(F32)
                    slot = jobs[j]
                    h, c = slot >> 1, slot & 1
                    rows = pl.ds(pl.multiple_of(c * 8, 8), 8)
                    k = k_ref[j]
                    col_ref[h, rows, :] = fold(mm(va[...], k, NN))
                    acc[...] += mm(split(xw_ref[h, rows, :] * live), k, NT)
                return carry

            lax.fori_loop(0, (count + 1) // 2, step, 0)
        row = fold(acc[...])
        row_ref[...] = row
        pairs = w_ref[...] * (0.5 * loc_ref[...] + ro_ref[...] + row) + wl_ref[...] * rl_ref[...]
        lane = lax.broadcasted_iota(jnp.int32, (8, 128), 1)
        pay = jnp.where(lane == 3, sum_ref[...] - jnp.sum(pairs, axis=1, keepdims=True), sum_ref[...])
        for h in range(8):
            col_ref[h, 16:24, 0:128] = pay
            col_ref[h, 16:24, 128:] = jnp.zeros((8, 128), F32)

    return pl.pallas_call(
        body,
        out_shape=(f32(8, 24, TILE), f32(8, n)),
        in_specs=[SMEM] + [VM] * 13,
        out_specs=(VM, VM),
        scratch_shapes=[
            pltpu.VMEM((16, n), BF16),
            pltpu.VMEM((16, n), F32),
            pltpu.SMEM((16,), jnp.int32),
            pltpu.VMEM((8, 16, TILE), F32),
        ],
        compiler_params=params(),
        name="cross_second",
    )(table, *k_caches, w, sums, loc, row_left, row_own, w_left, *xw)


def group_sum(table, w, deg, parts, ret):
    n = w.shape[1]
    m = len(parts)

    def body(q_ref, w_ref, deg_ref, *refs):
        part_refs, (x_ref, w2_ref, out_ref, acc) = refs[:m], refs[m:]
        total = part_refs[0][...]
        for p in part_refs[1:]:
            total = total + p[...]
        acc[...] = total
        for h in range(8):
            for c in range(2):
                t = q_ref[h * 2 + c]

                @pl.when(t >= 0)
                def _(h=h, c=c, t=t):
                    acc[:, span(t)] = acc[:, span(t)] + x_ref[h, c * 8 : c * 8 + 8, :]

        w2_ref[...] = 0.5 * (deg_ref[...] * w_ref[...] - acc[...])
        sums = x_ref[0, 16:24, 0:128]
        for h in range(1, 8):
            sums = sums + x_ref[h, 16:24, 0:128]
        for v in range(16):
            out_ref[v] = sums

    return pl.pallas_call(
        body,
        out_shape=(f32(8, n), f32(16, 8, 128)),
        in_specs=[SMEM] + [VM] * (3 + m),
        out_specs=(VM, VM),
        scratch_shapes=[pltpu.VMEM((8, n), F32)],
        compiler_params=params(),
        name="group_sum",
    )(table, w, deg, *parts, ret)


def finish(gathered, r, w, w2):
    n = r.shape[1]

    def body(g_ref, r_ref, w_ref, w2_ref, sol_ref, res_ref):
        sums = g_ref[0]
        for v in range(1, 16):
            sums = sums + g_ref[v]
        rho, mu, nu, xi = (sums[:, k : k + 1] for k in range(4))
        rv = r_ref[...]
        wv = w_ref[...]
        first = rho / (rho + mu)
        gap = (nu - mu * (mu / rho)) * (first * first)
        beta = gap / rho
        cr = mu / (rho + mu) + beta
        curvature = cr * cr * (rho + mu) - 2.0 * cr * first * (mu + nu) + first * first * (nu + xi)
        second = gap / curvature
        sol_ref[...] = (first + second * cr) * rv - (second * first) * wv
        res_ref[...] = (
            (mu / (rho + mu) - second * cr) * rv
            + (second * (first - cr) - first) * wv
            + (second * first) * w2_ref[...]
        )

    return pl.pallas_call(
        body,
        out_shape=(f32(8, n), f32(8, n)),
        in_specs=[VM] * 4,
        out_specs=(VM, VM),
        compiler_params=params(),
        name="finish",
    )(gathered, r, w, w2)


def on_device(points, targets, partner_tiles):
    dev_count = lax.axis_size("dev")
    to_right = [(i, i + 1) for i in range(dev_count - 1)]
    to_left = [(i + 1, i) for i in range(dev_count - 1)]

    def right_of(x):
        return lax.ppermute(x, "dev", to_left)

    def left_of(x):
        return lax.ppermute(x, "dev", to_right)

    def swap(x, k):
        return lax.ppermute(x, "group", [(i, i ^ k) for i in range(8)])

    def trade(x, axis="group"):
        return lax.all_to_all(x, axis, split_axis=0, concat_axis=0, tiled=True)

    table, own, *outgoing = prep(jnp.transpose(partner_tiles, (0, 2, 3, 1)), points, targets)
    arrived = {}
    for x, k in zip(outgoing, SWAPS[:5]):
        arrived[k] = swap(x, k)
    left = left_of(own)
    right = right_of(own)
    k_local, acc_local, norms, rhs = local_first(own)

    def cross(stage, after):
        return cross_first(stage, table, own, norms, rhs, [arrived[k] for k in stage], after)

    ret = {}

    def give_back(cols, stage):
        for x, k in zip(cols, stage):
            ret[k] = swap(x, k)

    k_a, row_a, *col_a = cross(STAGES[0], acc_local)
    give_back(col_a, STAGES[0])
    for x, k in zip(gate(outgoing[5:], [row_a, arrived[3], arrived[7]]), STAGES[2]):
        arrived[k] = swap(x, k)
    k_b, row_b, *col_b = cross(STAGES[1], row_a)
    give_back(col_b, STAGES[1])
    k_own, col_own, acc_band, right_norms, right_rhs = band_own(own, norms, rhs, right, row_b)
    k_left, to_r, to_l = band_left(left, right, right_norms, right_rhs, col_own)
    from_left, from_right = left_of(to_r), right_of(to_l)
    k_c, row_c, *col_c = cross(STAGES[2], to_l)
    give_back(col_c, STAGES[2])
    w_own, w_relay, w, deg, sums = combine(
        table, targets, (acc_local, acc_band, from_left, from_right, row_a, row_b, row_c), [ret[k] for k in SWAPS]
    )
    w_left = left_of(w)
    w_right = right_of(w)
    partner = swap(w_relay, 1)
    xw = [partner] + [swap(x, 2 * j + 2) for j, x in enumerate(relay(w_own, partner))]
    loc2 = local_second(k_local, w)
    col_r, rowl_b, rowo_b = band_second(k_left, k_own, w_left, w, w_right, loc2)
    from_left2 = left_of(col_r)
    from_right2 = right_of(rowl_b)
    col_x, row_x = cross_second(table, (k_a, k_b, k_c), w, xw, sums, loc2, rowl_b, rowo_b, w_left)
    w2, column = group_sum(table, w, deg, (loc2, rowo_b, row_x, from_left2, from_right2), trade(col_x))
    return finish(trade(column, "dev"), targets, w, w2)


def solution(mesh):
    return jax.shard_map(
        on_device,
        mesh=mesh,
        in_specs=(P(("group", "dev"), None), P(None, ("group", "dev")), P()),
        out_specs=(P(None, ("group", "dev")), P(None, ("group", "dev"))),
        check_vma=False,
    )
```

```python
import jax
import jax.numpy as jnp
from jax import lax
from jax.experimental import pallas as pl
from jax.experimental.pallas import tpu as pltpu
from jax.sharding import PartitionSpec as P


TILE = 256
EXTRA = 8
SCALE = 3.9
C4 = 4.0 / SCALE**5
CUT = 5.0 * SCALE / 4.0
NT = (((1,), (1,)), ((), ()))
NN = (((1,), (0,)), ((), ()))
F32 = jnp.float32
BF16 = jnp.bfloat16
STAGES = ((2, 6, 1), (3, 7), (4, 5))
SWAPS = STAGES[0] + STAGES[1] + STAGES[2]

SMEM = pl.BlockSpec(memory_space=pltpu.SMEM)
ANY = pl.BlockSpec(memory_space=pl.ANY)
HBM = pl.BlockSpec(memory_space=pltpu.HBM)
VM = pl.BlockSpec(memory_space=pltpu.VMEM)


def mm(a, b, dims):
    return lax.dot_general(a, b, dims, preferred_element_type=F32)


def col_norms(x):
    x = x.astype(F32)
    return jnp.broadcast_to(jnp.sum(x * x, axis=1, keepdims=True), (x.shape[0], 128))


def kernel_tile(a, b_scaled, na, nb):
    q = mm(a, b_scaled, NT) + (jnp.concatenate([na, na], axis=1) + nb)
    q = jnp.maximum(q, 1e-30)
    u = jnp.maximum(SCALE - q * lax.rsqrt(q), 0.0)
    t = u * u
    return (t * t * (CUT - u)).astype(BF16)


def split(v):
    hi = v.astype(BF16)
    lo = (v - hi.astype(F32)).astype(BF16)
    return jnp.concatenate([hi, lo], axis=0)


def rhs_ones(rows, one):
    v = rows.astype(F32)
    return jnp.concatenate([v[:, 0:TILE], v[:, TILE:], jnp.full((16, TILE), one, F32)], axis=0).astype(BF16)


def fold(acc):
    return (acc[0:8] + acc[8:16]) * C4


def fold_ones(acc):
    return jnp.concatenate([acc[0:8] + acc[8:16], acc[16:24]], axis=0) * C4


def span(t):
    return pl.ds(pl.multiple_of(t * TILE, TILE), TILE)


def params(mib=12):
    return pltpu.CompilerParams(vmem_limit_bytes=mib * 1024 * 1024)


def f32(*shape):
    return jax.ShapeDtypeStruct(shape, F32)


def vmem_bf16(*shape):
    return pltpu.VMEM(shape, BF16)


def prep(partners, points, targets):
    n, d = points.shape
    nt = n // TILE

    def body(p_hbm, pts_ref, r_hbm, table_ref, msg_ref, *refs):
        outs, (r_ref, p_ref, sems) = refs[:-3], refs[-3:]
        g = lax.axis_index("group")
        dev = lax.axis_index("dev")
        copies = [pltpu.make_async_copy(r_hbm, r_ref, sems.at[nt])]
        for t in range(nt):
            s = slice(t * TILE, (t + 1) * TILE)
            copies.append(pltpu.make_async_copy(pts_ref.at[s, :], msg_ref.at[t, pl.ds(0, TILE), :], sems.at[t]))
        table_copy = pltpu.make_async_copy(p_hbm, p_ref, sems.at[nt + 1])
        table_copy.start()
        for cp in copies:
            cp.start()
        table_copy.wait()
        for h in range(8):
            for c in range(2):
                table_ref[h * 2 + c] = p_ref[h, g, c, dev]
                table_ref[16 + h * 2 + c] = p_ref[g, h, c, dev]
        for cp in copies:
            cp.wait()
        for t in range(nt):
            s = slice(t * TILE, (t + 1) * TILE)
            v = r_ref[:, s]
            hi = v.astype(BF16).astype(F32)
            msg_ref[t, TILE:, :] = jnp.concatenate([hi, v - hi], axis=1).astype(BF16)
        for k, out in zip(SWAPS, outs):
            for c in range(2):
                out[c] = msg_ref[jnp.maximum(p_ref[g ^ k, g, c, dev], 0)]

    return pl.pallas_call(
        body,
        out_shape=[jax.ShapeDtypeStruct((32,), jnp.int32), vmem_bf16(nt, TILE + EXTRA, d)]
        + [vmem_bf16(2, TILE + EXTRA, d) for _ in SWAPS],
        in_specs=[HBM, HBM, HBM],
        out_specs=[SMEM] + [VM] * (1 + len(SWAPS)),
        scratch_shapes=[
            pltpu.VMEM((8, n), F32),
            pltpu.SMEM(partners.shape, jnp.int32),
            pltpu.SemaphoreType.DMA((nt + 2,)),
        ],
        compiler_params=params(),
        name="prep",
    )(*(pltpu.with_memory_space_constraint(x, pltpu.HBM) for x in (partners, points, targets)))


def gate(held, arrived):
    m = len(held)

    def body(*refs):
        pass

    return pl.pallas_call(
        body,
        out_shape=[vmem_bf16(*x.shape) for x in held],
        in_specs=[VM] * m + [ANY] * len(arrived),
        out_specs=[VM] * m,
        input_output_aliases={i: i for i in range(m)},
        compiler_params=params(4),
        name="gate",
    )(*held, *arrived)


def local_first(own):
    nt, _, _ = own.shape
    n = nt * TILE

    def body(a_ref, k_ref, acc_ref, na, va, nb):
        for i in range(nt):
            s = slice(i * TILE, (i + 1) * TILE)
            x = col_norms(a_ref[i, 0:TILE, :])
            na[s, :] = x
            nb[:, s] = x.T[0:8]
            va[:, s] = rhs_ones(a_ref[i, TILE:, :], 1.0)

        for t in range(nt):
            s = slice(t * TILE, (t + 1) * TILE)
            b = a_ref[t, 0:TILE, :] * jnp.asarray(-2.0, BF16)
            for i in range(nt):
                c = slice(i * TILE, (i + 1) * TILE)
                k_ref[t, c, :] = kernel_tile(a_ref[i, 0:TILE, :], b, na[c, :], nb[0:1, s])
            acc_ref[:, s] = fold_ones(mm(va[...], k_ref[t], NN))

    return pl.pallas_call(
        body,
        out_shape=(vmem_bf16(nt, n, TILE), f32(16, n), pltpu.VMEM((n, 128), F32), vmem_bf16(32, n)),
        in_specs=[VM],
        out_specs=(VM,) * 4,
        scratch_shapes=[pltpu.VMEM((8, n), F32)],
        compiler_params=params(),
        name="local_first",
    )(own)


def band_step(nt, a_ref, b_ref, na, va, nb, vb, before_ref, k_ref, col_ref, row_ref, acc):
    acc[...] = jnp.zeros_like(acc)

    for t in range(nt):
        s = slice(t * TILE, (t + 1) * TILE)
        b = b_ref[t, 0:TILE, :] * jnp.asarray(-2.0, BF16)
        for i in range(nt):
            c = slice(i * TILE, (i + 1) * TILE)
            k_ref[t, c, :] = kernel_tile(a_ref[i, 0:TILE, :], b, na[c, :], nb[0:1, s])
        k = k_ref[t]
        col = fold_ones(mm(va[...], k, NN))
        col_ref[:, s] = col if before_ref is None else before_ref[:, s] + col
        acc[...] += mm(vb[:, s], k, NT)
    row_ref[...] = fold_ones(acc[...])


def band_own(own, norms, rhs, right, after):
    nt, _, _ = own.shape
    n = nt * TILE

    def body(a_ref, na, va, b_ref, _, k_ref, col_ref, row_ref, nb, vb, acc):
        has_right = (lax.axis_index("dev") < lax.axis_size("dev") - 1).astype(F32)
        for i in range(nt):
            s = slice(i * TILE, (i + 1) * TILE)
            nb[:, s] = col_norms(b_ref[i, 0:TILE, :]).T[0:8]
            vb[:, s] = rhs_ones(b_ref[i, TILE:, :], has_right)
        band_step(nt, a_ref, b_ref, na, va, nb, vb, None, k_ref, col_ref, row_ref, acc)

    return pl.pallas_call(
        body,
        out_shape=(vmem_bf16(nt, n, TILE), f32(16, n), f32(16, n), pltpu.VMEM((8, n), F32), vmem_bf16(32, n)),
        in_specs=[VM] * 4 + [ANY],
        out_specs=(VM,) * 5,
        scratch_shapes=[pltpu.VMEM((32, n), F32)],
        compiler_params=params(),
        name="band_own",
    )(own, norms, rhs, right, after)


def band_left(left, right, right_norms, right_rhs, before):
    nt, _, _ = left.shape
    n = nt * TILE

    def body(a_ref, b_ref, nb, vb, before_ref, k_ref, col_ref, row_ref, na, va, acc):
        has_left = (lax.axis_index("dev") > 0).astype(F32)
        for i in range(nt):
            s = slice(i * TILE, (i + 1) * TILE)
            na[s, :] = col_norms(a_ref[i, 0:TILE, :])
            va[:, s] = rhs_ones(a_ref[i, TILE:, :], has_left)
        band_step(nt, a_ref, b_ref, na, va, nb, vb, before_ref, k_ref, col_ref, row_ref, acc)

    return pl.pallas_call(
        body,
        out_shape=(vmem_bf16(nt, n, TILE), f32(16, n), f32(16, n)),
        in_specs=[VM] * 5,
        out_specs=(VM,) * 3,
        scratch_shapes=[pltpu.VMEM((n, 128), F32), pltpu.VMEM((32, n), BF16), pltpu.VMEM((32, n), F32)],
        compiler_params=params(),
        name="band_left",
    )(left, right, right_norms, right_rhs, before)


def cross_first(ks, table, own, norms, rhs, tiles, after):
    nt, _, d = own.shape
    n = nt * TILE
    m = len(ks)
    slots = 2 * m

    def body(q_ref, a_ref, na, va, _, *refs):
        tile_refs = refs[:m]
        k_ref, row_ref, *cols = refs[m : 2 * m + 2]
        buf, jobs, sems, acc, nb, col = refs[2 * m + 2 :]
        g = lax.axis_index("group")
        count = jnp.int32(0)
        for i, k in enumerate(ks):
            for c in range(2):
                live = q_ref[16 + (g ^ k) * 2 + c] >= 0

                @pl.when(live)
                def _(count=count, i=i, k=k, c=c):
                    pltpu.make_async_copy(tile_refs[i].at[c], buf.at[count], sems.at[count]).start()
                    jobs[count] = 2 * i + c

                count = count + live.astype(jnp.int32)
        acc[...] = jnp.zeros_like(acc)

        def arrive(j, carry):
            pltpu.make_async_copy(tile_refs[0].at[0], buf.at[j], sems.at[j]).wait()
            return carry

        lax.fori_loop(0, count, arrive, 0)

        def step(pair, carry):
            for u in range(2):
                j = jnp.minimum(2 * pair + u, count - 1)
                live = (2 * pair + u < count).astype(F32)
                b = buf[j, 0:TILE, :]
                nb[u] = col_norms(b).T[0:8]
                b = b * jnp.asarray(-2.0, BF16)
                vb = rhs_ones(buf[j, TILE:, :].astype(F32) * live, live)
                for i in range(nt):
                    c = slice(i * TILE, (i + 1) * TILE)
                    k_ref[j, c, :] = kernel_tile(a_ref[i, 0:TILE, :], b, na[c, :], nb[u, 0:1, :])
                k = k_ref[j]
                col[jobs[j]] = fold_ones(mm(va[...], k, NN))
                acc[...] += mm(vb, k, NT)
            return carry

        lax.fori_loop(0, (count + 1) // 2, step, 0)
        row_ref[...] = fold_ones(acc[...])
        for i, out in enumerate(cols):
            out[...] = col[2 * i : 2 * i + 2]

    return pl.pallas_call(
        body,
        out_shape=[vmem_bf16(slots, n, TILE), f32(16, n)] + [f32(2, 16, TILE)] * m,
        in_specs=[SMEM, VM, VM, VM, ANY] + [ANY] * m,
        out_specs=[VM] * (2 + m),
        scratch_shapes=[
            pltpu.VMEM((slots, TILE + EXTRA, d), BF16),
            pltpu.SMEM((slots,), jnp.int32),
            pltpu.SemaphoreType.DMA((slots,)),
            pltpu.VMEM((32, n), F32),
            pltpu.VMEM((2, 8, TILE), F32),
            pltpu.VMEM((slots, 16, TILE), F32),
        ],
        compiler_params=params(),
    )(table, own, norms, rhs, after, *tiles)


def combine(table, r, parts, ret):
    n = r.shape[1]
    m = len(parts)

    def body(q_ref, r_ref, *refs):
        part_refs, (*x_refs, w_ref, deg_ref, sum_ref, acc) = refs[:m], refs[m:]
        x_refs, (own_ref, relay_ref) = x_refs[:7], x_refs[7:]
        g = lax.axis_index("group")
        total = part_refs[0][...]
        for p in part_refs[1:]:
            total = total + p[...]
        acc[...] = total
        for k, x in zip(SWAPS, x_refs):
            for c in range(2):
                t = q_ref[(g ^ k) * 2 + c]

                @pl.when(t >= 0)
                def _(x=x, c=c, t=t):
                    acc[:, span(t)] = acc[:, span(t)] + x[c]

        rv = r_ref[...]
        deg = acc[8:16, :]
        w = 0.5 * (deg * rv - acc[0:8, :])
        w_ref[...] = w
        deg_ref[...] = deg
        for j in range(4):
            for out, k in ((own_ref, 2 * j), (relay_ref, 2 * j + 1)):
                for c in range(2):
                    t = jnp.maximum(q_ref[(g ^ k) * 2 + c], 0)
                    out[j, c * 8 : c * 8 + 8, :] = w_ref[:, span(t)]
        lane = lax.broadcasted_iota(jnp.int32, (8, 128), 1)
        sums = jnp.zeros((8, 128), F32)
        for k, v in enumerate((rv * rv, rv * w, w * w, 0.5 * deg * w * w)):
            sums = jnp.where(lane == k, jnp.sum(v, axis=1, keepdims=True), sums)
        sum_ref[...] = sums

    return pl.pallas_call(
        body,
        out_shape=[f32(4, 16, TILE), f32(4, 16, TILE), f32(8, n), f32(8, n), f32(8, 128)],
        in_specs=[SMEM] + [VM] * (m + 8),
        out_specs=[VM] * 5,
        scratch_shapes=[pltpu.VMEM((16, n), F32)],
        compiler_params=params(),
        name="combine",
    )(table, r, *parts, *ret)


def relay(own, partner):
    def body(own_ref, partner_ref, *outs):
        for j, out in enumerate(outs):
            out[0] = own_ref[j + 1]
            out[1] = partner_ref[j + 1]

    return pl.pallas_call(
        body,
        out_shape=[f32(2, 16, TILE)] * 3,
        in_specs=[VM, VM],
        out_specs=[VM] * 3,
        compiler_params=params(4),
        name="relay",
    )(own, partner)


def local_second(k_local, w):
    nt, n, _ = k_local.shape

    def body(k_ref, w_ref, out_ref):
        va = split(w_ref[...])
        for t in range(nt):
            out_ref[:, t * TILE : (t + 1) * TILE] = fold(mm(va, k_ref[t], NN))

    return pl.pallas_call(
        body,
        out_shape=f32(8, n),
        in_specs=[VM, VM],
        out_specs=VM,
        compiler_params=params(),
        name="local_second",
    )(k_local, w)


def band_second(k_left, k_own, w_left, w, w_right, after):
    nt, n, _ = k_own.shape

    def body(kl_ref, ko_ref, wl_ref, w_ref, wb_ref, _, col_ref, rowl_ref, rowo_ref, acc_l, acc_o):
        va_l = split(wl_ref[...])
        va_o = split(w_ref[...])
        vb = split(wb_ref[...])
        for t in range(nt):
            s = slice(t * TILE, (t + 1) * TILE)
            col_ref[:, s] = fold(mm(va_l, kl_ref[t], NN) + mm(va_o, ko_ref[t], NN))
            for acc, k_ref in ((acc_l, kl_ref), (acc_o, ko_ref)):
                new = mm(vb[:, s], k_ref[t], NT)
                acc[...] = new if t == 0 else acc[...] + new
        rowl_ref[...] = fold(acc_l[...])
        rowo_ref[...] = fold(acc_o[...])

    return pl.pallas_call(
        body,
        out_shape=(f32(8, n), f32(8, n), f32(8, n)),
        in_specs=[VM] * 5 + [ANY],
        out_specs=(VM,) * 3,
        scratch_shapes=[pltpu.VMEM((16, n), F32), pltpu.VMEM((16, n), F32)],
        compiler_params=params(),
        name="band_second",
    )(k_left, k_own, w_left, w, w_right, after)


def cross_second(table, k_caches, w, xw, sums, loc, row_left, row_own, w_left):
    n = w.shape[1]

    def body(
        q_ref, ka_ref, kb_ref, kc_ref, w_ref, sum_ref, loc_ref, rl_ref, ro_ref, wl_ref, *refs
    ):
        near_ref, *chip_refs, col_ref, row_ref, va, acc, jobs, xw_ref = refs
        g = lax.axis_index("group")
        xw_ref[g ^ 1] = near_ref[0]
        for j, x in enumerate(chip_refs):
            for i in range(2):
                xw_ref[g ^ (2 * j + 2 + i)] = x[i]
        va[...] = split(w_ref[...])
        acc[...] = jnp.zeros_like(acc)
        for ks, k_ref in zip(STAGES, (ka_ref, kb_ref, kc_ref)):
            count = jnp.int32(0)
            for k in ks:
                for c in range(2):
                    live = q_ref[16 + (g ^ k) * 2 + c] >= 0

                    @pl.when(live)
                    def _(count=count, k=k, c=c):
                        jobs[count] = (g ^ k) * 2 + c

                    count = count + live.astype(jnp.int32)

            def step(pair, carry, k_ref=k_ref, count=count):
                for u in range(2):
                    j = jnp.minimum(2 * pair + u, count - 1)
                    live = (2 * pair + u < count).astype(F32)
                    slot = jobs[j]
                    h, c = slot >> 1, slot & 1
                    rows = pl.ds(pl.multiple_of(c * 8, 8), 8)
                    k = k_ref[j]
                    col_ref[h, rows, :] = fold(mm(va[...], k, NN))
                    acc[...] += mm(split(xw_ref[h, rows, :] * live), k, NT)
                return carry

            lax.fori_loop(0, (count + 1) // 2, step, 0)
        row = fold(acc[...])
        row_ref[...] = row
        pairs = w_ref[...] * (0.5 * loc_ref[...] + ro_ref[...] + row) + wl_ref[...] * rl_ref[...]
        lane = lax.broadcasted_iota(jnp.int32, (8, 128), 1)
        pay = jnp.where(lane == 3, sum_ref[...] - jnp.sum(pairs, axis=1, keepdims=True), sum_ref[...])
        for h in range(8):
            col_ref[h, 16:24, 0:128] = pay
            col_ref[h, 16:24, 128:] = jnp.zeros((8, 128), F32)

    return pl.pallas_call(
        body,
        out_shape=(f32(8, 24, TILE), f32(8, n)),
        in_specs=[SMEM] + [VM] * 13,
        out_specs=(VM, VM),
        scratch_shapes=[
            pltpu.VMEM((16, n), BF16),
            pltpu.VMEM((16, n), F32),
            pltpu.SMEM((16,), jnp.int32),
            pltpu.VMEM((8, 16, TILE), F32),
        ],
        compiler_params=params(),
        name="cross_second",
    )(table, *k_caches, w, sums, loc, row_left, row_own, w_left, *xw)


def group_sum(table, w, deg, parts, ret):
    n = w.shape[1]
    m = len(parts)

    def body(q_ref, w_ref, deg_ref, *refs):
        part_refs, (x_ref, w2_ref, out_ref, acc) = refs[:m], refs[m:]
        total = part_refs[0][...]
        for p in part_refs[1:]:
            total = total + p[...]
        acc[...] = total
        for h in range(8):
            for c in range(2):
                t = q_ref[h * 2 + c]

                @pl.when(t >= 0)
                def _(h=h, c=c, t=t):
                    acc[:, span(t)] = acc[:, span(t)] + x_ref[h, c * 8 : c * 8 + 8, :]

        w2_ref[...] = 0.5 * (deg_ref[...] * w_ref[...] - acc[...])
        sums = x_ref[0, 16:24, 0:128]
        for h in range(1, 8):
            sums = sums + x_ref[h, 16:24, 0:128]
        for v in range(16):
            out_ref[v] = sums

    return pl.pallas_call(
        body,
        out_shape=(f32(8, n), f32(16, 8, 128)),
        in_specs=[SMEM] + [VM] * (3 + m),
        out_specs=(VM, VM),
        scratch_shapes=[pltpu.VMEM((8, n), F32)],
        compiler_params=params(),
        name="group_sum",
    )(table, w, deg, *parts, ret)


def finish(gathered, r, w, w2):
    n = r.shape[1]

    def body(g_ref, r_ref, w_ref, w2_ref, sol_ref, res_ref):
        sums = g_ref[0]
        for v in range(1, 16):
            sums = sums + g_ref[v]
        rho, mu, nu, xi = (sums[:, k : k + 1] for k in range(4))
        rv = r_ref[...]
        wv = w_ref[...]
        first = rho / (rho + mu)
        gap = (nu - mu * (mu / rho)) * (first * first)
        beta = gap / rho
        cr = mu / (rho + mu) + beta
        curvature = cr * cr * (rho + mu) - 2.0 * cr * first * (mu + nu) + first * first * (nu + xi)
        second = gap / curvature
        sol_ref[...] = (first + second * cr) * rv - (second * first) * wv
        res_ref[...] = (
            (mu / (rho + mu) - second * cr) * rv
            + (second * (first - cr) - first) * wv
            + (second * first) * w2_ref[...]
        )

    return pl.pallas_call(
        body,
        out_shape=(f32(8, n), f32(8, n)),
        in_specs=[VM] * 4,
        out_specs=(VM, VM),
        compiler_params=params(),
        name="finish",
    )(gathered, r, w, w2)


def on_device(points, targets, partner_tiles):
    dev_count = lax.axis_size("dev")
    to_right = [(i, i + 1) for i in range(dev_count - 1)]
    to_left = [(i + 1, i) for i in range(dev_count - 1)]

    def right_of(x):
        return lax.ppermute(x, "dev", to_left)

    def left_of(x):
        return lax.ppermute(x, "dev", to_right)

    def swap(x, k):
        return lax.ppermute(x, "group", [(i, i ^ k) for i in range(8)])

    def trade(x, axis="group"):
        return lax.all_to_all(x, axis, split_axis=0, concat_axis=0, tiled=True)

    table, own, *outgoing = prep(jnp.transpose(partner_tiles, (0, 2, 3, 1)), points, targets)
    arrived = {}
    for x, k in zip(outgoing, SWAPS[:5]):
        arrived[k] = swap(x, k)
    left = left_of(own)
    right = right_of(own)
    k_local, acc_local, norms, rhs = local_first(own)

    def cross(stage, after):
        return cross_first(stage, table, own, norms, rhs, [arrived[k] for k in stage], after)

    ret = {}

    def give_back(cols, stage):
        for x, k in zip(cols, stage):
            ret[k] = swap(x, k)

    k_a, row_a, *col_a = cross(STAGES[0], acc_local)
    give_back(col_a, STAGES[0])
    for x, k in zip(gate(outgoing[5:], [row_a, arrived[3], arrived[7]]), STAGES[2]):
        arrived[k] = swap(x, k)
    k_b, row_b, *col_b = cross(STAGES[1], row_a)
    give_back(col_b, STAGES[1])
    k_own, col_own, acc_band, right_norms, right_rhs = band_own(own, norms, rhs, right, row_b)
    k_left, to_r, to_l = band_left(left, right, right_norms, right_rhs, col_own)
    from_left, from_right = left_of(to_r), right_of(to_l)
    k_c, row_c, *col_c = cross(STAGES[2], to_l)
    give_back(col_c, STAGES[2])
    w_own, w_relay, w, deg, sums = combine(
        table, targets, (acc_local, acc_band, from_left, from_right, row_a, row_b, row_c), [ret[k] for k in SWAPS]
    )
    w_left = left_of(w)
    w_right = right_of(w)
    partner = swap(w_relay, 1)
    xw = [partner] + [swap(x, 2 * j + 2) for j, x in enumerate(relay(w_own, partner))]
    loc2 = local_second(k_local, w)
    col_r, rowl_b, rowo_b = band_second(k_left, k_own, w_left, w, w_right, loc2)
    from_left2 = left_of(col_r)
    from_right2 = right_of(rowl_b)
    col_x, row_x = cross_second(table, (k_a, k_b, k_c), w, xw, sums, loc2, rowl_b, rowo_b, w_left)
    w2, column = group_sum(table, w, deg, (loc2, rowo_b, row_x, from_left2, from_right2), trade(col_x))
    return finish(trade(column, "dev"), targets, w, w2)


def solution(mesh):
    return jax.shard_map(
        on_device,
        mesh=mesh,
        in_specs=(P(("group", "dev"), None), P(None, ("group", "dev")), P()),
        out_specs=(P(None, ("group", "dev")), P(None, ("group", "dev"))),
        check_vma=False,
    )
```
